32 devices in a mesh: dp: 4 (over x, core), ctx: 2 (over y), tensor: 4 (over z).
Axes of the slice: x: 2, y: 2, z: 4, core: 2. Of those that a mesh axis runs over, the one named last changes fastest.
Arguments:
- inputs: bfloat16 [1024, 8, 768], P(('ctx', 'tensor'), 'dp'), may hold values from -6 to 6
- cotangent: bfloat16 [1024, 8, 768], P(('ctx', 'tensor'), 'dp'), may hold values from -6 to 6
- segments: int32 [8, 1024], P('dp'), may hold values from 0 to 3, never falling along the last dimension, each value on 1 to 512 neighbouring positions
- triple_weight: bfloat16 [3, 768, 768], P(None, ('dp', 'ctx'), 'tensor'), may hold values from -0.21875 to 0.21875
- attend_bias: bfloat16 [2, 4, 192], P(None, 'tensor', ('dp', 'ctx')), may hold values from -1.75 to 1.75
- merge_weight: bfloat16 [768, 768], P('tensor', ('dp', 'ctx')), may hold values from -1.75 to 1.75
- merge_bias: bfloat16 [4, 192], P('tensor', ('dp', 'ctx')), may hold values from -3 to 3
- first_gain: bfloat16 [4, 192], P('tensor', ('dp', 'ctx')), may hold values from 0.5 to 1.5
- first_shift: bfloat16 [4, 192], P('tensor', ('dp', 'ctx')), may hold values from -3 to 3
- expand_weight: bfloat16 [768, 3072], P(('dp', 'ctx'), 'tensor'), may hold values from -0.21875 to 0.21875
- expand_bias: bfloat16 [4, 768], P('tensor', ('dp', 'ctx')), may hold values from -3 to 3
- shrink_weight: bfloat16 [3072, 768], P('tensor', ('dp', 'ctx')), may hold values from -0.109375 to 0.109375
- shrink_bias: bfloat16 [4, 192], P('tensor', ('dp', 'ctx')), may hold values from -3 to 3
- second_gain: bfloat16 [4, 192], P('tensor', ('dp', 'ctx')), may hold values from 0.5 to 1.5
- second_shift: bfloat16 [4, 192], P('tensor', ('dp', 'ctx')), may hold values from -3 to 3
Outputs:
- outputs: float32 [1024, 8, 768], P(('ctx', 'tensor'), 'dp')
- inputs_gradient: float32 [1024, 8, 768], P(('ctx', 'tensor'), 'dp')
- triple_weight_gradient: float32 [3, 768, 768], P(None, ('dp', 'ctx'), 'tensor')
- attend_bias_gradient: float32 [2, 4, 192], P(None, 'tensor', ('dp', 'ctx'))
- merge_weight_gradient: float32 [768, 768], P('tensor', ('dp', 'ctx'))
- merge_bias_gradient: float32 [4, 192], P('tensor', ('dp', 'ctx'))
- first_gain_gradient: float32 [4, 192], P('tensor', ('dp', 'ctx'))
- first_shift_gradient: float32 [4, 192], P('tensor', ('dp', 'ctx'))
- expand_weight_gradient: float32 [768, 3072], P(('dp', 'ctx'), 'tensor')
- expand_bias_gradient: float32 [4, 768], P('tensor', ('dp', 'ctx'))
- shrink_weight_gradient: float32 [3072, 768], P('tensor', ('dp', 'ctx'))
- shrink_bias_gradient: float32 [4, 192], P('tensor', ('dp', 'ctx'))
- second_gain_gradient: float32 [4, 192], P('tensor', ('dp', 'ctx'))
- second_shift_gradient: float32 [4, 192], P('tensor', ('dp', 'ctx'))
The draws below stay inside these ranges and needn't reach their ends.
Inputs may be any that keep to these rules, and one draw needn't show every extreme that they name: `segments`: along each sequence the document numbers never fall; every document has 1 to 512 tokens, and in each sequence some document has exactly 512.
All inputs are finite; a program needn't handle non-finite values.
Results may differ from the reference program's by a relative error of at most 0.02.
Values may be sent and summed in bfloat16 or wider, within the bound.
A program may use at most 192 MiB of HBM per device.

```python
import math
import jax
import jax.numpy as jnp
import numpy as np
from jax import lax

D = 768
HEADS = 12
HEAD_DIM = 64
FF = 3072
SEQUENCES = 8
LEN = 1024
DOCS = 4
LONGEST = 512
N_TENSOR = 4


def spiked(values, own_key, source, target, blocks, factor):
    owner, partner = [(jnp.arange(values.shape[dim]) // (values.shape[dim] // blocks)).reshape([-1 if axis == dim else 1 for axis in range(values.ndim)]) for dim in (source, target)]
    chosen = jax.random.permutation(own_key, blocks)[partner]
    strong = (owner == chosen) | (owner == (partner + blocks // 2) % blocks)
    return jnp.where(strong, factor * values, values)


def level_of(key, shape, split, smallest, high):
    factor_of = 1.0
    for dim, parts in split:
        heights = jax.random.uniform(jax.random.fold_in(jax.random.fold_in(key, 6), dim), (parts,), jnp.float32, smallest / len(split), high / len(split))
        factor_of = factor_of * jnp.repeat(jnp.exp(heights), shape[dim] // parts).reshape((-1,) + (1,) * (len(shape) - 1 - dim))
    return factor_of


def profile(count, total, bound, lean):
    portions = [(1 << 20) // math.isqrt(rank ** lean) + 1 for rank in range(2, count + 1)]
    rest, holding = total - bound - (count - 1), [1] * (count - 1)
    while rest > 0:
        candidates = [i for i in range(count - 1) if holding[i] < bound]
        pool, budget = sum([portions[i] for i in candidates]), rest
        for i in candidates:
            extra = min(bound - holding[i], max(1, budget * portions[i] // pool), rest)
            holding[i] = holding[i] + extra
            rest = rest - extra
    return np.array([bound] + holding)


def uneven(key, amount, total, limit, slope):
    if amount == 2:
        one = jax.random.randint(key, (), max(1, total - limit), min(limit, total - 1) + 1)
        return jnp.stack([one, total - one])
    lengths = jnp.asarray(profile(amount, total, limit, slope), jnp.int32)
    pairs = (amount - 1) // 2
    source_of, sink = lengths[1:1 + 2 * pairs:2], lengths[2:2 + 2 * pairs:2]
    margin = jnp.minimum(source_of - 1, limit - sink)
    shifted = jax.random.randint(jax.random.fold_in(key, 1), (pairs,), 0, 1 << 20) % (margin + 1)
    lengths = lengths.at[1:1 + 2 * pairs:2].set(source_of - shifted).at[2:2 + 2 * pairs:2].set(sink + shifted)
    return lengths[jax.random.permutation(jax.random.fold_in(key, 2), amount)]


def gaussian(own_key, dims, width, limit, split=(), kind=jnp.bfloat16):
    level = level_of(own_key, dims, split, -0.22, 0.18) if split else 1.0
    values = jax.random.normal(own_key, dims, jnp.float32) * width * level
    return jnp.minimum(jnp.maximum(values, -limit), limit).astype(kind)


def gaussian_with(own_key, dims, scale, reach, pieces, heavy, kind=jnp.bfloat16):
    array = scale * jax.random.normal(own_key, dims, jnp.float32)
    if pieces:
        array = array * level_of(own_key, dims, pieces, -0.22, 0.18)
    return jnp.clip(spiked(array, jax.random.fold_in(own_key, 3), *heavy), -reach, reach).astype(kind)


def setup_inputs(seed: int = 0) -> dict:
    seeds = jax.random.split(jax.random.key(seed), 16)
    return {
        "inputs": gaussian_with(seeds[0], (LEN, SEQUENCES, D), 1.0, 6.0, ((0, 8), (1, 4)), (0, 2, 8, 2.0)),
        "cotangent": gaussian_with(seeds[1], (LEN, SEQUENCES, D), 1.0, 6.0, ((0, 8), (1, 4)), (0, 2, 8, 2.0)),
        "segments": jax.vmap(lambda own: jnp.searchsorted(jnp.cumsum(uneven(own, DOCS, LEN, LONGEST, 2)), jnp.arange(LEN), side="right"))(jax.random.split(seeds[2], SEQUENCES)).reshape((SEQUENCES, LEN)).astype(jnp.int32),
        "triple_weight": gaussian(seeds[3], (3, D, D), D ** -0.5, 0.21875, ((1, 8), (2, 4))),
        "attend_bias": gaussian(seeds[4], (2, N_TENSOR, D // N_TENSOR), 0.3, 1.75, ((1, 4), (2, 8))),
        "merge_weight": gaussian(seeds[5], (D, D), (D // 64) ** -0.5, 1.75, ((0, 4), (1, 8))),
        "merge_bias": gaussian(seeds[6], (N_TENSOR, D // N_TENSOR), 0.5, 3.0, ((0, 4), (1, 8))),
        "first_gain": jnp.clip(1.0 + 0.1 * jax.random.normal(seeds[7], (N_TENSOR, D // N_TENSOR), jnp.float32), 0.5, 1.5).astype(jnp.bfloat16),
        "first_shift": gaussian(seeds[8], (N_TENSOR, D // N_TENSOR), 0.5, 3.0, ((0, 4), (1, 8))),
        "expand_weight": gaussian(seeds[9], (D, FF), D ** -0.5, 0.21875, ((0, 8), (1, 4))),
        "expand_bias": gaussian(seeds[10], (N_TENSOR, FF // N_TENSOR), 0.5, 3.0, ((0, 4), (1, 8))),
        "shrink_weight": gaussian(seeds[11], (FF, D), FF ** -0.5, 0.109375, ((0, 4), (1, 8))),
        "shrink_bias": gaussian(seeds[12], (N_TENSOR, D // N_TENSOR), 0.5, 3.0, ((0, 4), (1, 8))),
        "second_gain": jnp.clip(1.0 + 0.1 * jax.random.normal(seeds[13], (N_TENSOR, D // N_TENSOR), jnp.float32), 0.5, 1.5).astype(jnp.bfloat16),
        "second_shift": gaussian(seeds[14], (N_TENSOR, D // N_TENSOR), 0.5, 3.0, ((0, 4), (1, 8))),
    }


EPS = 1e-12
NEG = -1e+30
HIGH = lax.Precision.HIGHEST

@jax.custom_vjp
def low(v):
    return lax.optimization_barrier(v.astype(jnp.bfloat16)).astype(jnp.float32)

@jax.custom_vjp
def low_back(v):
    return v

def low_keep(v):
    return (low(v), None)

def low_pass(kept, grad):
    return (grad,)

def back_keep(v):
    return (v, None)

def back_low(kept, grad):
    return (low(grad),)
low.defvjp(low_keep, low_pass)
low_back.defvjp(back_keep, back_low)

def matmul(left, right):
    return jnp.dot(left, right, precision=HIGH, preferred_element_type=jnp.float32)

def norm_rows(total, gain, shift):
    center = total - lax.optimization_barrier(jnp.mean(total, axis=-1, keepdims=True))
    spread = lax.optimization_barrier(jnp.mean(center * center, axis=-1, keepdims=True))
    return center * lax.rsqrt(spread + EPS) * gain + shift

def attention(queries, keys_all, values_all, labels):
    length = queries.shape[0]
    block = min(512, length)
    count = length // block

    def one_block(args):
        query_block, label_block = args
        scores = 0.125 * jnp.einsum('qhd,khd->hqk', query_block, keys_all, precision=HIGH)
        scores = low_back(scores)
        allowed = label_block[:, None] == labels[None, :]
        scores = jnp.where(allowed[None], scores, NEG)
        top = lax.optimization_barrier(jnp.max(scores, axis=-1, keepdims=True))
        expo = jnp.where(allowed[None], jnp.exp(scores - top), 0.0)
        probs = low(expo / lax.optimization_barrier(jnp.sum(expo, axis=-1, keepdims=True)))
        return jnp.einsum('hqk,khd->qhd', probs, values_all, precision=HIGH)
    result = lax.map(jax.checkpoint(one_block), (queries.reshape(count, block, HEADS, HEAD_DIM), labels.reshape(count, block)))
    return result.reshape(length, HEADS * HEAD_DIM)

def layer(inputs, triple_weight, attend_bias, merge_weight, merge_bias, first_gain, first_shift, expand_weight, expand_bias, shrink_weight, shrink_bias, second_gain, second_shift, labels):
    length = inputs.shape[0]
    queries = low(low_back(matmul(inputs, triple_weight[0]) + attend_bias[0]))
    keys_all = low(low_back(matmul(inputs, triple_weight[1])))
    values_all = low(low_back(matmul(inputs, triple_weight[2]) + attend_bias[1]))
    shape_four = (length, HEADS, HEAD_DIM)
    mixed = attention(queries.reshape(shape_four), keys_all.reshape(shape_four), values_all.reshape(shape_four), labels)
    mixed = low(low_back(mixed))
    first_sum = inputs + low_back(matmul(mixed, merge_weight)) + merge_bias
    first_norm = norm_rows(first_sum, first_gain, first_shift)
    before = low_back(matmul(low(first_norm), expand_weight) + expand_bias)
    active = low(jax.nn.gelu(before, approximate=False))
    second_sum = first_norm + low_back(matmul(active, shrink_weight)) + shrink_bias
    return norm_rows(second_sum, second_gain, second_shift)

def reference(inputs, cotangent, segments, triple_weight, attend_bias, merge_weight, merge_bias, first_gain, first_shift, expand_weight, expand_bias, shrink_weight, shrink_bias, second_gain, second_shift):
    shapes = (triple_weight.shape, attend_bias.shape, merge_weight.shape, merge_bias.shape, first_gain.shape, first_shift.shape, expand_weight.shape, expand_bias.shape, shrink_weight.shape, shrink_bias.shape, second_gain.shape, second_shift.shape)
    params = (triple_weight.astype(jnp.float32), attend_bias.astype(jnp.float32).reshape(2, -1), merge_weight.astype(jnp.float32), merge_bias.astype(jnp.float32).reshape(-1), first_gain.astype(jnp.float32).reshape(-1), first_shift.astype(jnp.float32).reshape(-1), expand_weight.astype(jnp.float32), expand_bias.astype(jnp.float32).reshape(-1), shrink_weight.astype(jnp.float32), shrink_bias.astype(jnp.float32).reshape(-1), second_gain.astype(jnp.float32).reshape(-1), second_shift.astype(jnp.float32).reshape(-1))
    seq_inputs = jnp.moveaxis(inputs.astype(jnp.float32), 1, 0)
    seq_cotan = jnp.moveaxis(cotangent.astype(jnp.float32), 1, 0)
    zeros = tuple((jnp.zeros(p.shape, jnp.float32) for p in params))

    def step(carry, item):
        row_in, row_cotan, labels = item

        def forward(row, *weights):
            return layer(row, *weights, labels)
        result, pull = jax.vjp(forward, row_in, *params)
        grads = pull(row_cotan)
        carry = tuple((c + g for c, g in zip(carry, grads[1:])))
        return (carry, (result, grads[0]))
    totals, (results, row_grads) = lax.scan(step, zeros, (seq_inputs, seq_cotan, segments))
    outputs = jnp.moveaxis(results, 0, 1)
    inputs_gradient = jnp.moveaxis(row_grads, 0, 1)
    shaped = tuple((t.reshape(s) for t, s in zip(totals, shapes)))
    return (outputs, inputs_gradient, shaped[0], shaped[1], shaped[2], shaped[3], shaped[4], shaped[5], shaped[6], shaped[7], shaped[8], shaped[9], shaped[10], shaped[11])
```

```python
import functools

import jax
import jax.numpy as jnp
from jax import lax
from jax.experimental import pallas as pl
from jax.experimental.pallas import tpu as pltpu
from jax.sharding import PartitionSpec as P

HEAD_DIM = 64

EPS = 1e-12
NEG = -1e30
SCALE = 0.125
MESH = pl.DeviceIdType.MESH
BF16 = jnp.bfloat16
F32 = jnp.float32
ALL = ("dp", "ctx", "tensor")
TOKENS = ("ctx", "tensor")


def at(dp, ctx, tensor):
    return {"dp": dp, "ctx": ctx, "tensor": tensor}


def remote(src, dst, send, recv, where):
    return pltpu.make_async_remote_copy(
        src_ref=src, dst_ref=dst, send_sem=send, recv_sem=recv, device_id=where, device_id_type=MESH
    )


def greet(peers):
    barrier = pltpu.get_barrier_semaphore()
    for peer in peers:
        pl.semaphore_signal(barrier, inc=1, device_id=peer, device_id_type=MESH)
    pl.semaphore_wait(barrier, len(peers))


def everyone(n_dp, n_ctx, n_tensor):
    dp, ctx, tensor = (lax.axis_index(a) for a in ALL)
    peers = []
    for i in range(n_dp):
        for j in range(n_ctx):
            for k in range(n_tensor):
                if i or j or k:
                    peers.append(
                        (lax.rem(dp + i, n_dp), lax.rem(ctx + j, n_ctx), lax.rem(tensor + k, n_tensor))
                    )
    return peers


def gather_kernel(n_tensor, w0, w1, w2, small, o0, o1, o2, small_all, *sems):
    (own_sem, z_send, z_recv, x_send, x_recv, y_send, y_recv, a_send, a_recv, b_send, b_recv,
     c_send, c_recv, s_send, s_recv) = sems
    shards, outs = (w0, w1, w2), (o0, o1, o2)
    dp, ctx, z = (lax.axis_index(a) for a in ALL)
    rows = w0.shape[0]
    half = rows // 2
    xp = lax.rem(dp + 2, 4)
    cp = dp + 1 - 2 * lax.rem(dp, 2)
    yp = 1 - ctx
    xcp = lax.rem(cp + 2, 4)
    me = dp * 2 + ctx
    mine = z * 8 + me
    peers = everyone(4, 2, n_tensor)
    greet([at(*p) for p in peers])
    x_dev, y_dev, c_dev = at(xp, ctx, z), at(dp, yp, z), at(cp, ctx, z)

    def to_z(g, k):
        there = lax.rem(z + k, n_tensor)
        return remote(shards[g], outs[g].at[z, me], z_send.at[g, there], z_recv.at[g, z], at(dp, ctx, there))

    def from_z(g, origin):
        return remote(
            outs[g].at[origin, me], outs[g].at[origin, me], z_send.at[g, origin], z_recv.at[g, origin], x_dev
        )

    def along(g, origin, slot, send, recv, dev, src=None):
        block = outs[g].at[origin, slot]
        return remote(block if src is None else src, block, send.at[g, origin], recv.at[g, origin], dev)

    def part(g, origin, slot, lo, send, recv, dev):
        block = outs[g].at[origin, slot, pl.ds(lo, half)]
        return remote(block, block, send.at[g, origin], recv.at[g, origin], dev)

    def core(g, origin, kind, slot, src=None):
        block = outs[g].at[origin, slot]
        return remote(
            block if src is None else src, block, c_send.at[g, kind, origin], c_recv.at[g, kind, origin], c_dev
        )

    x_slot, y_slot, d_slot = xp * 2 + ctx, dp * 2 + yp, xp * 2 + yp

    own = [pltpu.make_async_copy(shards[g], outs[g].at[z, me], own_sem.at[g]) for g in range(3)]
    for g in range(3):
        along(g, z, me, x_send, x_recv, x_dev, shards[g]).start()
        along(g, z, me, y_send, y_recv, y_dev, shards[g]).start()
        for k in range(1, n_tensor):
            to_z(g, k).start()
        core(g, z, 0, me, shards[g]).start()
        own[g].start()
    small_own = pltpu.make_async_copy(small, small_all.at[mine], s_send.at[0])
    small_own.start()
    for n, p in enumerate(peers):
        remote(small, small_all.at[mine], s_send.at[n + 1], s_recv.at[n], at(*p)).start()

    def step(j, carry):
        @pl.when((j >= 1) & (j < n_tensor))
        def _():
            origin = lax.rem(z + n_tensor - j, n_tensor)
            for g in range(3):
                from_z(g, origin).wait_recv()
                along(g, origin, me, x_send, x_recv, x_dev).start()
                along(g, origin, me, y_send, y_recv, y_dev).start()
                core(g, origin, 0, me).start()

        @pl.when((j >= 1) & (j < n_tensor + 1))
        def _():
            origin = lax.rem(z + n_tensor + 1 - j, n_tensor)
            for g in range(3):
                along(g, origin, x_slot, x_send, x_recv, x_dev).wait_recv()
                part(g, origin, x_slot, 0, a_send, a_recv, y_dev).start()
                core(g, origin, 1, x_slot).start()
                along(g, origin, y_slot, y_send, y_recv, y_dev).wait_recv()
                part(g, origin, y_slot, half, b_send, b_recv, x_dev).start()
                core(g, origin, 2, y_slot).start()

        @pl.when(j >= 2)
        def _():
            origin = lax.rem(z + n_tensor + 2 - j, n_tensor)
            for g in range(3):
                part(g, origin, d_slot, 0, a_send, a_recv, y_dev).wait_recv()
                part(g, origin, d_slot, half, b_send, b_recv, x_dev).wait_recv()
                core(g, origin, 3, d_slot).start()

        return carry

    lax.fori_loop(0, n_tensor + 2, step, 0)

    slots = (cp * 2 + ctx, xcp * 2 + ctx, cp * 2 + yp, xcp * 2 + yp)

    def finish(origin, carry):
        for g in range(3):
            for kind in range(4):
                core(g, origin, kind, slots[kind]).wait_recv()
                core(g, origin, kind, slots[kind]).wait_send()
            along(g, origin, me, x_send, x_recv, x_dev).wait_send()
            along(g, origin, me, y_send, y_recv, y_dev).wait_send()
            part(g, origin, x_slot, 0, a_send, a_recv, y_dev).wait_send()
            part(g, origin, y_slot, half, b_send, b_recv, x_dev).wait_send()
        return carry

    lax.fori_loop(0, n_tensor, finish, 0)
    for g in range(3):
        own[g].wait()
        for k in range(1, n_tensor):
            to_z(g, k).wait_send()
    small_own.wait()
    for n, p in enumerate(peers):
        back = remote(small, small_all.at[mine], s_send.at[n + 1], s_recv.at[n], at(*p))
        back.wait_send()
        back.wait_recv()


def gather_weights(n_tensor, w0, w1, w2, small):
    rows, cols = w0.shape
    n_small = 8 * n_tensor
    full = jax.ShapeDtypeStruct((n_tensor, 8, rows, cols), BF16)
    dma = pltpu.SemaphoreType.DMA
    pair = [dma((3, n_tensor)), dma((3, n_tensor))]
    total = 3 * rows * cols * 2
    return pl.pallas_call(
        functools.partial(gather_kernel, n_tensor),
        out_shape=(full, full, full, jax.ShapeDtypeStruct((n_small,) + small.shape, F32)),
        in_specs=[pl.BlockSpec(memory_space=pltpu.VMEM)] * 4,
        out_specs=(pl.BlockSpec(memory_space=pl.ANY),) * 3 + (pl.BlockSpec(memory_space=pltpu.VMEM),),
        scratch_shapes=[dma((3,))] + pair * 5
        + [dma((3, 4, n_tensor)), dma((3, 4, n_tensor)), dma((n_small,)), dma((n_small,))],
        compiler_params=pltpu.CompilerParams(collective_id=0, has_side_effects=True),
        cost_estimate=pl.CostEstimate(flops=0, bytes_accessed=total * 64, transcendentals=0),
        name="gather_weights",
    )(w0, w1, w2, small)


def swap_kernel(n_ctx, n_tensor, by_place, src, dst, own_sem, send, recv):
    dp, ctx, z = (lax.axis_index(a) for a in ALL)
    steps = [(j, k) for j in range(n_ctx) for k in range(n_tensor) if j or k]
    peers = [(lax.rem(ctx + j, n_ctx), lax.rem(z + k, n_tensor)) for j, k in steps]
    greet([at(dp, *p) for p in peers])

    def slot(c, t, place):
        return c * n_tensor + t if place else t * n_ctx + c

    order = sorted(range(len(steps)), key=lambda n: -abs(steps[n][1] - 0.5))
    here = pltpu.make_async_copy(src.at[slot(ctx, z, by_place)], dst.at[slot(ctx, z, not by_place)], own_sem)

    def copy(n):
        c, t = peers[n]
        return remote(
            src.at[slot(c, t, by_place)], dst.at[slot(ctx, z, not by_place)], send.at[n], recv.at[n], at(dp, c, t)
        )

    for n in order:
        copy(n).start()
    here.start()
    here.wait()
    for n in range(len(steps)):
        copy(n).wait()


def swap(value, n_ctx, n_tensor, by_place, collective_id):
    n = n_ctx * n_tensor
    dma = pltpu.SemaphoreType.DMA
    return pl.pallas_call(
        functools.partial(swap_kernel, n_ctx, n_tensor, by_place),
        out_shape=jax.ShapeDtypeStruct(value.shape, value.dtype),
        in_specs=[pl.BlockSpec(memory_space=pltpu.VMEM)],
        out_specs=pl.BlockSpec(memory_space=pltpu.VMEM),
        scratch_shapes=[dma, dma((n - 1,)), dma((n - 1,))],
        compiler_params=pltpu.CompilerParams(collective_id=collective_id, has_side_effects=True),
        cost_estimate=pl.CostEstimate(flops=0, bytes_accessed=value.size * 32, transcendentals=0),
        name="swap",
    )(value)


def sum_kernel(n_tensor, g0, g1, g2, small, o0, o1, o2, small_out, acc, core_in, y1_in, x1_in, x2_in, y2_in, z_in,
               small_in, load_sem, c_send, c_recv, y1_send, y1_recv, x1_send, x1_recv, x2_send, x2_recv,
               y2_send, y2_recv, z_send, z_recv, s_send, s_recv):
    grads, outs = (g0, g1, g2), (o0, o1, o2)
    dp, ctx, z = (lax.axis_index(a) for a in ALL)
    rows = o0.shape[0]
    half = rows // 2
    core = lax.rem(dp, 2)
    x = lax.div(dp, 2)
    xp, yp = 1 - x, 1 - ctx
    mine = z * 8 + dp * 2 + ctx
    peers = everyone(4, 2, n_tensor)
    greet([at(*p) for p in peers])
    x_dev, y_dev, c_dev = at(xp * 2 + core, ctx, z), at(dp, yp, z), at(x * 2 + 1 - core, ctx, z)
    low, high = pl.ds(0, half), pl.ds(half, half)

    def load(g, t):
        return pltpu.make_async_copy(grads[g].at[t, :, core], acc.at[g, t], load_sem.at[g, t])

    def to_core(g, t):
        return remote(grads[g].at[t, :, 1 - core], core_in.at[g, t], c_send.at[g, t], c_recv.at[g, t], c_dev)

    def y1(g, t):
        return remote(acc.at[g, t, :, yp, low], y1_in.at[g, t], y1_send.at[g, t], y1_recv.at[g, t], y_dev)

    def x1(g, t):
        return remote(acc.at[g, t, xp, :, high], x1_in.at[g, t], x1_send.at[g, t], x1_recv.at[g, t], x_dev)

    def x2(g, t):
        return remote(acc.at[g, t, xp, ctx, low], x2_in.at[g, t], x2_send.at[g, t], x2_recv.at[g, t], x_dev)

    def y2(g, t):
        return remote(acc.at[g, t, x, yp, high], y2_in.at[g, t], y2_send.at[g, t], y2_recv.at[g, t], y_dev)

    def to_z(g, t):
        return remote(acc.at[g, t, x, ctx], z_in.at[g, z], z_send.at[g, t], z_recv.at[g, z], at(dp, ctx, t))

    def add(a, b):
        return (a.astype(F32) + b.astype(F32)).astype(BF16)

    small_copies = []
    for n, (pd, pc, pt) in enumerate(peers):
        small_copies.append(
            remote(small.at[pt * 8 + pd * 2 + pc], small_in.at[n], s_send.at[n], s_recv.at[n], at(pd, pc, pt))
        )

    def begin(j, carry):
        t = lax.rem(z + 1 + j, n_tensor)
        for g in range(3):
            to_core(g, t).start()
            load(g, t).start()
        return carry

    lax.fori_loop(0, n_tensor, begin, 0)
    for copy in small_copies:
        copy.start()

    def step(j, carry):
        @pl.when(j < n_tensor)
        def _():
            t = lax.rem(z + 1 + j, n_tensor)
            for g in range(3):
                load(g, t).wait()
                to_core(g, t).wait_recv()
                acc[g, t] = add(acc[g, t], core_in[g, t])
                y1(g, t).start()
                x1(g, t).start()

        @pl.when((j >= 1) & (j < n_tensor + 1))
        def _():
            t = lax.rem(z + j, n_tensor)
            for g in range(3):
                y1(g, t).wait_recv()
                for i in range(2):
                    acc[g, t, i, ctx, low] = add(acc[g, t, i, ctx, low], y1_in[g, t, i])
                x2(g, t).start()
                x1(g, t).wait_recv()
                for i in range(2):
                    acc[g, t, x, i, high] = add(acc[g, t, x, i, high], x1_in[g, t, i])
                y2(g, t).start()

        @pl.when(j >= 2)
        def _():
            t = lax.rem(z + j - 1, n_tensor)
            for g in range(3):
                x2(g, t).wait_recv()
                acc[g, t, x, ctx, low] = add(acc[g, t, x, ctx, low], x2_in[g, t])
                y2(g, t).wait_recv()
                acc[g, t, x, ctx, high] = add(acc[g, t, x, ctx, high], y2_in[g, t])

                @pl.when(j < n_tensor + 1)
                def _():
                    to_z(g, t).start()

        return carry

    lax.fori_loop(0, n_tensor + 2, step, 0)

    for g in range(3):
        outs[g][...] = acc[g, z, x, ctx].astype(F32)
        for k in range(1, n_tensor):
            origin = lax.rem(z + k, n_tensor)
            remote(z_in.at[g, origin], z_in.at[g, origin], z_send.at[g, origin], z_recv.at[g, origin], x_dev).wait_recv()
            outs[g][...] += z_in[g, origin].astype(F32)
    total = small[mine]
    for n in range(len(peers)):
        small_copies[n].wait()
        total = total + small_in[n]
    small_out[...] = total

    def finish(t, carry):
        for g in range(3):
            for copy in (to_core, y1, x1, x2, y2):
                copy(g, t).wait_send()
        return carry

    lax.fori_loop(0, n_tensor, finish, 0)
    for g in range(3):
        for k in range(1, n_tensor):
            to_z(g, lax.rem(z + k, n_tensor)).wait_send()


def sum_grads(n_tensor, g0, g1, g2, small):
    rows, cols = g0.shape[-2:]
    n_small = 8 * n_tensor
    dma = pltpu.SemaphoreType.DMA
    grid = (3, n_tensor)
    vmem = pl.BlockSpec(memory_space=pltpu.VMEM)
    half = rows // 2
    out = jax.ShapeDtypeStruct((rows, cols), F32)
    return pl.pallas_call(
        functools.partial(sum_kernel, n_tensor),
        out_shape=(out, out, out, jax.ShapeDtypeStruct(small.shape[1:], F32)),
        in_specs=[pl.BlockSpec(memory_space=pl.ANY)] * 3 + [vmem],
        out_specs=(vmem,) * 4,
        scratch_shapes=[
            pltpu.VMEM(grid + (2, 2, rows, cols), BF16),
            pltpu.VMEM(grid + (2, 2, rows, cols), BF16),
            pltpu.VMEM(grid + (2, half, cols), BF16),
            pltpu.VMEM(grid + (2, half, cols), BF16),
            pltpu.VMEM(grid + (half, cols), BF16),
            pltpu.VMEM(grid + (half, cols), BF16),
            pltpu.VMEM(grid + (rows, cols), BF16),
            pltpu.VMEM((n_small - 1,) + small.shape[1:], F32),
        ]
        + [dma(grid)] * 13
        + [dma((n_small - 1,))] * 2,
        compiler_params=pltpu.CompilerParams(collective_id=1, has_side_effects=True, vmem_limit_bytes=56 << 20),
        cost_estimate=pl.CostEstimate(flops=0, bytes_accessed=g0.size * 12, transcendentals=0),
        name="sum_grads",
    )(g0, g1, g2, small)


def norm_rows(total, gain, shift):
    center = total - jnp.mean(total, axis=-1, keepdims=True)
    spread = jnp.mean(center * center, axis=-1, keepdims=True)
    return center * lax.rsqrt(spread + EPS) * gain + shift


def gelu_exact(before):
    return jax.nn.gelu(before, approximate=False)


def dot(spec, a, b):
    return jnp.einsum(spec, a, b, preferred_element_type=F32)


def add_up(spec, a, b):
    return sum(dot(spec, a[t], b[t]) for t in range(a.shape[0]))


def local(
    inputs,
    cotangent,
    segments,
    triple_weight,
    attend_bias,
    merge_weight,
    merge_bias,
    first_gain,
    first_shift,
    expand_weight,
    expand_bias,
    shrink_weight,
    shrink_bias,
    second_gain,
    second_shift,
):
    n_dp, n_ctx, n_tensor = (lax.axis_size(a) for a in ALL)
    span, batch, width = inputs.shape
    rows = triple_weight.shape[1]
    part = triple_weight.shape[2]
    units = expand_weight.shape[1]
    owners = n_dp * n_ctx
    heads = part // HEAD_DIM
    count = batch * span
    small_part = part // owners
    unit_part = units // owners
    own_kernels = n_dp == 4 and n_ctx == 2 and rows % 32 == 0
    by_sequence = batch == n_ctx and own_kernels

    w0 = jnp.concatenate(
        [jnp.transpose(triple_weight, (1, 0, 2)).reshape(rows, 3 * part), merge_weight.T], axis=1
    )
    w2 = shrink_weight.T
    vectors = (merge_bias, first_gain, first_shift, shrink_bias, second_gain, second_shift)
    small = jnp.concatenate(
        [attend_bias[0, 0], attend_bias[1, 0]] + [v[0] for v in vectors] + [expand_bias[0]]
    ).astype(F32)
    n_values = small.shape[0]
    if own_kernels:
        pad = -n_values % 1024
        block = ((n_values + pad) // 128, 128)
        f0, f1, f2, small_all = gather_weights(
            n_tensor, w0, expand_weight, w2, jnp.pad(small, (0, pad)).reshape(block)
        )
        small_all = small_all.reshape(n_tensor, owners, -1)[:, :, :n_values]
    else:
        f0, f1, f2 = (
            lax.all_gather(lax.all_gather(w, ("dp", "ctx"), axis=0, tiled=True), "tensor", axis=0, tiled=False)
            for w in (w0, expand_weight, w2)
        )
        small_all = lax.all_gather(lax.all_gather(small, ("dp", "ctx")), "tensor")
    f0, f1, f2 = (w.reshape(n_tensor, width, -1) for w in (f0, f1, f2))
    w_qkv, w_merge, w_expand, w_shrink = f0[:, :, : 3 * part], f0[:, :, 3 * part :], f1, f2
    narrow = small_all[:, :, : 8 * small_part].reshape(n_tensor, owners, 8, small_part)
    narrow = jnp.transpose(narrow, (2, 0, 1, 3)).reshape(8, n_tensor, part)
    merge_vec, gain_one, shift_one, shrink_vec, gain_two, shift_two = narrow[2:].reshape(6, width)
    expand_vec = small_all[:, :, 8 * small_part :].reshape(n_tensor, 1, units)
    qkv_vec = jnp.concatenate([narrow[0], jnp.zeros_like(narrow[0]), narrow[1]], axis=-1)[:, None]

    x_low = jnp.transpose(inputs, (1, 0, 2)).reshape(count, width)
    x = x_low.astype(F32)
    upstream = jnp.transpose(cotangent, (1, 0, 2)).reshape(count, width).astype(F32)

    qkv = (dot("rd,tde->tre", x_low, w_qkv) + qkv_vec).astype(BF16)
    here = lax.axis_index("ctx")
    if by_sequence:
        rows_all = swap(qkv.reshape(n_tensor * n_ctx, span, 3 * part), n_ctx, n_tensor, False, 2)
        rows_all = rows_all.reshape(1, n_ctx * n_tensor * span, 3 * part)
        labels = lax.dynamic_slice_in_dim(segments, here, 1, 0)
        own_labels = labels
        q_rows = rows_all[..., :part]
        kv_rows = rows_all[..., part:]
    else:
        mine = lax.all_to_all(
            qkv.reshape(n_tensor, batch, span, 3 * part), "tensor", split_axis=0, concat_axis=0
        )
        mine = jnp.transpose(mine, (1, 0, 2, 3)).reshape(batch, n_tensor * span, 3 * part)
        labels = segments
        own_labels = lax.dynamic_slice_in_dim(segments, here * n_tensor * span, n_tensor * span, 1)
        q_rows = mine[..., :part]
        kv_rows = lax.all_gather(mine[..., part:], "ctx", axis=1, tiled=True)
    n_seq, n_query = q_rows.shape[:2]
    n_key = kv_rows.shape[1]
    q_four = q_rows.reshape(n_seq, n_query, heads, HEAD_DIM)
    k_four = kv_rows[..., :part].reshape(n_seq, n_key, heads, HEAD_DIM)
    v_four = kv_rows[..., part:].reshape(n_seq, n_key, heads, HEAD_DIM)
    allowed = own_labels[:, None, :, None] == labels[:, None, None, :]
    scores = jnp.where(allowed, SCALE * dot("sqhd,skhd->shqk", q_four, k_four), NEG)
    top = jnp.max(scores, axis=-1)
    weights = jnp.where(allowed, jnp.exp(scores - top[..., None]), 0.0)
    total = jnp.sum(weights, axis=-1)
    mixed_float = dot("shqk,skhd->shqd", weights.astype(BF16), v_four) / total[..., None]
    logsum = top + jnp.log(total)
    mixed_heads = jnp.transpose(mixed_float, (0, 2, 1, 3)).reshape(n_seq, n_query, part).astype(BF16)

    def to_tokens(value, ident):
        if by_sequence:
            out = swap(value.reshape(n_ctx * n_tensor, span, -1), n_ctx, n_tensor, True, ident)
            return out.reshape(n_tensor, count, -1)
        value = value.reshape(batch, n_tensor, span, -1)
        out = lax.all_to_all(jnp.transpose(value, (1, 0, 2, 3)), "tensor", split_axis=0, concat_axis=0)
        return out.reshape(n_tensor, count, -1)

    mixed = to_tokens(mixed_heads, 3)
    first_sum = x + add_up("re,de->rd", mixed, w_merge) + merge_vec
    first_norm = norm_rows(first_sum, gain_one, shift_one)
    first_low = first_norm.astype(BF16)
    before = dot("rd,tdf->trf", first_low, w_expand) + expand_vec
    active = gelu_exact(before).astype(BF16)
    second_sum = first_norm + add_up("rf,df->rd", active, w_shrink) + shrink_vec
    outputs_rows = norm_rows(second_sum, gain_two, shift_two)

    second_grad, gain_two_grad, shift_two_grad = jax.vjp(norm_rows, second_sum, gain_two, shift_two)[1](upstream)
    shrink_vec_grad = jnp.sum(second_grad, axis=0)
    second_low = second_grad.astype(BF16)
    shrink_grad = dot("rd,trf->tdf", second_low, active).astype(BF16)
    active_grad = dot("rd,tdf->trf", second_low, w_shrink)
    before_low = jax.vjp(gelu_exact, before)[1](active_grad)[0].astype(BF16)
    expand_vec_grad = jnp.sum(before_low.astype(F32), axis=1)
    expand_grad = dot("rd,trf->tdf", first_low, before_low).astype(BF16)
    norm_back = add_up("rf,df->rd", before_low, w_expand)
    first_grad, gain_one_grad, shift_one_grad = jax.vjp(norm_rows, first_sum, gain_one, shift_one)[1](
        second_grad + norm_back
    )
    merge_vec_grad = jnp.sum(first_grad, axis=0)
    first_low_grad = first_grad.astype(BF16)
    merge_grad = dot("rd,tre->tde", first_low_grad, mixed).astype(BF16)
    mixed_grad = dot("rd,tde->tre", first_low_grad, w_merge).astype(BF16)
    if by_sequence:
        grad_rows = swap(mixed_grad.reshape(n_tensor * n_ctx, span, part), n_ctx, n_tensor, False, 4)
    else:
        grad_rows = lax.all_to_all(
            mixed_grad.reshape(n_tensor, batch, span, part), "tensor", split_axis=0, concat_axis=0
        )
        grad_rows = jnp.transpose(grad_rows, (1, 0, 2, 3))
    grad_four = grad_rows.reshape(n_seq, n_query, heads, HEAD_DIM)
    delta = jnp.sum(jnp.transpose(grad_four.astype(F32), (0, 2, 1, 3)) * mixed_float, axis=-1)
    back_scores = SCALE * dot("sqhd,skhd->shqk", q_four, k_four)
    probs = jnp.where(allowed, jnp.exp(back_scores - logsum[..., None]), 0.0)
    prob_grad = dot("sqhd,skhd->shqk", grad_four, v_four)
    score_low = (probs * (prob_grad - delta[..., None])).astype(BF16)
    value_part = dot("shqk,sqhd->skhd", probs.astype(BF16), grad_four)
    query_part = SCALE * dot("shqk,skhd->sqhd", score_low, k_four)
    key_part = SCALE * dot("shqk,sqhd->skhd", score_low, q_four)
    query_part, key_part, value_part = (
        v.reshape(n_seq, -1, part).astype(BF16) for v in (query_part, key_part, value_part)
    )
    if not by_sequence:
        key_part, value_part = (
            lax.psum_scatter(v, "ctx", scatter_dimension=1, tiled=True) for v in (key_part, value_part)
        )
    qkv_grad = to_tokens(jnp.concatenate([query_part, key_part, value_part], axis=-1), 5)
    triple_grad = dot("rd,tre->tde", x_low, qkv_grad).astype(BF16)
    attend_grad = jnp.sum(qkv_grad.astype(F32), axis=1).reshape(n_tensor, 3, part)
    inputs_gradient = first_grad + add_up("re,de->rd", qkv_grad, w_qkv)

    vec_grads = jnp.stack(
        [merge_vec_grad, gain_one_grad, shift_one_grad, shrink_vec_grad, gain_two_grad, shift_two_grad]
    ).reshape(6, n_tensor, part)
    narrow_grads = jnp.concatenate(
        [jnp.stack([attend_grad[:, 0], attend_grad[:, 2]]), vec_grads]
    ).reshape(8, n_tensor, owners, small_part)
    narrow_grads = jnp.transpose(narrow_grads, (1, 2, 0, 3)).reshape(n_tensor, owners, 8 * small_part)
    small_grads = jnp.concatenate([narrow_grads, expand_vec_grad.reshape(n_tensor, owners, unit_part)], axis=-1)
    grads = (jnp.concatenate([triple_grad, merge_grad], axis=-1), expand_grad, shrink_grad)
    if own_kernels:
        sent = jnp.pad(small_grads.reshape(n_tensor * owners, n_values), ((0, 0), (0, pad)))
        r0, r1, r2, small_sum = sum_grads(
            n_tensor,
            *(g.reshape(n_tensor, 2, 2, 2, rows, width) for g in grads),
            sent.reshape((n_tensor * owners,) + block),
        )
        small_sum = small_sum.reshape(-1)[:n_values]
    else:
        r0, r1, r2 = (
            lax.psum_scatter(
                lax.psum_scatter(g, "tensor", scatter_dimension=0), ("dp", "ctx"), scatter_dimension=0, tiled=True
            ).astype(F32)
            for g in grads
        )
        small_sum = lax.psum_scatter(
            lax.psum_scatter(small_grads, "tensor", scatter_dimension=0), ("dp", "ctx"), scatter_dimension=0
        )
    triple_out = jnp.transpose(r0[:, : 3 * part].reshape(rows, 3, part), (1, 0, 2))
    narrow_out = small_sum[: 8 * small_part].reshape(8, 1, small_part)
    outputs_rows, inputs_gradient = (
        jnp.transpose(v.reshape(batch, span, width), (1, 0, 2)) for v in (outputs_rows, inputs_gradient)
    )
    return (
        outputs_rows,
        inputs_gradient,
        triple_out,
        narrow_out[:2],
        r0[:, 3 * part :].T,
        narrow_out[2],
        narrow_out[3],
        narrow_out[4],
        r1,
        small_sum[8 * small_part :].reshape(1, unit_part),
        r2.T,
        narrow_out[5],
        narrow_out[6],
        narrow_out[7],
    )


def solution(mesh):
    in_specs = (
        P(("ctx", "tensor"), "dp", None),
        P(("ctx", "tensor"), "dp", None),
        P("dp", None),
        P(None, ("dp", "ctx"), "tensor"),
        P(None, "tensor", ("dp", "ctx")),
        P("tensor", ("dp", "ctx")),
        P("tensor", ("dp", "ctx")),
        P("tensor", ("dp", "ctx")),
        P("tensor", ("dp", "ctx")),
        P(("dp", "ctx"), "tensor"),
        P("tensor", ("dp", "ctx")),
        P("tensor", ("dp", "ctx")),
        P("tensor", ("dp", "ctx")),
        P("tensor", ("dp", "ctx")),
        P("tensor", ("dp", "ctx")),
    )
    out_specs = (
        P(("ctx", "tensor"), "dp", None),
        P(("ctx", "tensor"), "dp", None),
        P(None, ("dp", "ctx"), "tensor"),
        P(None, "tensor", ("dp", "ctx")),
        P("tensor", ("dp", "ctx")),
        P("tensor", ("dp", "ctx")),
        P("tensor", ("dp", "ctx")),
        P("tensor", ("dp", "ctx")),
        P(("dp", "ctx"), "tensor"),
        P("tensor", ("dp", "ctx")),
        P("tensor", ("dp", "ctx")),
        P("tensor", ("dp", "ctx")),
        P("tensor", ("dp", "ctx")),
        P("tensor", ("dp", "ctx")),
    )
    return jax.shard_map(local, mesh=mesh, in_specs=in_specs, out_specs=out_specs, check_vma=False)
```

```python
import functools

import jax
import jax.numpy as jnp
import numpy as np
from jax import lax
from jax.experimental import pallas as pl
from jax.experimental.pallas import tpu as pltpu
from jax.sharding import PartitionSpec as P

HEAD_DIM = 64

EPS = 1e-12
NEG = -1e30
SCALE = 0.125
MESH = pl.DeviceIdType.MESH
BF16 = jnp.bfloat16
F32 = jnp.float32
ALL = ("dp", "ctx", "tensor")
TOKENS = ("ctx", "tensor")


def at(dp, ctx, tensor):
    return {"dp": dp, "ctx": ctx, "tensor": tensor}


def remote(src, dst, send, recv, where):
    return pltpu.make_async_remote_copy(
        src_ref=src, dst_ref=dst, send_sem=send, recv_sem=recv, device_id=where, device_id_type=MESH
    )


def greet(peers):
    barrier = pltpu.get_barrier_semaphore()
    for peer in peers:
        pl.semaphore_signal(barrier, inc=1, device_id=peer, device_id_type=MESH)
    pl.semaphore_wait(barrier, len(peers))


def everyone(n_dp, n_ctx, n_tensor):
    dp, ctx, tensor = (lax.axis_index(a) for a in ALL)
    peers = []
    for i in range(n_dp):
        for j in range(n_ctx):
            for k in range(n_tensor):
                if i or j or k:
                    peers.append(
                        (lax.rem(dp + i, n_dp), lax.rem(ctx + j, n_ctx), lax.rem(tensor + k, n_tensor))
                    )
    return peers


def place(rows, names):
    part = rows["part"]
    owners = rows["owners"]
    piece = part // owners
    spread = np.zeros((128, 3 * part), np.float32)
    owned = np.zeros((owners, 3 * part), np.float32)
    for first, start in names:
        for n in range(part):
            spread[first + n % piece, start + n] = 1.0
            owned[n // piece, start + n] = 1.0
    return jnp.asarray(spread, BF16), jnp.asarray(owned)


def forward_kernel(n_tensor, heads, x, w0, w1, w2, small, spread, owned, seg_row, seg_col,
                   f0, f1, f2, small_all, rows, mixed_float, probs_out, mixed,
                   send_rows, send_mixed, probs,
                   own_sem, z_send, z_recv, x_send, x_recv, y_send, y_recv, a_send, a_recv, b_send, b_recv,
                   c_send, c_recv, s_send, s_recv, q_send, q_recv, m_send, m_recv, p_sem):
    shards, outs = (w0, w1, w2), (f0, f1, f2)
    dp, ctx, z = (lax.axis_index(a) for a in ALL)
    n_ctx = 2
    n_rows = w0.shape[0]
    half = n_rows // 2
    xp = lax.rem(dp + 2, 4)
    cp = dp + 1 - 2 * lax.rem(dp, 2)
    yp = 1 - ctx
    xcp = lax.rem(cp + 2, 4)
    me = dp * 2 + ctx
    mine = z * 8 + me
    peers = everyone(4, 2, n_tensor)
    greet([at(*p) for p in peers])
    x_dev, y_dev, c_dev = at(xp, ctx, z), at(dp, yp, z), at(cp, ctx, z)
    x_slot, y_slot, d_slot = xp * 2 + ctx, dp * 2 + yp, xp * 2 + yp
    slots = (cp * 2 + ctx, xcp * 2 + ctx, cp * 2 + yp, xcp * 2 + yp)

    def to_z(g, k):
        there = lax.rem(z + k, n_tensor)
        return remote(shards[g], outs[g].at[z, me], z_send.at[g, there], z_recv.at[g, z], at(dp, ctx, there))

    def from_z(g, origin):
        block = outs[g].at[origin, me]
        return remote(block, block, z_send.at[g, origin], z_recv.at[g, origin], x_dev)

    def along(g, origin, slot, send, recv, dev, src=None):
        block = outs[g].at[origin, slot]
        return remote(block if src is None else src, block, send.at[g, origin], recv.at[g, origin], dev)

    def part(g, origin, slot, lo, send, recv, dev):
        block = outs[g].at[origin, slot, pl.ds(lo, half)]
        return remote(block, block, send.at[g, origin], recv.at[g, origin], dev)

    def core(g, origin, kind, slot, src=None):
        block = outs[g].at[origin, slot]
        return remote(
            block if src is None else src, block, c_send.at[g, kind, origin], c_recv.at[g, kind, origin], c_dev
        )

    def back(j):
        return lax.rem(z + n_tensor - j, n_tensor)

    own = [pltpu.make_async_copy(shards[g], outs[g].at[z, me], own_sem.at[g]) for g in range(3)]

    def begin(g, far):
        if not far:
            along(g, z, me, x_send, x_recv, x_dev, shards[g]).start()
            along(g, z, me, y_send, y_recv, y_dev, shards[g]).start()
            core(g, z, 0, me, shards[g]).start()
            own[g].start()
        else:
            for k in range(1, n_tensor):
                to_z(g, k).start()

    def column(g, origin):
        from_z(g, origin).wait_recv()
        along(g, origin, me, x_send, x_recv, x_dev).start()
        along(g, origin, me, y_send, y_recv, y_dev).start()
        core(g, origin, 0, me).start()

    def sides(g, origin):
        along(g, origin, x_slot, x_send, x_recv, x_dev).wait_recv()
        part(g, origin, x_slot, 0, a_send, a_recv, y_dev).start()
        core(g, origin, 1, x_slot).start()
        along(g, origin, y_slot, y_send, y_recv, y_dev).wait_recv()
        part(g, origin, y_slot, half, b_send, b_recv, x_dev).start()
        core(g, origin, 2, y_slot).start()

    def corner(g, origin):
        part(g, origin, d_slot, 0, a_send, a_recv, y_dev).wait_recv()
        part(g, origin, d_slot, half, b_send, b_recv, x_dev).wait_recv()
        core(g, origin, 3, d_slot).start()

    def partner(g, origin):
        for kind in range(4):
            core(g, origin, kind, slots[kind]).wait_recv()

    begin(0, True)
    begin(0, False)
    small_own = pltpu.make_async_copy(small, small_all.at[mine], s_send.at[0])
    small_own.start()
    for n, p in enumerate(peers):
        remote(small, small_all.at[mine], s_send.at[n + 1], s_recv.at[n], at(*p)).start()

    def first(j, carry):
        @pl.when((j >= 1) & (j < n_tensor))
        def _():
            column(0, back(j))

        @pl.when((j >= 1) & (j < n_tensor + 1))
        def _():
            sides(0, back(j - 1))

        @pl.when(j >= 2)
        def _():
            corner(0, back(j - 2))

        return carry

    lax.fori_loop(0, n_tensor + 2, first, 0)
    for g in (1, 2):
        begin(g, False)
    small_own.wait()
    for n, p in enumerate(peers):
        copy = remote(small, small_all.at[mine], s_send.at[n + 1], s_recv.at[n], at(*p))
        copy.wait_send()
        copy.wait_recv()
    own[0].wait()

    def to_heads(t, c):
        return remote(send_rows.at[t, c], rows.at[ctx * n_tensor + z], q_send.at[t, c],
                      q_recv.at[ctx * n_tensor + z], at(dp, c, t))

    def from_token(block):
        return remote(rows.at[block], rows.at[block], q_send.at[0, 0], q_recv.at[block], x_dev)

    span = x.shape[0] // n_ctx
    wide = spread.shape[1]
    here = pltpu.make_async_copy(send_rows.at[z, ctx], rows.at[ctx * n_tensor + z], own_sem.at[3])

    def project(j, carry):
        t = lax.rem(z + 1 + j, n_tensor)
        partner(0, t)
        vectors = small_all[pl.ds(t * 8, 8), 0, :].astype(BF16)
        vectors = jnp.dot(vectors, spread[...], preferred_element_type=F32)
        bias = jnp.sum(vectors * owned[...], axis=0, keepdims=True)
        weight = f0[t].reshape(8 * n_rows, f0.shape[-1])
        value = jnp.dot(x[...], weight, preferred_element_type=F32)[:, :wide] + bias
        send_rows[t] = value.astype(BF16).reshape(n_ctx, span, wide)

        @pl.when(t != z)
        def _():
            to_heads(t, yp).start()
            to_heads(t, ctx).start()

        @pl.when(t == z)
        def _():
            to_heads(t, yp).start()
            here.start()

        return carry

    lax.fori_loop(0, n_tensor, project, 0)
    for g in (1, 2):
        sides(g, z)
    for g in (1, 2):
        corner(g, z)
    for g in (1, 2):
        begin(g, True)
    here.wait()
    for j in range(n_ctx):
        for k in range(n_tensor):
            if j or k:
                from_token(lax.rem(ctx + j, n_ctx) * n_tensor + lax.rem(z + k, n_tensor)).wait_recv()

    n_blocks = n_ctx * n_tensor
    total_rows = n_blocks * span
    n_units = n_blocks // 2

    def to_tokens(block):
        c, t = lax.div(block, n_tensor), lax.rem(block, n_tensor)
        return remote(send_mixed.at[block], mixed.at[z * n_ctx + ctx], m_send.at[block],
                      m_recv.at[z * n_ctx + ctx], at(dp, c, t))

    def keep(i):
        return pltpu.make_async_copy(probs.at[:, pl.ds(i * 2 * span, 2 * span)],
                                     probs_out.at[:, pl.ds(i * 2 * span, 2 * span)], p_sem.at[i])

    own_block = ctx * n_tensor + z
    own_mixed = pltpu.make_async_copy(send_mixed.at[own_block], mixed.at[z * n_ctx + ctx], own_sem.at[4])

    def attend(i, carry):
        blocks = pl.ds(2 * i, 2)
        lines = pl.ds(pl.multiple_of(i * 2 * span, 2 * span), 2 * span)
        allowed = seg_col[lines, :] == seg_row[...]
        for h in range(heads):
            q = rows[blocks, :, pl.ds(HEAD_DIM * h, HEAD_DIM)].reshape(2 * span, HEAD_DIM)
            k = rows[:, :, pl.ds(HEAD_DIM * (heads + h), HEAD_DIM)].reshape(total_rows, HEAD_DIM)
            v = rows[:, :, pl.ds(HEAD_DIM * (2 * heads + h), HEAD_DIM)].reshape(total_rows, HEAD_DIM)
            scores = SCALE * lax.dot_general(q, k, (((1,), (1,)), ((), ())), preferred_element_type=F32)
            scores = jnp.where(allowed, scores, NEG)
            weights = jnp.exp(scores - jnp.max(scores, axis=-1, keepdims=True))
            low = (weights * (1.0 / jnp.sum(weights, axis=-1, keepdims=True))).astype(BF16)
            probs[h, lines, :] = low
            value = jnp.dot(low, v, preferred_element_type=F32)
            mixed_float[lines, pl.ds(HEAD_DIM * h, HEAD_DIM)] = value
            send_mixed[blocks, :, pl.ds(HEAD_DIM * h, HEAD_DIM)] = value.astype(BF16).reshape(2, span, HEAD_DIM)
        keep(i).start()
        for n in range(2):
            @pl.when(2 * i + n != own_block)
            def _():
                to_tokens(2 * i + n).start()

            @pl.when(2 * i + n == own_block)
            def _():
                own_mixed.start()

        @pl.when((i >= 1) & (i < n_tensor))
        def _():
            for g in (1, 2):
                column(g, back(i))

        @pl.when((i >= 2) & (i < n_tensor))
        def _():
            for g in (1, 2):
                sides(g, back(i - 1))

        return carry

    lax.fori_loop(0, n_units, attend, 0)

    def rest(j, carry):
        @pl.when((j >= n_units) & (j < n_tensor))
        def _():
            for g in (1, 2):
                column(g, back(j))

        @pl.when((j >= n_units) & (j < n_tensor + 1))
        def _():
            for g in (1, 2):
                sides(g, back(j - 1))

        @pl.when(j >= 3)
        def _():
            for g in (1, 2):
                corner(g, back(j - 2))

        return carry

    lax.fori_loop(3, n_tensor + 2, rest, 0)

    own_mixed.wait()
    for j in range(n_ctx):
        for k in range(n_tensor):
            if j or k:
                c, t = lax.rem(ctx + j, n_ctx), lax.rem(z + k, n_tensor)
                slot = t * n_ctx + c
                remote(mixed.at[slot], mixed.at[slot], m_send.at[0], m_recv.at[slot], x_dev).wait_recv()
                to_tokens(c * n_tensor + t).wait_send()
                to_heads(t, c).wait_send()
    for i in range(n_units):
        keep(i).wait()

    def finish(origin, carry):
        for g in range(3):
            if g:
                partner(g, origin)
            for kind in range(4):
                core(g, origin, kind, slots[kind]).wait_send()
            along(g, origin, me, x_send, x_recv, x_dev).wait_send()
            along(g, origin, me, y_send, y_recv, y_dev).wait_send()
            part(g, origin, x_slot, 0, a_send, a_recv, y_dev).wait_send()
            part(g, origin, y_slot, half, b_send, b_recv, x_dev).wait_send()
        return carry

    lax.fori_loop(0, n_tensor, finish, 0)
    for g in range(3):
        if g:
            own[g].wait()
        for k in range(1, n_tensor):
            to_z(g, k).wait_send()


def forward_attention(n_tensor, heads, x, w0, w1, w2, small, spread, owned, seg_row, seg_col):
    rows, cols = w0.shape
    n_small = 8 * n_tensor
    blocks = 2 * n_tensor
    span = x.shape[0] // 2
    length = blocks * span
    part = heads * HEAD_DIM
    dma = pltpu.SemaphoreType.DMA
    shape = jax.ShapeDtypeStruct
    full = shape((n_tensor, 8, rows, cols), BF16)
    pair = [dma((3, n_tensor)), dma((3, n_tensor))]
    vmem = pl.BlockSpec(memory_space=pltpu.VMEM)
    hbm = pl.BlockSpec(memory_space=pl.ANY)
    return pl.pallas_call(
        functools.partial(forward_kernel, n_tensor, heads),
        out_shape=(
            full, full, full, shape((n_small,) + small.shape, F32), shape((blocks, span, 3 * part), BF16),
            shape((length, part), F32), shape((heads, length, length), BF16), shape((blocks, span, part), BF16),
        ),
        in_specs=[vmem] * 9,
        out_specs=(vmem, hbm, hbm, vmem, vmem, vmem, hbm, vmem),
        scratch_shapes=[
            pltpu.VMEM((n_tensor, 2, span, 3 * part), BF16),
            pltpu.VMEM((blocks, span, part), BF16),
            pltpu.VMEM((heads, length, length), BF16),
            dma((5,)),
        ] + pair * 5 + [
            dma((3, 4, n_tensor)), dma((3, 4, n_tensor)), dma((n_small,)), dma((n_small,)),
            dma((n_tensor, 2)), dma((blocks,)), dma((blocks,)), dma((blocks,)), dma((blocks // 2,)),
        ],
        compiler_params=pltpu.CompilerParams(collective_id=0, has_side_effects=True, vmem_limit_bytes=56 << 20),
        cost_estimate=pl.CostEstimate(flops=0, bytes_accessed=w0.size * 400, transcendentals=0),
        name="forward_attention",
    )(x, w0, w1, w2, small, spread, owned, seg_row, seg_col)


def sum_steps(n_tensor, grads, acc, core_in, y1_in, x1_in, x2_in, y2_in, z_in, load_sem, c_send, c_recv,
              y1_send, y1_recv, x1_send, x1_recv, x2_send, x2_recv, y2_send, y2_recv, z_send, z_recv):
    dp, ctx, z = (lax.axis_index(a) for a in ALL)
    rows = acc.shape[-2]
    half = rows // 2
    core = lax.rem(dp, 2)
    x = lax.div(dp, 2)
    xp, yp = 1 - x, 1 - ctx
    x_dev, y_dev, c_dev = at(xp * 2 + core, ctx, z), at(dp, yp, z), at(x * 2 + 1 - core, ctx, z)
    low, high = pl.ds(0, half), pl.ds(half, half)
    count = range(len(grads))

    def load(g, t):
        return pltpu.make_async_copy(grads[g].at[t, :, core], acc.at[g, t], load_sem.at[g, t])

    def to_core(g, t):
        return remote(grads[g].at[t, :, 1 - core], core_in.at[g, t], c_send.at[g, t], c_recv.at[g, t], c_dev)

    def y1(g, t):
        return remote(acc.at[g, t, :, yp, low], y1_in.at[g, t], y1_send.at[g, t], y1_recv.at[g, t], y_dev)

    def x1(g, t):
        return remote(acc.at[g, t, xp, :, high], x1_in.at[g, t], x1_send.at[g, t], x1_recv.at[g, t], x_dev)

    def x2(g, t):
        return remote(acc.at[g, t, xp, ctx, low], x2_in.at[g, t], x2_send.at[g, t], x2_recv.at[g, t], x_dev)

    def y2(g, t):
        return remote(acc.at[g, t, x, yp, high], y2_in.at[g, t], y2_send.at[g, t], y2_recv.at[g, t], y_dev)

    def to_z(g, t):
        return remote(acc.at[g, t, x, ctx], z_in.at[g, z], z_send.at[g, t], z_recv.at[g, z], at(dp, ctx, t))

    def add(a, b):
        return (a.astype(F32) + b.astype(F32)).astype(BF16)

    def target(j):
        return lax.rem(z + 1 + j, n_tensor)

    def begin():
        def one(j, carry):
            t = target(j)
            for g in count:
                to_core(g, t).start()
                load(g, t).start()
            return carry

        lax.fori_loop(0, n_tensor, one, 0)

    def core_step(j):
        t = target(j)
        for g in count:
            load(g, t).wait()
            to_core(g, t).wait_recv()
            acc[g, t] = add(acc[g, t], core_in[g, t])
            y1(g, t).start()
            x1(g, t).start()

    def first_step(j):
        t = target(j)
        for g in count:
            y1(g, t).wait_recv()
            for i in range(2):
                acc[g, t, i, ctx, low] = add(acc[g, t, i, ctx, low], y1_in[g, t, i])
            x2(g, t).start()
            x1(g, t).wait_recv()
            for i in range(2):
                acc[g, t, x, i, high] = add(acc[g, t, x, i, high], x1_in[g, t, i])
            y2(g, t).start()

    def second_step(j):
        t = target(j)
        for g in count:
            x2(g, t).wait_recv()
            acc[g, t, x, ctx, low] = add(acc[g, t, x, ctx, low], x2_in[g, t])
            y2(g, t).wait_recv()
            acc[g, t, x, ctx, high] = add(acc[g, t, x, ctx, high], y2_in[g, t])

            @pl.when(j < n_tensor - 1)
            def _():
                to_z(g, t).start()

    def step(j):
        @pl.when(j < n_tensor)
        def _():
            core_step(j)

        @pl.when((j >= 1) & (j < n_tensor + 1))
        def _():
            first_step(j - 1)

        @pl.when(j >= 2)
        def _():
            second_step(j - 2)

    def end(outs):
        for g in count:
            outs[g][...] = acc[g, z, x, ctx].astype(F32)
            for k in range(1, n_tensor):
                origin = lax.rem(z + n_tensor - k, n_tensor)
                block = z_in.at[g, origin]
                remote(block, block, z_send.at[g, origin], z_recv.at[g, origin], x_dev).wait_recv()
                outs[g][...] += z_in[g, origin].astype(F32)

        def finish(t, carry):
            for g in count:
                for copy in (to_core, y1, x1, x2, y2):
                    copy(g, t).wait_send()
            return carry

        lax.fori_loop(0, n_tensor, finish, 0)
        for g in count:
            for k in range(1, n_tensor):
                to_z(g, lax.rem(z + k, n_tensor)).wait_send()

    return begin, step, end


def sum_scratch(n_grads, n_tensor, rows, cols):
    dma = pltpu.SemaphoreType.DMA
    grid = (n_grads, n_tensor)
    half = rows // 2
    return [
        pltpu.VMEM(grid + (2, 2, rows, cols), BF16),
        pltpu.VMEM(grid + (2, 2, rows, cols), BF16),
        pltpu.VMEM(grid + (2, half, cols), BF16),
        pltpu.VMEM(grid + (2, half, cols), BF16),
        pltpu.VMEM(grid + (half, cols), BF16),
        pltpu.VMEM(grid + (half, cols), BF16),
        pltpu.VMEM(grid + (rows, cols), BF16),
    ] + [dma(grid)] * 13


def sum_kernel(n_tensor, grad, small, out, small_out, small_in, s_send, s_recv, *scratch):
    dp, ctx, z = (lax.axis_index(a) for a in ALL)
    mine = z * 8 + dp * 2 + ctx
    peers = everyone(4, 2, n_tensor)
    greet([at(*p) for p in peers])
    begin, step, end = sum_steps(n_tensor, (grad,), *scratch)
    begin()
    small_copies = [
        remote(small.at[pt * 8 + pd * 2 + pc], small_in.at[n], s_send.at[n], s_recv.at[n], at(pd, pc, pt))
        for n, (pd, pc, pt) in enumerate(peers)
    ]
    for copy in small_copies:
        copy.start()

    def one(j, carry):
        step(j)
        return carry

    lax.fori_loop(0, n_tensor + 2, one, 0)
    end((out,))
    total = small[mine]
    for n in range(len(peers)):
        small_copies[n].wait()
        total = total + small_in[n]
    small_out[...] = total


def sum_grads(n_tensor, grad, small):
    rows, cols = grad.shape[-2:]
    n_small = 8 * n_tensor
    dma = pltpu.SemaphoreType.DMA
    vmem = pl.BlockSpec(memory_space=pltpu.VMEM)
    return pl.pallas_call(
        functools.partial(sum_kernel, n_tensor),
        out_shape=(jax.ShapeDtypeStruct((rows, cols), F32), jax.ShapeDtypeStruct(small.shape[1:], F32)),
        in_specs=[pl.BlockSpec(memory_space=pl.ANY), vmem],
        out_specs=(vmem,) * 2,
        scratch_shapes=[pltpu.VMEM((n_small - 1,) + small.shape[1:], F32)] + [dma((n_small - 1,))] * 2
        + sum_scratch(1, n_tensor, rows, cols),
        compiler_params=pltpu.CompilerParams(collective_id=1, has_side_effects=True, vmem_limit_bytes=56 << 20),
        cost_estimate=pl.CostEstimate(flops=0, bytes_accessed=grad.size * 12, transcendentals=0),
        name="sum_grads",
    )(grad, small)


def backward_kernel(n_tensor, heads, mixed_grad, rows, mixed_float, probs_in, g1, g2, qkv_grad, o1, o2,
                    grad, probs, send_rows, key_sum, value_sum, own_sem, g_send, g_recv, q_send, q_recv, p_sem,
                    *scratch):
    dp, ctx, z = (lax.axis_index(a) for a in ALL)
    n_ctx = 2
    n_blocks = n_ctx * n_tensor
    n_units = n_blocks // 2
    span = grad.shape[1]
    total_rows = n_blocks * span
    own_block = ctx * n_tensor + z
    own_slot = z * n_ctx + ctx
    greet([at(*p) for p in everyone(4, 2, n_tensor)])
    others = [(lax.rem(ctx + j, n_ctx), lax.rem(z + k, n_tensor))
              for k in (2, 3, 1, 0) for j in range(n_ctx) if (j or k) and k < n_tensor]
    begin, step, end = sum_steps(n_tensor, (g1, g2), *scratch)

    def to_heads(c, t):
        return remote(mixed_grad.at[t * n_ctx + c], grad.at[own_block], g_send.at[t * n_ctx + c],
                      g_recv.at[own_block], at(dp, c, t))

    def load(i):
        lines = pl.ds(i * 2 * span, 2 * span)
        return pltpu.make_async_copy(probs_in.at[:, lines], probs.at[:, lines], p_sem.at[i])

    here = pltpu.make_async_copy(mixed_grad.at[own_slot], grad.at[own_block], own_sem.at[0])
    for c, t in others:
        to_heads(c, t).start()
    here.start()
    for i in range(n_units):
        load(i).start()
    begin()
    step(0)
    here.wait()
    for c, t in others:
        block = c * n_tensor + t
        remote(grad.at[block], grad.at[block], g_send.at[0], g_recv.at[block], at(dp, c, t)).wait_recv()
    for i in range(n_units):
        load(i).wait()

    def one_head(h):
        lanes = pl.ds(HEAD_DIM * h, HEAD_DIM)
        k_lanes = pl.ds(HEAD_DIM * (heads + h), HEAD_DIM)
        v_lanes = pl.ds(HEAD_DIM * (2 * heads + h), HEAD_DIM)
        key_sum[...] = jnp.zeros_like(key_sum)
        value_sum[...] = jnp.zeros_like(value_sum)

        def unit(i, carry):
            blocks = pl.ds(2 * i, 2)
            lines = pl.ds(pl.multiple_of(i * 2 * span, 2 * span), 2 * span)
            q = rows[blocks, :, lanes].reshape(2 * span, HEAD_DIM)
            k = rows[:, :, k_lanes].reshape(total_rows, HEAD_DIM)
            v = rows[:, :, v_lanes].reshape(total_rows, HEAD_DIM)
            up = grad[blocks, :, lanes].reshape(2 * span, HEAD_DIM)
            low = probs[h, lines, :]
            delta = jnp.sum(up.astype(F32) * mixed_float[lines, lanes], axis=-1, keepdims=True)
            pull = lax.dot_general(up, v, (((1,), (1,)), ((), ())), preferred_element_type=F32)
            score = (low.astype(F32) * (pull - delta)).astype(BF16)
            query = SCALE * jnp.dot(score, k, preferred_element_type=F32)
            send_rows[blocks, :, lanes] = query.astype(BF16).reshape(2, span, HEAD_DIM)
            key_sum[...] += lax.dot_general(q, score, (((0,), (0,)), ((), ())), preferred_element_type=F32)
            value_sum[...] += lax.dot_general(up, low, (((0,), (0,)), ((), ())), preferred_element_type=F32)
            return carry

        lax.fori_loop(0, n_units, unit, 0)
        key = (SCALE * key_sum[...]).T.astype(BF16)
        value = value_sum[...].T.astype(BF16)
        send_rows[:, :, k_lanes] = key.reshape(n_blocks, span, HEAD_DIM)
        send_rows[:, :, v_lanes] = value.reshape(n_blocks, span, HEAD_DIM)

    for h in range(heads):
        one_head(h)
        if h == 0:
            step(1)
        elif h == 1:
            step(2)

    def to_tokens(c, t):
        return remote(send_rows.at[c * n_tensor + t], qkv_grad.at[own_slot], q_send.at[c * n_tensor + t],
                      q_recv.at[own_slot], at(dp, c, t))

    there = pltpu.make_async_copy(send_rows.at[own_block], qkv_grad.at[own_slot], own_sem.at[1])
    for c, t in others:
        to_tokens(c, t).start()
    there.start()

    def one(j, carry):
        step(j)
        return carry

    lax.fori_loop(min(heads, 3), n_tensor + 2, one, 0)
    end((o1, o2))
    there.wait()
    for c, t in others:
        slot = t * n_ctx + c
        remote(qkv_grad.at[slot], qkv_grad.at[slot], q_send.at[0], q_recv.at[slot], at(dp, c, t)).wait_recv()
        to_tokens(c, t).wait_send()
        to_heads(c, t).wait_send()


def backward_attention(n_tensor, heads, mixed_grad, rows, mixed_float, probs, g1, g2):
    blocks, span, wide = rows.shape
    part = heads * HEAD_DIM
    length = blocks * span
    n_rows, cols = g1.shape[-2:]
    dma = pltpu.SemaphoreType.DMA
    vmem = pl.BlockSpec(memory_space=pltpu.VMEM)
    hbm = pl.BlockSpec(memory_space=pl.ANY)
    out = jax.ShapeDtypeStruct((n_rows, cols), F32)
    return pl.pallas_call(
        functools.partial(backward_kernel, n_tensor, heads),
        out_shape=(jax.ShapeDtypeStruct(rows.shape, BF16), out, out),
        in_specs=[vmem, vmem, vmem, hbm, hbm, hbm],
        out_specs=(vmem,) * 3,
        scratch_shapes=[
            pltpu.VMEM((blocks, span, part), BF16),
            pltpu.VMEM((heads, length, length), BF16),
            pltpu.VMEM((blocks, span, wide), BF16),
            pltpu.VMEM((HEAD_DIM, length), F32),
            pltpu.VMEM((HEAD_DIM, length), F32),
            dma((2,)), dma((blocks,)), dma((blocks,)), dma((blocks,)), dma((blocks,)), dma((blocks // 2,)),
        ] + sum_scratch(2, n_tensor, n_rows, cols),
        compiler_params=pltpu.CompilerParams(collective_id=2, has_side_effects=True, vmem_limit_bytes=58 << 20),
        cost_estimate=pl.CostEstimate(flops=0, bytes_accessed=g1.size * 24, transcendentals=0),
        name="backward_attention",
    )(mixed_grad, rows, mixed_float, probs, g1, g2)


def norm_rows(total, gain, shift):
    center = total - jnp.mean(total, axis=-1, keepdims=True)
    spread = jnp.mean(center * center, axis=-1, keepdims=True)
    return center * lax.rsqrt(spread + EPS) * gain + shift


def gelu_exact(before):
    share = 0.5 + 0.5 * lax.erf(before * 0.5**0.5)
    dense = (0.5 / np.pi) ** 0.5 * jnp.exp(-0.5 * before * before)
    return before * share, share + before * dense


def dot(spec, a, b):
    return jnp.einsum(spec, a, b, preferred_element_type=F32)


def add_up(spec, a, b):
    return sum(dot(spec, a[t], b[t]) for t in range(a.shape[0]))


def local(
    inputs,
    cotangent,
    segments,
    triple_weight,
    attend_bias,
    merge_weight,
    merge_bias,
    first_gain,
    first_shift,
    expand_weight,
    expand_bias,
    shrink_weight,
    shrink_bias,
    second_gain,
    second_shift,
):
    n_dp, n_ctx, n_tensor = (lax.axis_size(a) for a in ALL)
    span, batch, width = inputs.shape
    rows = triple_weight.shape[1]
    part = triple_weight.shape[2]
    units = expand_weight.shape[1]
    owners = n_dp * n_ctx
    heads = part // HEAD_DIM
    count = batch * span
    small_part = part // owners
    unit_part = units // owners
    own_kernels = n_dp == 4 and n_ctx == 2 and batch == 2 and n_tensor == 4 and rows % 32 == 0

    w0 = jnp.concatenate(
        [jnp.transpose(triple_weight, (1, 0, 2)).reshape(rows, 3 * part), merge_weight.T], axis=1
    )
    w2 = shrink_weight.T
    vectors = (merge_bias, first_gain, first_shift, shrink_bias, second_gain, second_shift)
    small = jnp.concatenate(
        [attend_bias[0, 0], attend_bias[1, 0]] + [v[0] for v in vectors] + [expand_bias[0]]
    ).astype(F32)
    n_values = small.shape[0]
    x_low = jnp.transpose(inputs, (1, 0, 2)).reshape(count, width)
    here = lax.axis_index("ctx")
    if own_kernels:
        pad = -n_values % 1024
        block = ((n_values + pad) // 128, 128)
        labels = lax.dynamic_slice_in_dim(segments, here, 1, 0)
        spread, owned = place({"part": part, "owners": owners}, ((0, 0), (small_part, 2 * part)))
        f0, f1, f2, small_all, rows_all, mixed_float, probs, mixed = forward_attention(
            n_tensor, heads, x_low, w0, expand_weight, w2, jnp.pad(small, (0, pad)).reshape(block),
            spread, owned, labels, labels.reshape(-1, 1)
        )
        mixed = mixed.reshape(n_tensor, count, part)
        small_all = small_all.reshape(n_tensor, owners, -1)[:, :, :n_values]
    else:
        f0, f1, f2 = (
            lax.all_gather(lax.all_gather(w, ("dp", "ctx"), axis=0, tiled=True), "tensor", axis=0, tiled=False)
            for w in (w0, expand_weight, w2)
        )
        small_all = lax.all_gather(lax.all_gather(small, ("dp", "ctx")), "tensor")
    f0, f1, f2 = (w.reshape(n_tensor, width, -1) for w in (f0, f1, f2))
    w_qkv, w_merge, w_expand, w_shrink = f0[:, :, : 3 * part], f0[:, :, 3 * part :], f1, f2
    narrow = small_all[:, :, : 8 * small_part].reshape(n_tensor, owners, 8, small_part)
    narrow = jnp.transpose(narrow, (2, 0, 1, 3)).reshape(8, n_tensor, part)
    merge_vec, gain_one, shift_one, shrink_vec, gain_two, shift_two = narrow[2:].reshape(6, width)
    expand_vec = small_all[:, :, 8 * small_part :].reshape(n_tensor, 1, units)
    qkv_vec = jnp.concatenate([narrow[0], jnp.zeros_like(narrow[0]), narrow[1]], axis=-1)[:, None]

    x = x_low.astype(F32)
    upstream = jnp.transpose(cotangent, (1, 0, 2)).reshape(count, width).astype(F32)

    def to_tokens(value):
        value = value.reshape(batch, n_tensor, span, -1)
        out = lax.all_to_all(jnp.transpose(value, (1, 0, 2, 3)), "tensor", split_axis=0, concat_axis=0)
        return out.reshape(n_tensor, count, -1)

    if not own_kernels:
        qkv = (dot("rd,tde->tre", x_low, w_qkv) + qkv_vec).astype(BF16)
        mine = lax.all_to_all(
            qkv.reshape(n_tensor, batch, span, 3 * part), "tensor", split_axis=0, concat_axis=0
        )
        mine = jnp.transpose(mine, (1, 0, 2, 3)).reshape(batch, n_tensor * span, 3 * part)
        n_query = n_tensor * span
        own_labels = lax.dynamic_slice_in_dim(segments, here * n_query, n_query, 1)
        kv_rows = lax.all_gather(mine[..., part:], "ctx", axis=1, tiled=True)
        n_key = kv_rows.shape[1]
        q_four = mine[..., :part].reshape(batch, n_query, heads, HEAD_DIM)
        k_four = kv_rows[..., :part].reshape(batch, n_key, heads, HEAD_DIM)
        v_four = kv_rows[..., part:].reshape(batch, n_key, heads, HEAD_DIM)
        allowed = own_labels[:, None, :, None] == segments[:, None, None, :]
        scores = jnp.where(allowed, SCALE * dot("sqhd,skhd->shqk", q_four, k_four), NEG)
        top = jnp.max(scores, axis=-1)
        weights = jnp.where(allowed, jnp.exp(scores - top[..., None]), 0.0)
        total = jnp.sum(weights, axis=-1)
        mixed_float = dot("shqk,skhd->shqd", weights.astype(BF16), v_four) / total[..., None]
        logsum = top + jnp.log(total)
        mixed = to_tokens(jnp.transpose(mixed_float, (0, 2, 1, 3)).reshape(batch, n_query, part).astype(BF16))

    first_sum = x + add_up("re,de->rd", mixed, w_merge) + merge_vec
    first_norm = norm_rows(first_sum, gain_one, shift_one)
    first_low = first_norm.astype(BF16)
    before = dot("rd,tdf->trf", first_low, w_expand) + expand_vec
    active, slope = gelu_exact(before)
    active = active.astype(BF16)
    second_sum = first_norm + add_up("rf,df->rd", active, w_shrink) + shrink_vec
    outputs_rows = norm_rows(second_sum, gain_two, shift_two)

    second_grad, gain_two_grad, shift_two_grad = jax.vjp(norm_rows, second_sum, gain_two, shift_two)[1](upstream)
    shrink_vec_grad = jnp.sum(second_grad, axis=0)
    second_low = second_grad.astype(BF16)
    shrink_grad = dot("rd,trf->tdf", second_low, active).astype(BF16)
    active_grad = dot("rd,tdf->trf", second_low, w_shrink)
    before_low = (active_grad * slope).astype(BF16)
    expand_vec_grad = jnp.sum(before_low.astype(F32), axis=1)
    expand_grad = dot("rd,trf->tdf", first_low, before_low).astype(BF16)
    norm_back = add_up("rf,df->rd", before_low, w_expand)
    first_grad, gain_one_grad, shift_one_grad = jax.vjp(norm_rows, first_sum, gain_one, shift_one)[1](
        second_grad + norm_back
    )
    merge_vec_grad = jnp.sum(first_grad, axis=0)
    first_low_grad = first_grad.astype(BF16)
    merge_grad = dot("rd,tre->tde", first_low_grad, mixed).astype(BF16)
    mixed_grad = dot("rd,tde->tre", first_low_grad, w_merge).astype(BF16)
    if own_kernels:
        qkv_grad, r1, r2 = backward_attention(
            n_tensor, heads, mixed_grad.reshape(rows_all.shape[:2] + (part,)), rows_all, mixed_float, probs,
            *(g.reshape(n_tensor, 2, 2, 2, rows, width) for g in (expand_grad, shrink_grad))
        )
        qkv_grad = qkv_grad.reshape(n_tensor, count, 3 * part)
    else:
        grad_rows = lax.all_to_all(
            mixed_grad.reshape(n_tensor, batch, span, part), "tensor", split_axis=0, concat_axis=0
        )
        grad_four = jnp.transpose(grad_rows, (1, 0, 2, 3)).reshape(batch, n_query, heads, HEAD_DIM)
        delta = jnp.sum(jnp.transpose(grad_four.astype(F32), (0, 2, 1, 3)) * mixed_float, axis=-1)
        back_scores = SCALE * dot("sqhd,skhd->shqk", q_four, k_four)
        probs = jnp.where(allowed, jnp.exp(back_scores - logsum[..., None]), 0.0)
        prob_grad = dot("sqhd,skhd->shqk", grad_four, v_four)
        score_low = (probs * (prob_grad - delta[..., None])).astype(BF16)
        value_part = dot("shqk,sqhd->skhd", probs.astype(BF16), grad_four)
        query_part = SCALE * dot("shqk,skhd->sqhd", score_low, k_four)
        key_part = SCALE * dot("shqk,sqhd->skhd", score_low, q_four)
        query_part, key_part, value_part = (
            v.reshape(batch, -1, part).astype(BF16) for v in (query_part, key_part, value_part)
        )
        key_part, value_part = (
            lax.psum_scatter(v, "ctx", scatter_dimension=1, tiled=True) for v in (key_part, value_part)
        )
        qkv_grad = to_tokens(jnp.concatenate([query_part, key_part, value_part], axis=-1))
    triple_grad = dot("rd,tre->tde", x_low, qkv_grad).astype(BF16)
    attend_grad = jnp.sum(qkv_grad.astype(F32), axis=1).reshape(n_tensor, 3, part)
    inputs_gradient = first_grad + add_up("re,de->rd", qkv_grad, w_qkv)

    vec_grads = jnp.stack(
        [merge_vec_grad, gain_one_grad, shift_one_grad, shrink_vec_grad, gain_two_grad, shift_two_grad]
    ).reshape(6, n_tensor, part)
    narrow_grads = jnp.concatenate(
        [jnp.stack([attend_grad[:, 0], attend_grad[:, 2]]), vec_grads]
    ).reshape(8, n_tensor, owners, small_part)
    narrow_grads = jnp.transpose(narrow_grads, (1, 2, 0, 3)).reshape(n_tensor, owners, 8 * small_part)
    small_grads = jnp.concatenate([narrow_grads, expand_vec_grad.reshape(n_tensor, owners, unit_part)], axis=-1)
    grads = (jnp.concatenate([triple_grad, merge_grad], axis=-1), expand_grad, shrink_grad)
    if own_kernels:
        sent = jnp.pad(small_grads.reshape(n_tensor * owners, n_values), ((0, 0), (0, pad)))
        r0, small_sum = sum_grads(
            n_tensor,
            grads[0].reshape(n_tensor, 2, 2, 2, rows, width),
            sent.reshape((n_tensor * owners,) + block),
        )
        small_sum = small_sum.reshape(-1)[:n_values]
    else:
        r0, r1, r2 = (
            lax.psum_scatter(
                lax.psum_scatter(g, "tensor", scatter_dimension=0), ("dp", "ctx"), scatter_dimension=0, tiled=True
            ).astype(F32)
            for g in grads
        )
        small_sum = lax.psum_scatter(
            lax.psum_scatter(small_grads, "tensor", scatter_dimension=0), ("dp", "ctx"), scatter_dimension=0
        )
    triple_out = jnp.transpose(r0[:, : 3 * part].reshape(rows, 3, part), (1, 0, 2))
    narrow_out = small_sum[: 8 * small_part].reshape(8, 1, small_part)
    outputs_rows, inputs_gradient = (
        jnp.transpose(v.reshape(batch, span, width), (1, 0, 2)) for v in (outputs_rows, inputs_gradient)
    )
    return (
        outputs_rows,
        inputs_gradient,
        triple_out,
        narrow_out[:2],
        r0[:, 3 * part :].T,
        narrow_out[2],
        narrow_out[3],
        narrow_out[4],
        r1,
        small_sum[8 * small_part :].reshape(1, unit_part),
        r2.T,
        narrow_out[5],
        narrow_out[6],
        narrow_out[7],
    )


def solution(mesh):
    in_specs = (
        P(("ctx", "tensor"), "dp", None),
        P(("ctx", "tensor"), "dp", None),
        P("dp", None),
        P(None, ("dp", "ctx"), "tensor"),
        P(None, "tensor", ("dp", "ctx")),
        P("tensor", ("dp", "ctx")),
        P("tensor", ("dp", "ctx")),
        P("tensor", ("dp", "ctx")),
        P("tensor", ("dp", "ctx")),
        P(("dp", "ctx"), "tensor"),
        P("tensor", ("dp", "ctx")),
        P("tensor", ("dp", "ctx")),
        P("tensor", ("dp", "ctx")),
        P("tensor", ("dp", "ctx")),
        P("tensor", ("dp", "ctx")),
    )
    out_specs = (
        P(("ctx", "tensor"), "dp", None),
        P(("ctx", "tensor"), "dp", None),
        P(None, ("dp", "ctx"), "tensor"),
        P(None, "tensor", ("dp", "ctx")),
        P("tensor", ("dp", "ctx")),
        P("tensor", ("dp", "ctx")),
        P("tensor", ("dp", "ctx")),
        P("tensor", ("dp", "ctx")),
        P(("dp", "ctx"), "tensor"),
        P("tensor", ("dp", "ctx")),
        P("tensor", ("dp", "ctx")),
        P("tensor", ("dp", "ctx")),
        P("tensor", ("dp", "ctx")),
        P("tensor", ("dp", "ctx")),
    )
    return jax.shard_map(local, mesh=mesh, in_specs=in_specs, out_specs=out_specs, check_vma=False)
```

```python
import functools

import jax
import jax.numpy as jnp
import numpy as np
from jax import lax
from jax.experimental import pallas as pl
from jax.experimental.pallas import tpu as pltpu
from jax.sharding import PartitionSpec as P

HEAD_DIM = 64

EPS = 1e-12
NEG = -1e30
SCALE = 0.125
MESH = pl.DeviceIdType.MESH
BF16 = jnp.bfloat16
F32 = jnp.float32
ALL = ("dp", "ctx", "tensor")
TOKENS = ("ctx", "tensor")


def at(dp, ctx, tensor):
    return {"dp": dp, "ctx": ctx, "tensor": tensor}


def remote(src, dst, send, recv, where):
    return pltpu.make_async_remote_copy(
        src_ref=src, dst_ref=dst, send_sem=send, recv_sem=recv, device_id=where, device_id_type=MESH
    )


def greet(peers):
    barrier = pltpu.get_barrier_semaphore()
    for peer in peers:
        pl.semaphore_signal(barrier, inc=1, device_id=peer, device_id_type=MESH)
    pl.semaphore_wait(barrier, len(peers))


def everyone(n_dp, n_ctx, n_tensor):
    dp, ctx, tensor = (lax.axis_index(a) for a in ALL)
    peers = []
    for i in range(n_dp):
        for j in range(n_ctx):
            for k in range(n_tensor):
                if i or j or k:
                    peers.append(
                        (lax.rem(dp + i, n_dp), lax.rem(ctx + j, n_ctx), lax.rem(tensor + k, n_tensor))
                    )
    return peers


def place(rows, names):
    part = rows["part"]
    owners = rows["owners"]
    piece = part // owners
    spread = np.zeros((128, 3 * part), np.float32)
    owned = np.zeros((owners, 3 * part), np.float32)
    for first, start in names:
        for n in range(part):
            spread[first + n % piece, start + n] = 1.0
            owned[n // piece, start + n] = 1.0
    return jnp.asarray(spread, BF16), jnp.asarray(owned)


def forward_kernel(n_tensor, heads, x, triple, merge, w1, shrink, small, spread, owned, seg_row, seg_col,
                   f0, f1, f2, small_all, rows, mixed_float, probs_out, mixed,
                   w0, w2, send_rows, send_mixed, probs,
                   own_sem, z_send, z_recv, x_send, x_recv, y_send, y_recv, a_send, a_recv, b_send, b_recv,
                   c_send, c_recv, s_send, s_recv, q_send, q_recv, m_send, m_recv, p_sem):
    shards, outs = (w0, w1, w2), (f0, f1, f2)
    dp, ctx, z = (lax.axis_index(a) for a in ALL)
    n_ctx = 2
    n_rows = w0.shape[0]
    half = n_rows // 2
    xp = lax.rem(dp + 2, 4)
    cp = dp + 1 - 2 * lax.rem(dp, 2)
    yp = 1 - ctx
    xcp = lax.rem(cp + 2, 4)
    me = dp * 2 + ctx
    mine = z * 8 + me
    peers = everyone(4, 2, n_tensor)
    wide = spread.shape[1]
    for i in range(3):
        w0[:, pl.ds(i * triple.shape[2], triple.shape[2])] = triple[i]
    w0[:, pl.ds(wide, merge.shape[0])] = merge[...].T
    w2[...] = shrink[...].T
    greet([at(*p) for p in peers])
    x_dev, y_dev, c_dev = at(xp, ctx, z), at(dp, yp, z), at(cp, ctx, z)
    x_slot, y_slot, d_slot = xp * 2 + ctx, dp * 2 + yp, xp * 2 + yp
    slots = (cp * 2 + ctx, xcp * 2 + ctx, cp * 2 + yp, xcp * 2 + yp)

    def to_z(g, k):
        there = lax.rem(z + k, n_tensor)
        return remote(shards[g], outs[g].at[z, me], z_send.at[g, there], z_recv.at[g, z], at(dp, ctx, there))

    def from_z(g, origin):
        block = outs[g].at[origin, me]
        return remote(block, block, z_send.at[g, origin], z_recv.at[g, origin], x_dev)

    def along(g, origin, slot, send, recv, dev, src=None):
        block = outs[g].at[origin, slot]
        return remote(block if src is None else src, block, send.at[g, origin], recv.at[g, origin], dev)

    def part(g, origin, slot, lo, send, recv, dev):
        block = outs[g].at[origin, slot, pl.ds(lo, half)]
        return remote(block, block, send.at[g, origin], recv.at[g, origin], dev)

    def core(g, origin, kind, slot, src=None):
        block = outs[g].at[origin, slot]
        return remote(
            block if src is None else src, block, c_send.at[g, kind, origin], c_recv.at[g, kind, origin], c_dev
        )

    def back(j):
        return lax.rem(z + n_tensor - j, n_tensor)

    own = [pltpu.make_async_copy(shards[g], outs[g].at[z, me], own_sem.at[g]) for g in range(3)]

    def begin(g, far):
        if not far:
            along(g, z, me, x_send, x_recv, x_dev, shards[g]).start()
            along(g, z, me, y_send, y_recv, y_dev, shards[g]).start()
            core(g, z, 0, me, shards[g]).start()
            own[g].start()
        else:
            for k in range(1, n_tensor):
                to_z(g, k).start()

    def column(g, origin):
        from_z(g, origin).wait_recv()
        along(g, origin, me, x_send, x_recv, x_dev).start()
        along(g, origin, me, y_send, y_recv, y_dev).start()
        core(g, origin, 0, me).start()

    def sides(g, origin):
        along(g, origin, x_slot, x_send, x_recv, x_dev).wait_recv()
        part(g, origin, x_slot, 0, a_send, a_recv, y_dev).start()
        core(g, origin, 1, x_slot).start()
        along(g, origin, y_slot, y_send, y_recv, y_dev).wait_recv()
        part(g, origin, y_slot, half, b_send, b_recv, x_dev).start()
        core(g, origin, 2, y_slot).start()

    def corner(g, origin):
        part(g, origin, d_slot, 0, a_send, a_recv, y_dev).wait_recv()
        part(g, origin, d_slot, half, b_send, b_recv, x_dev).wait_recv()
        core(g, origin, 3, d_slot).start()

    def partner(g, origin):
        for kind in range(4):
            core(g, origin, kind, slots[kind]).wait_recv()

    begin(0, True)
    begin(0, False)
    small_own = pltpu.make_async_copy(small, small_all.at[mine], s_send.at[0])
    small_own.start()
    for n, p in enumerate(peers):
        remote(small, small_all.at[mine], s_send.at[n + 1], s_recv.at[n], at(*p)).start()

    def first(j, carry):
        @pl.when((j >= 1) & (j < n_tensor))
        def _():
            column(0, back(j))

        @pl.when((j >= 1) & (j < n_tensor + 1))
        def _():
            sides(0, back(j - 1))

        @pl.when(j >= 2)
        def _():
            corner(0, back(j - 2))

        return carry

    lax.fori_loop(0, n_tensor + 2, first, 0)
    for g in (1, 2):
        begin(g, False)
    small_own.wait()
    for n, p in enumerate(peers):
        copy = remote(small, small_all.at[mine], s_send.at[n + 1], s_recv.at[n], at(*p))
        copy.wait_send()
        copy.wait_recv()
    own[0].wait()

    def to_heads(t, c):
        return remote(send_rows.at[t, c], rows.at[ctx * n_tensor + z], q_send.at[t, c],
                      q_recv.at[ctx * n_tensor + z], at(dp, c, t))

    def from_token(block):
        return remote(rows.at[block], rows.at[block], q_send.at[0, 0], q_recv.at[block], x_dev)

    span = x.shape[0] // n_ctx
    here = pltpu.make_async_copy(send_rows.at[z, ctx], rows.at[ctx * n_tensor + z], own_sem.at[3])

    def project(j, carry):
        t = lax.rem(z + 1 + j, n_tensor)
        partner(0, t)
        vectors = small_all[pl.ds(t * 8, 8), 0, :].astype(BF16)
        vectors = jnp.dot(vectors, spread[...], preferred_element_type=F32)
        bias = jnp.sum(vectors * owned[...], axis=0, keepdims=True)
        weight = f0[t].reshape(8 * n_rows, f0.shape[-1])
        value = jnp.dot(x[...], weight, preferred_element_type=F32)[:, :wide] + bias
        send_rows[t] = value.astype(BF16).reshape(n_ctx, span, wide)

        @pl.when(t != z)
        def _():
            to_heads(t, yp).start()
            to_heads(t, ctx).start()

        @pl.when(t == z)
        def _():
            to_heads(t, yp).start()
            here.start()

        return carry

    lax.fori_loop(0, n_tensor, project, 0)
    for g in (1, 2):
        sides(g, z)
    for g in (1, 2):
        corner(g, z)
    for g in (1, 2):
        begin(g, True)
    here.wait()
    for j in range(n_ctx):
        for k in range(n_tensor):
            if j or k:
                from_token(lax.rem(ctx + j, n_ctx) * n_tensor + lax.rem(z + k, n_tensor)).wait_recv()

    n_blocks = n_ctx * n_tensor
    total_rows = n_blocks * span
    n_units = n_blocks // 2

    def to_tokens(block):
        c, t = lax.div(block, n_tensor), lax.rem(block, n_tensor)
        return remote(send_mixed.at[block], mixed.at[z * n_ctx + ctx], m_send.at[block],
                      m_recv.at[z * n_ctx + ctx], at(dp, c, t))

    def keep(i):
        return pltpu.make_async_copy(probs.at[:, pl.ds(i * 2 * span, 2 * span)],
                                     probs_out.at[:, pl.ds(i * 2 * span, 2 * span)], p_sem.at[i])

    own_block = ctx * n_tensor + z
    own_mixed = pltpu.make_async_copy(send_mixed.at[own_block], mixed.at[z * n_ctx + ctx], own_sem.at[4])

    def attend(i, carry):
        blocks = pl.ds(2 * i, 2)
        lines = pl.ds(pl.multiple_of(i * 2 * span, 2 * span), 2 * span)
        allowed = seg_col[lines, :] == seg_row[...]
        for h in range(heads):
            q = rows[blocks, :, pl.ds(HEAD_DIM * h, HEAD_DIM)].reshape(2 * span, HEAD_DIM)
            k = rows[:, :, pl.ds(HEAD_DIM * (heads + h), HEAD_DIM)].reshape(total_rows, HEAD_DIM)
            v = rows[:, :, pl.ds(HEAD_DIM * (2 * heads + h), HEAD_DIM)].reshape(total_rows, HEAD_DIM)
            scores = SCALE * lax.dot_general(q, k, (((1,), (1,)), ((), ())), preferred_element_type=F32)
            scores = jnp.where(allowed, scores, NEG)
            weights = jnp.exp(scores - jnp.max(scores, axis=-1, keepdims=True))
            low = (weights * (1.0 / jnp.sum(weights, axis=-1, keepdims=True))).astype(BF16)
            probs[h, lines, :] = low
            value = jnp.dot(low, v, preferred_element_type=F32)
            mixed_float[lines, pl.ds(HEAD_DIM * h, HEAD_DIM)] = value
            send_mixed[blocks, :, pl.ds(HEAD_DIM * h, HEAD_DIM)] = value.astype(BF16).reshape(2, span, HEAD_DIM)
        keep(i).start()
        for n in range(2):
            @pl.when(2 * i + n != own_block)
            def _():
                to_tokens(2 * i + n).start()

            @pl.when(2 * i + n == own_block)
            def _():
                own_mixed.start()

        @pl.when((i >= 1) & (i < n_tensor))
        def _():
            for g in (1, 2):
                column(g, back(i))

        @pl.when((i >= 2) & (i < n_tensor))
        def _():
            for g in (1, 2):
                sides(g, back(i - 1))

        return carry

    lax.fori_loop(0, n_units, attend, 0)

    def rest(j, carry):
        @pl.when((j >= n_units) & (j < n_tensor))
        def _():
            for g in (1, 2):
                column(g, back(j))

        @pl.when((j >= n_units) & (j < n_tensor + 1))
        def _():
            for g in (1, 2):
                sides(g, back(j - 1))

        @pl.when(j >= 3)
        def _():
            for g in (1, 2):
                corner(g, back(j - 2))

        return carry

    lax.fori_loop(3, n_tensor + 2, rest, 0)

    own_mixed.wait()
    for j in range(n_ctx):
        for k in range(n_tensor):
            if j or k:
                c, t = lax.rem(ctx + j, n_ctx), lax.rem(z + k, n_tensor)
                slot = t * n_ctx + c
                remote(mixed.at[slot], mixed.at[slot], m_send.at[0], m_recv.at[slot], x_dev).wait_recv()
                to_tokens(c * n_tensor + t).wait_send()
                to_heads(t, c).wait_send()
    for i in range(n_units):
        keep(i).wait()

    def finish(origin, carry):
        for g in range(3):
            if g:
                partner(g, origin)
            for kind in range(4):
                core(g, origin, kind, slots[kind]).wait_send()
            along(g, origin, me, x_send, x_recv, x_dev).wait_send()
            along(g, origin, me, y_send, y_recv, y_dev).wait_send()
            part(g, origin, x_slot, 0, a_send, a_recv, y_dev).wait_send()
            part(g, origin, y_slot, half, b_send, b_recv, x_dev).wait_send()
        return carry

    lax.fori_loop(0, n_tensor, finish, 0)
    for g in range(3):
        if g:
            own[g].wait()
        for k in range(1, n_tensor):
            to_z(g, k).wait_send()


def forward_attention(n_tensor, heads, x, triple, merge, w1, shrink, small, spread, owned, seg_row, seg_col):
    rows, cols = w1.shape
    n_small = 8 * n_tensor
    blocks = 2 * n_tensor
    span = x.shape[0] // 2
    length = blocks * span
    part = heads * HEAD_DIM
    dma = pltpu.SemaphoreType.DMA
    shape = jax.ShapeDtypeStruct
    full = shape((n_tensor, 8, rows, cols), BF16)
    pair = [dma((3, n_tensor)), dma((3, n_tensor))]
    vmem = pl.BlockSpec(memory_space=pltpu.VMEM)
    hbm = pl.BlockSpec(memory_space=pl.ANY)
    return pl.pallas_call(
        functools.partial(forward_kernel, n_tensor, heads),
        out_shape=(
            full, full, full, shape((n_small,) + small.shape, F32), shape((blocks, span, 3 * part), BF16),
            shape((length, part), F32), shape((heads, length, length), BF16), shape((blocks, span, part), BF16),
        ),
        in_specs=[vmem] * 10,
        out_specs=(vmem, hbm, hbm, vmem, vmem, vmem, hbm, vmem),
        scratch_shapes=[
            pltpu.VMEM((rows, cols), BF16),
            pltpu.VMEM((rows, cols), BF16),
            pltpu.VMEM((n_tensor, 2, span, 3 * part), BF16),
            pltpu.VMEM((blocks, span, part), BF16),
            pltpu.VMEM((heads, length, length), BF16),
            dma((5,)),
        ] + pair * 5 + [
            dma((3, 4, n_tensor)), dma((3, 4, n_tensor)), dma((n_small,)), dma((n_small,)),
            dma((n_tensor, 2)), dma((blocks,)), dma((blocks,)), dma((blocks,)), dma((blocks // 2,)),
        ],
        compiler_params=pltpu.CompilerParams(collective_id=0, has_side_effects=True, vmem_limit_bytes=56 << 20),
        cost_estimate=pl.CostEstimate(flops=0, bytes_accessed=w1.size * 400, transcendentals=0),
        name="forward_attention",
    )(x, triple, merge, w1, shrink, small, spread, owned, seg_row, seg_col)


def sum_steps(n_tensor, grads, acc, core_in, y1_in, x1_in, x2_in, y2_in, z_in, load_sem, c_send, c_recv,
              y1_send, y1_recv, x1_send, x1_recv, x2_send, x2_recv, y2_send, y2_recv, z_send, z_recv):
    dp, ctx, z = (lax.axis_index(a) for a in ALL)
    rows = acc.shape[-2]
    half = rows // 2
    core = lax.rem(dp, 2)
    x = lax.div(dp, 2)
    xp, yp = 1 - x, 1 - ctx
    x_dev, y_dev, c_dev = at(xp * 2 + core, ctx, z), at(dp, yp, z), at(x * 2 + 1 - core, ctx, z)
    low, high = pl.ds(0, half), pl.ds(half, half)
    count = range(len(grads))

    def load(g, t):
        return pltpu.make_async_copy(grads[g].at[t, :, core], acc.at[g, t], load_sem.at[g, t])

    def to_core(g, t):
        return remote(grads[g].at[t, :, 1 - core], core_in.at[g, t], c_send.at[g, t], c_recv.at[g, t], c_dev)

    def y1(g, t):
        return remote(acc.at[g, t, :, yp, low], y1_in.at[g, t], y1_send.at[g, t], y1_recv.at[g, t], y_dev)

    def x1(g, t):
        return remote(acc.at[g, t, xp, :, high], x1_in.at[g, t], x1_send.at[g, t], x1_recv.at[g, t], x_dev)

    def x2(g, t):
        return remote(acc.at[g, t, xp, ctx, low], x2_in.at[g, t], x2_send.at[g, t], x2_recv.at[g, t], x_dev)

    def y2(g, t):
        return remote(acc.at[g, t, x, yp, high], y2_in.at[g, t], y2_send.at[g, t], y2_recv.at[g, t], y_dev)

    def to_z(g, t):
        return remote(acc.at[g, t, x, ctx], z_in.at[g, z], z_send.at[g, t], z_recv.at[g, z], at(dp, ctx, t))

    def add(a, b):
        return (a.astype(F32) + b.astype(F32)).astype(BF16)

    def target(j):
        return lax.rem(z + 1 + j, n_tensor)

    def begin(j):
        t = target(j)
        for g in count:
            to_core(g, t).start()
            load(g, t).start()

    def core_step(j):
        t = target(j)
        for g in count:
            load(g, t).wait()
            to_core(g, t).wait_recv()
            acc[g, t] = add(acc[g, t], core_in[g, t])
            y1(g, t).start()
            x1(g, t).start()

    def first_step(j):
        t = target(j)
        for g in count:
            y1(g, t).wait_recv()
            for i in range(2):
                acc[g, t, i, ctx, low] = add(acc[g, t, i, ctx, low], y1_in[g, t, i])
            x2(g, t).start()
            x1(g, t).wait_recv()
            for i in range(2):
                acc[g, t, x, i, high] = add(acc[g, t, x, i, high], x1_in[g, t, i])
            y2(g, t).start()

    def second_step(j):
        t = target(j)
        for g in count:
            x2(g, t).wait_recv()
            acc[g, t, x, ctx, low] = add(acc[g, t, x, ctx, low], x2_in[g, t])
            y2(g, t).wait_recv()
            acc[g, t, x, ctx, high] = add(acc[g, t, x, ctx, high], y2_in[g, t])

            @pl.when(j < n_tensor - 1)
            def _():
                to_z(g, t).start()

    def step(j):
        @pl.when(j < n_tensor)
        def _():
            core_step(j)

        @pl.when((j >= 1) & (j < n_tensor + 1))
        def _():
            first_step(j - 1)

        @pl.when(j >= 2)
        def _():
            second_step(j - 2)

    def end(outs):
        for g in count:
            outs[g][...] = acc[g, z, x, ctx].astype(F32)
            for k in range(1, n_tensor):
                origin = lax.rem(z + n_tensor - k, n_tensor)
                block = z_in.at[g, origin]
                remote(block, block, z_send.at[g, origin], z_recv.at[g, origin], x_dev).wait_recv()
                outs[g][...] += z_in[g, origin].astype(F32)

        def finish(t, carry):
            for g in count:
                for copy in (to_core, y1, x1, x2, y2):
                    copy(g, t).wait_send()
            return carry

        lax.fori_loop(0, n_tensor, finish, 0)
        for g in count:
            for k in range(1, n_tensor):
                to_z(g, lax.rem(z + k, n_tensor)).wait_send()

    return begin, step, end


def sum_scratch(n_grads, n_tensor, rows, cols):
    dma = pltpu.SemaphoreType.DMA
    grid = (n_grads, n_tensor)
    half = rows // 2
    return [
        pltpu.VMEM(grid + (2, 2, rows, cols), BF16),
        pltpu.VMEM(grid + (2, 2, rows, cols), BF16),
        pltpu.VMEM(grid + (2, half, cols), BF16),
        pltpu.VMEM(grid + (2, half, cols), BF16),
        pltpu.VMEM(grid + (half, cols), BF16),
        pltpu.VMEM(grid + (half, cols), BF16),
        pltpu.VMEM(grid + (rows, cols), BF16),
    ] + [dma(grid)] * 13


def backward_kernel(n_tensor, heads, first_low, first_grad, x, f0, mixed, small, spread, owned, rows, mixed_float,
                    probs_in, g1, g2, input_grad, o0, o1, o2, small_out,
                    turned, g0, mixed_grad, grad, probs, send_rows, qkv_grad, key_sum, value_sum, small_send, small_in,
                    own_sem, g_send, g_recv, q_send, q_recv, p_sem, s_send, s_recv, *scratch):
    dp, ctx, z = (lax.axis_index(a) for a in ALL)
    n_ctx = 2
    n_blocks = n_ctx * n_tensor
    n_units = n_blocks // 2
    span = grad.shape[1]
    part = grad.shape[2]
    wide = 3 * part
    n_rows, width = f0.shape[-2:]
    total_rows = n_blocks * span
    own_block = ctx * n_tensor + z
    own_slot = z * n_ctx + ctx
    mine = z * 8 + dp * 2 + ctx
    peers = everyone(4, 2, n_tensor)
    greet([at(*p) for p in peers])
    others = [(lax.rem(ctx + j, n_ctx), lax.rem(z + k, n_tensor))
              for k in (2, 3, 1, 0) for j in range(n_ctx) if (j or k) and k < n_tensor]
    half = len(scratch) // 2
    begin, step, end = sum_steps(n_tensor, (g1, g2), *scratch[:half])
    begin_last, step_last, end_last = sum_steps(n_tensor, (g0,), *scratch[half:])

    def to_heads(c, t):
        return remote(mixed_grad.at[t * n_ctx + c], grad.at[own_block], g_send.at[t * n_ctx + c],
                      g_recv.at[own_block], at(dp, c, t))

    def load(i):
        lines = pl.ds(i * 2 * span, 2 * span)
        return pltpu.make_async_copy(probs_in.at[:, lines], probs.at[:, lines], p_sem.at[i])

    here = pltpu.make_async_copy(mixed_grad.at[own_slot], grad.at[own_block], own_sem.at[0])

    def begin_all(j, carry):
        begin(j)
        return carry

    lax.fori_loop(0, n_tensor, begin_all, 0)

    def spread_grad(j, carry):
        t = lax.rem(z + 1 + j, n_tensor)
        weight = f0[t].reshape(8 * n_rows, width)[:, wide:]
        value = jnp.dot(first_low[...], weight, preferred_element_type=F32).astype(BF16)
        mixed_grad[pl.ds(t * n_ctx, n_ctx)] = value.reshape(n_ctx, span, part)
        to_heads(1 - ctx, t).start()

        @pl.when(t != z)
        def _():
            to_heads(ctx, t).start()

        @pl.when(t == z)
        def _():
            here.start()

        return carry

    lax.fori_loop(0, n_tensor, spread_grad, 0)
    for i in range(n_units):
        load(i).start()
    turned[0] = first_low[...].T
    turned[1] = x[...].T
    small_send[...] = small[...]

    def merge_grad(t, carry):
        value = jnp.dot(turned[0], mixed[pl.ds(t * n_ctx, n_ctx)].reshape(n_ctx * span, part),
                        preferred_element_type=F32)
        g0[t, :, :, :, :, pl.ds(wide, part)] = value.astype(BF16).reshape(2, 2, 2, n_rows, part)
        return carry

    lax.fori_loop(0, n_tensor, merge_grad, 0)
    step(0)
    here.wait()
    for c, t in others:
        block = c * n_tensor + t
        remote(grad.at[block], grad.at[block], g_send.at[0], g_recv.at[block], at(dp, c, t)).wait_recv()
    for i in range(n_units):
        load(i).wait()

    def one_head(h):
        lanes = pl.ds(HEAD_DIM * h, HEAD_DIM)
        k_lanes = pl.ds(HEAD_DIM * (heads + h), HEAD_DIM)
        v_lanes = pl.ds(HEAD_DIM * (2 * heads + h), HEAD_DIM)
        key_sum[...] = jnp.zeros_like(key_sum)
        value_sum[...] = jnp.zeros_like(value_sum)

        def unit(i, carry):
            blocks = pl.ds(2 * i, 2)
            lines = pl.ds(pl.multiple_of(i * 2 * span, 2 * span), 2 * span)
            q = rows[blocks, :, lanes].reshape(2 * span, HEAD_DIM)
            k = rows[:, :, k_lanes].reshape(total_rows, HEAD_DIM)
            v = rows[:, :, v_lanes].reshape(total_rows, HEAD_DIM)
            up = grad[blocks, :, lanes].reshape(2 * span, HEAD_DIM)
            low = probs[h, lines, :]
            delta = jnp.sum(up.astype(F32) * mixed_float[lines, lanes], axis=-1, keepdims=True)
            pull = lax.dot_general(up, v, (((1,), (1,)), ((), ())), preferred_element_type=F32)
            score = (low.astype(F32) * (pull - delta)).astype(BF16)
            query = SCALE * jnp.dot(score, k, preferred_element_type=F32)
            send_rows[blocks, :, lanes] = query.astype(BF16).reshape(2, span, HEAD_DIM)
            key_sum[...] += lax.dot_general(q, score, (((0,), (0,)), ((), ())), preferred_element_type=F32)
            value_sum[...] += lax.dot_general(up, low, (((0,), (0,)), ((), ())), preferred_element_type=F32)
            return carry

        lax.fori_loop(0, n_units, unit, 0)
        key = (SCALE * key_sum[...]).T.astype(BF16)
        value = value_sum[...].T.astype(BF16)
        send_rows[:, :, k_lanes] = key.reshape(n_blocks, span, HEAD_DIM)
        send_rows[:, :, v_lanes] = value.reshape(n_blocks, span, HEAD_DIM)

    for h in range(heads):
        one_head(h)
        if h == 0:
            step(1)
        elif h == 1:
            step(2)

    def to_tokens(c, t):
        return remote(send_rows.at[c * n_tensor + t], qkv_grad.at[own_slot], q_send.at[c * n_tensor + t],
                      q_recv.at[own_slot], at(dp, c, t))

    there = pltpu.make_async_copy(send_rows.at[own_block], qkv_grad.at[own_slot], own_sem.at[1])
    for c, t in others:
        to_tokens(c, t).start()
    there.start()

    def one(j, carry):
        step(j)
        return carry

    lax.fori_loop(min(heads, 3), n_tensor + 2, one, 0)

    def arrived(t, c):
        slot = t * n_ctx + c
        remote(qkv_grad.at[slot], qkv_grad.at[slot], q_send.at[0], q_recv.at[slot], at(dp, c, t)).wait_recv()

    def weight_grad(j, carry):
        t = lax.rem(z + 1 + j, n_tensor)
        arrived(t, 1 - ctx)

        @pl.when(t != z)
        def _():
            arrived(t, ctx)

        @pl.when(t == z)
        def _():
            there.wait()

        pull = qkv_grad[pl.ds(t * n_ctx, n_ctx)].reshape(n_ctx * span, wide)
        value = jnp.dot(turned[1], pull, preferred_element_type=F32)
        g0[t, :, :, :, :, pl.ds(0, wide)] = value.astype(BF16).reshape(2, 2, 2, n_rows, wide)
        begin_last(j)
        total = jnp.sum(pull.astype(F32), axis=0, keepdims=True) * owned[...]
        upper = total.astype(BF16)
        lower = (total - upper.astype(F32)).astype(BF16)
        flip = (((1,), (1,)), ((), ()))
        pieces = lax.dot_general(upper, spread[...], flip, preferred_element_type=F32)
        pieces += lax.dot_general(lower, spread[...], flip, preferred_element_type=F32)
        targets = pl.ds(t * 8, 8)
        small_send[targets, 0, :] = small_send[targets, 0, :] + pieces
        return carry

    lax.fori_loop(0, n_tensor, weight_grad, 0)
    small_copies = [
        remote(small_send.at[pt * 8 + pd * 2 + pc], small_in.at[n], s_send.at[n], s_recv.at[n], at(pd, pc, pt))
        for n, (pd, pc, pt) in enumerate(peers)
    ]
    for copy in small_copies:
        copy.start()
    input_grad[...] = first_grad[...]

    def last(j, carry):
        step_last(j)

        @pl.when(j < n_tensor)
        def _():
            pull = qkv_grad[pl.ds(j * n_ctx, n_ctx)].reshape(n_ctx * span, wide)
            weight = f0[j].reshape(8 * n_rows, width)[:, :wide]
            input_grad[...] += lax.dot_general(pull, weight, (((1,), (1,)), ((), ())), preferred_element_type=F32)

        return carry

    lax.fori_loop(0, n_tensor + 2, last, 0)
    end((o1, o2))
    end_last((o0,))
    total = small_send[mine]
    for n in range(len(peers)):
        small_copies[n].wait()
        total = total + small_in[n]
    small_out[...] = total
    for c, t in others:
        to_tokens(c, t).wait_send()
        to_heads(c, t).wait_send()


def backward_attention(n_tensor, heads, first_low, first_grad, x, f0, mixed, small, spread, owned, rows, mixed_float,
                       probs, g1, g2):
    blocks, span, wide = rows.shape
    part = heads * HEAD_DIM
    length = blocks * span
    n_rows, cols = g1.shape[-2:]
    n_small = 8 * n_tensor
    dma = pltpu.SemaphoreType.DMA
    vmem = pl.BlockSpec(memory_space=pltpu.VMEM)
    hbm = pl.BlockSpec(memory_space=pl.ANY)
    shape = jax.ShapeDtypeStruct
    out = shape((n_rows, cols), F32)
    return pl.pallas_call(
        functools.partial(backward_kernel, n_tensor, heads),
        out_shape=(shape(first_grad.shape, F32), out, out, out, shape(small.shape[1:], F32)),
        in_specs=[vmem] * 10 + [hbm] * 3,
        out_specs=(vmem,) * 5,
        scratch_shapes=[
            pltpu.VMEM((2,) + x.shape[::-1], BF16),
            pltpu.VMEM(g1.shape, BF16),
            pltpu.VMEM((blocks, span, part), BF16),
            pltpu.VMEM((blocks, span, part), BF16),
            pltpu.VMEM((heads, length, length), BF16),
            pltpu.VMEM((blocks, span, wide), BF16),
            pltpu.VMEM((blocks, span, wide), BF16),
            pltpu.VMEM((HEAD_DIM, length), F32),
            pltpu.VMEM((HEAD_DIM, length), F32),
            pltpu.VMEM(small.shape, F32),
            pltpu.VMEM((n_small - 1,) + small.shape[1:], F32),
            dma((2,)), dma((blocks,)), dma((blocks,)), dma((blocks,)), dma((blocks,)), dma((blocks // 2,)),
            dma((n_small - 1,)), dma((n_small - 1,)),
        ] + sum_scratch(2, n_tensor, n_rows, cols) + sum_scratch(1, n_tensor, n_rows, cols),
        compiler_params=pltpu.CompilerParams(collective_id=2, has_side_effects=True, vmem_limit_bytes=58 << 20),
        cost_estimate=pl.CostEstimate(flops=0, bytes_accessed=g1.size * 24, transcendentals=0),
        name="backward_attention",
    )(first_low, first_grad, x, f0, mixed, small, spread, owned, rows, mixed_float, probs, g1, g2)


def norm_rows(total, gain, shift):
    center = total - jnp.mean(total, axis=-1, keepdims=True)
    spread = jnp.mean(center * center, axis=-1, keepdims=True)
    return center * lax.rsqrt(spread + EPS) * gain + shift


def gelu_exact(before):
    share = 0.5 + 0.5 * lax.erf(before * 0.5**0.5)
    dense = (0.5 / np.pi) ** 0.5 * jnp.exp(-0.5 * before * before)
    return before * share, share + before * dense


def dot(spec, a, b):
    return jnp.einsum(spec, a, b, preferred_element_type=F32)


def add_up(spec, a, b):
    return sum(dot(spec, a[t], b[t]) for t in range(a.shape[0]))


def local(
    inputs,
    cotangent,
    segments,
    triple_weight,
    attend_bias,
    merge_weight,
    merge_bias,
    first_gain,
    first_shift,
    expand_weight,
    expand_bias,
    shrink_weight,
    shrink_bias,
    second_gain,
    second_shift,
):
    n_dp, n_ctx, n_tensor = (lax.axis_size(a) for a in ALL)
    span, batch, width = inputs.shape
    rows = triple_weight.shape[1]
    part = triple_weight.shape[2]
    units = expand_weight.shape[1]
    owners = n_dp * n_ctx
    heads = part // HEAD_DIM
    count = batch * span
    small_part = part // owners
    unit_part = units // owners
    own_kernels = n_dp == 4 and n_ctx == 2 and batch == 2 and n_tensor == 4 and rows % 32 == 0

    vectors = (merge_bias, first_gain, first_shift, shrink_bias, second_gain, second_shift)
    pieces = [attend_bias[0, 0], attend_bias[1, 0]] + [v[0] for v in vectors] + [expand_bias[0]]
    n_values = sum(v.shape[0] for v in pieces)
    pad = -n_values % 1024
    x_low = jnp.transpose(inputs, (1, 0, 2)).reshape(count, width)
    here = lax.axis_index("ctx")
    if own_kernels:
        block = ((n_values + pad) // 128, 128)
        labels = lax.dynamic_slice_in_dim(segments, here, 1, 0)
        small, start = jnp.zeros((n_values + pad,), F32), 0
        for v in pieces:
            small += jnp.pad(v.astype(F32), (start, n_values + pad - start - v.shape[0]))
            start += v.shape[0]
        small = small.reshape(block)
        spread, owned = place({"part": part, "owners": owners}, ((0, 0), (small_part, 2 * part)))
        f0, f1, f2, small_all, rows_all, mixed_float, probs, mixed = forward_attention(
            n_tensor, heads, x_low, triple_weight, merge_weight, expand_weight, shrink_weight, small,
            spread, owned, labels, labels.reshape(-1, 1)
        )
        mixed_blocks = mixed
        mixed = mixed.reshape(n_tensor, count, part)
        small_all = small_all.reshape(n_tensor, owners, -1)[:, :, :n_values]
    else:
        w0 = jnp.concatenate(
            [jnp.transpose(triple_weight, (1, 0, 2)).reshape(rows, 3 * part), merge_weight.T], axis=1
        )
        w2 = shrink_weight.T
        small = jnp.concatenate(pieces).astype(F32)
        f0, f1, f2 = (
            lax.all_gather(lax.all_gather(w, ("dp", "ctx"), axis=0, tiled=True), "tensor", axis=0, tiled=False)
            for w in (w0, expand_weight, w2)
        )
        small_all = lax.all_gather(lax.all_gather(small, ("dp", "ctx")), "tensor")
    f0_blocks = f0
    f0, f1, f2 = (w.reshape(n_tensor, width, -1) for w in (f0, f1, f2))
    w_qkv, w_merge, w_expand, w_shrink = f0[:, :, : 3 * part], f0[:, :, 3 * part :], f1, f2
    narrow = small_all[:, :, : 8 * small_part].reshape(n_tensor, owners, 8, small_part)
    narrow = jnp.transpose(narrow, (2, 0, 1, 3)).reshape(8, n_tensor, part)
    merge_vec, gain_one, shift_one, shrink_vec, gain_two, shift_two = narrow[2:].reshape(6, width)
    expand_vec = small_all[:, :, 8 * small_part :].reshape(n_tensor, 1, units)
    qkv_vec = jnp.concatenate([narrow[0], jnp.zeros_like(narrow[0]), narrow[1]], axis=-1)[:, None]

    x = x_low.astype(F32)
    upstream = jnp.transpose(cotangent, (1, 0, 2)).reshape(count, width).astype(F32)

    def to_tokens(value):
        value = value.reshape(batch, n_tensor, span, -1)
        out = lax.all_to_all(jnp.transpose(value, (1, 0, 2, 3)), "tensor", split_axis=0, concat_axis=0)
        return out.reshape(n_tensor, count, -1)

    if not own_kernels:
        qkv = (dot("rd,tde->tre", x_low, w_qkv) + qkv_vec).astype(BF16)
        mine = lax.all_to_all(
            qkv.reshape(n_tensor, batch, span, 3 * part), "tensor", split_axis=0, concat_axis=0
        )
        mine = jnp.transpose(mine, (1, 0, 2, 3)).reshape(batch, n_tensor * span, 3 * part)
        n_query = n_tensor * span
        own_labels = lax.dynamic_slice_in_dim(segments, here * n_query, n_query, 1)
        kv_rows = lax.all_gather(mine[..., part:], "ctx", axis=1, tiled=True)
        n_key = kv_rows.shape[1]
        q_four = mine[..., :part].reshape(batch, n_query, heads, HEAD_DIM)
        k_four = kv_rows[..., :part].reshape(batch, n_key, heads, HEAD_DIM)
        v_four = kv_rows[..., part:].reshape(batch, n_key, heads, HEAD_DIM)
        allowed = own_labels[:, None, :, None] == segments[:, None, None, :]
        scores = jnp.where(allowed, SCALE * dot("sqhd,skhd->shqk", q_four, k_four), NEG)
        top = jnp.max(scores, axis=-1)
        weights = jnp.where(allowed, jnp.exp(scores - top[..., None]), 0.0)
        total = jnp.sum(weights, axis=-1)
        mixed_float = dot("shqk,skhd->shqd", weights.astype(BF16), v_four) / total[..., None]
        logsum = top + jnp.log(total)
        mixed = to_tokens(jnp.transpose(mixed_float, (0, 2, 1, 3)).reshape(batch, n_query, part).astype(BF16))

    first_sum = x + add_up("re,de->rd", mixed, w_merge) + merge_vec
    first_norm = norm_rows(first_sum, gain_one, shift_one)
    first_low = first_norm.astype(BF16)
    before = dot("rd,tdf->trf", first_low, w_expand) + expand_vec
    active, slope = gelu_exact(before)
    active = active.astype(BF16)
    second_sum = first_norm + add_up("rf,df->rd", active, w_shrink) + shrink_vec
    outputs_rows = norm_rows(second_sum, gain_two, shift_two)

    second_grad, gain_two_grad, shift_two_grad = jax.vjp(norm_rows, second_sum, gain_two, shift_two)[1](upstream)
    shrink_vec_grad = jnp.sum(second_grad, axis=0)
    second_low = second_grad.astype(BF16)
    shrink_grad = dot("rd,trf->tdf", second_low, active).astype(BF16)
    active_grad = dot("rd,tdf->trf", second_low, w_shrink)
    before_low = (active_grad * slope).astype(BF16)
    expand_vec_grad = jnp.sum(before_low.astype(F32), axis=1)
    expand_grad = dot("rd,trf->tdf", first_low, before_low).astype(BF16)
    norm_back = add_up("rf,df->rd", before_low, w_expand)
    first_grad, gain_one_grad, shift_one_grad = jax.vjp(norm_rows, first_sum, gain_one, shift_one)[1](
        second_grad + norm_back
    )
    merge_vec_grad = jnp.sum(first_grad, axis=0)
    first_low_grad = first_grad.astype(BF16)
    vec_grads = jnp.stack(
        [merge_vec_grad, gain_one_grad, shift_one_grad, shrink_vec_grad, gain_two_grad, shift_two_grad]
    ).reshape(6, n_tensor, owners, small_part)
    vec_grads = jnp.transpose(vec_grads, (1, 2, 0, 3)).reshape(n_tensor, owners, 6 * small_part)
    small_grads = jnp.concatenate([vec_grads, expand_vec_grad.reshape(n_tensor, owners, unit_part)], axis=-1)
    if own_kernels:
        sent = jnp.pad(small_grads.reshape(n_tensor * owners, -1), ((0, 0), (2 * small_part, pad)))
        inputs_gradient, r0, r1, r2, small_sum = backward_attention(
            n_tensor, heads, first_low_grad, first_grad, x_low, f0_blocks, mixed_blocks,
            sent.reshape((n_tensor * owners,) + block), spread, owned, rows_all, mixed_float, probs,
            *(g.reshape(n_tensor, 2, 2, 2, rows, width) for g in (expand_grad, shrink_grad))
        )
        small_sum = small_sum.reshape(-1)[:n_values]
    else:
        merge_grad = dot("rd,tre->tde", first_low_grad, mixed).astype(BF16)
        mixed_grad = dot("rd,tde->tre", first_low_grad, w_merge).astype(BF16)
        grad_rows = lax.all_to_all(
            mixed_grad.reshape(n_tensor, batch, span, part), "tensor", split_axis=0, concat_axis=0
        )
        grad_four = jnp.transpose(grad_rows, (1, 0, 2, 3)).reshape(batch, n_query, heads, HEAD_DIM)
        delta = jnp.sum(jnp.transpose(grad_four.astype(F32), (0, 2, 1, 3)) * mixed_float, axis=-1)
        back_scores = SCALE * dot("sqhd,skhd->shqk", q_four, k_four)
        probs = jnp.where(allowed, jnp.exp(back_scores - logsum[..., None]), 0.0)
        prob_grad = dot("sqhd,skhd->shqk", grad_four, v_four)
        score_low = (probs * (prob_grad - delta[..., None])).astype(BF16)
        value_part = dot("shqk,sqhd->skhd", probs.astype(BF16), grad_four)
        query_part = SCALE * dot("shqk,skhd->sqhd", score_low, k_four)
        key_part = SCALE * dot("shqk,sqhd->skhd", score_low, q_four)
        query_part, key_part, value_part = (
            v.reshape(batch, -1, part).astype(BF16) for v in (query_part, key_part, value_part)
        )
        key_part, value_part = (
            lax.psum_scatter(v, "ctx", scatter_dimension=1, tiled=True) for v in (key_part, value_part)
        )
        qkv_grad = to_tokens(jnp.concatenate([query_part, key_part, value_part], axis=-1))
        triple_grad = dot("rd,tre->tde", x_low, qkv_grad).astype(BF16)
        attend_grad = jnp.sum(qkv_grad.astype(F32), axis=1).reshape(n_tensor, 3, owners, small_part)
        inputs_gradient = first_grad + add_up("re,de->rd", qkv_grad, w_qkv)
        small_grads = jnp.concatenate([attend_grad[:, 0], attend_grad[:, 2], small_grads], axis=-1)
        grads = (jnp.concatenate([triple_grad, merge_grad], axis=-1), expand_grad, shrink_grad)
        r0, r1, r2 = (
            lax.psum_scatter(
                lax.psum_scatter(g, "tensor", scatter_dimension=0), ("dp", "ctx"), scatter_dimension=0, tiled=True
            ).astype(F32)
            for g in grads
        )
        small_sum = lax.psum_scatter(
            lax.psum_scatter(small_grads, "tensor", scatter_dimension=0), ("dp", "ctx"), scatter_dimension=0
        )
    triple_out = jnp.transpose(r0[:, : 3 * part].reshape(rows, 3, part), (1, 0, 2))
    narrow_out = small_sum[: 8 * small_part].reshape(8, 1, small_part)
    outputs_rows, inputs_gradient = (
        jnp.transpose(v.reshape(batch, span, width), (1, 0, 2)) for v in (outputs_rows, inputs_gradient)
    )
    return (
        outputs_rows,
        inputs_gradient,
        triple_out,
        narrow_out[:2],
        r0[:, 3 * part :].T,
        narrow_out[2],
        narrow_out[3],
        narrow_out[4],
        r1,
        small_sum[8 * small_part :].reshape(1, unit_part),
        r2.T,
        narrow_out[5],
        narrow_out[6],
        narrow_out[7],
    )


def solution(mesh):
    in_specs = (
        P(("ctx", "tensor"), "dp", None),
        P(("ctx", "tensor"), "dp", None),
        P("dp", None),
        P(None, ("dp", "ctx"), "tensor"),
        P(None, "tensor", ("dp", "ctx")),
        P("tensor", ("dp", "ctx")),
        P("tensor", ("dp", "ctx")),
        P("tensor", ("dp", "ctx")),
        P("tensor", ("dp", "ctx")),
        P(("dp", "ctx"), "tensor"),
        P("tensor", ("dp", "ctx")),
        P("tensor", ("dp", "ctx")),
        P("tensor", ("dp", "ctx")),
        P("tensor", ("dp", "ctx")),
        P("tensor", ("dp", "ctx")),
    )
    out_specs = (
        P(("ctx", "tensor"), "dp", None),
        P(("ctx", "tensor"), "dp", None),
        P(None, ("dp", "ctx"), "tensor"),
        P(None, "tensor", ("dp", "ctx")),
        P("tensor", ("dp", "ctx")),
        P("tensor", ("dp", "ctx")),
        P("tensor", ("dp", "ctx")),
        P("tensor", ("dp", "ctx")),
        P(("dp", "ctx"), "tensor"),
        P("tensor", ("dp", "ctx")),
        P("tensor", ("dp", "ctx")),
        P("tensor", ("dp", "ctx")),
        P("tensor", ("dp", "ctx")),
        P("tensor", ("dp", "ctx")),
    )
    return jax.shard_map(local, mesh=mesh, in_specs=in_specs, out_specs=out_specs, check_vma=False)
```

```python
import functools

import jax
import jax.numpy as jnp
import numpy as np
from jax import lax
from jax.experimental import pallas as pl
from jax.experimental.pallas import tpu as pltpu
from jax.sharding import PartitionSpec as P

HEAD_DIM = 64

EPS = 1e-12
NEG = -1e30
SCALE = 0.125
MESH = pl.DeviceIdType.MESH
BF16 = jnp.bfloat16
F32 = jnp.float32
ALL = ("dp", "ctx", "tensor")
TOKENS = ("ctx", "tensor")


def at(dp, ctx, tensor):
    return {"dp": dp, "ctx": ctx, "tensor": tensor}


def remote(src, dst, send, recv, where):
    return pltpu.make_async_remote_copy(
        src_ref=src, dst_ref=dst, send_sem=send, recv_sem=recv, device_id=where, device_id_type=MESH
    )


def greet(peers):
    barrier = pltpu.get_barrier_semaphore()
    for peer in peers:
        pl.semaphore_signal(barrier, inc=1, device_id=peer, device_id_type=MESH)
    pl.semaphore_wait(barrier, len(peers))


def everyone(n_dp, n_ctx, n_tensor):
    dp, ctx, tensor = (lax.axis_index(a) for a in ALL)
    peers = []
    for i in range(n_dp):
        for j in range(n_ctx):
            for k in range(n_tensor):
                if i or j or k:
                    peers.append(
                        (lax.rem(dp + i, n_dp), lax.rem(ctx + j, n_ctx), lax.rem(tensor + k, n_tensor))
                    )
    return peers


def one_hot(n_lanes, owners, picks, width):
    spread = np.zeros((n_lanes, width), np.float32)
    owned = np.zeros((owners, width), np.float32)
    for feature, (lane, owner) in picks.items():
        spread[lane, feature] = 1.0
        owned[owner, feature] = 1.0
    return jnp.asarray(spread, BF16), jnp.asarray(owned)


def tables(n_tensor, owners, part, units):
    piece, unit = part // owners, units // owners
    attend = {n: (n % piece, n // piece) for n in range(part)}
    attend.update({2 * part + n: (piece + n % piece, n // piece) for n in range(part)})
    whole = {t * part + n: (n % piece, t * owners + n // piece) for t in range(n_tensor) for n in range(part)}
    expand = {n: (n % unit, n // unit) for n in range(units)}
    return (
        one_hot(128, owners, attend, 3 * part)
        + one_hot(128, n_tensor * owners, whole, n_tensor * part)
        + one_hot(128, owners, expand, units)
    )


def gathered(pieces, spread, owned):
    value = jnp.dot(pieces.astype(BF16), spread[...], preferred_element_type=F32)
    return jnp.sum(value * owned[...], axis=0, keepdims=True)


def scattered(vector, spread, owned):
    total = vector * owned[...]
    upper = total.astype(BF16)
    lower = (total - upper.astype(F32)).astype(BF16)
    flip = (((1,), (1,)), ((), ()))
    return lax.dot_general(upper, spread[...], flip, preferred_element_type=F32) + lax.dot_general(
        lower, spread[...], flip, preferred_element_type=F32
    )


def normalize(total):
    center = total - jnp.mean(total, axis=-1, keepdims=True)
    spread = jnp.mean(center * center, axis=-1, keepdims=True)
    scale = lax.rsqrt(spread + EPS)
    return center * scale, scale


def normalize_back(up, normal, scale, gain):
    pull = up * gain
    return scale * (
        pull - jnp.mean(pull, axis=-1, keepdims=True) - normal * jnp.mean(pull * normal, axis=-1, keepdims=True)
    )


def total_rows_of(value):
    return jnp.sum(value, axis=0, keepdims=True)


def forward_kernel(n_tensor, heads, x, cotangent, triple, merge, w1, shrink, small, a_spread, a_owned, v_spread,
                   v_owned, e_spread, e_owned, seg_row, seg_col,
                   f0, rows, mixed_float, probs_out, mixed, outputs, first_low, first_low_grad, first_grad,
                   small_grads, g1_out, g2_out,
                   w0, w2, f1, f2, small_all, send_rows, send_mixed, probs, vectors, normal, scale, active, slope,
                   total, second_low, turned, g1, g2,
                   own_sem, z_up, z_down, z_recv, x_send, x_recv, y_send, y_recv, a_send, a_recv, b_send, b_recv,
                   c_send, c_recv, s_send, s_recv, q_send, q_recv, m_send, m_recv, p_sem, g_sem):
    shards, outs = (w0, w1, w2), (f0, f1, f2)
    dp, ctx, z = (lax.axis_index(a) for a in ALL)
    n_ctx = 2
    n_rows = w0.shape[0]
    half = n_rows // 2
    xp = lax.rem(dp + 2, 4)
    cp = dp + 1 - 2 * lax.rem(dp, 2)
    yp = 1 - ctx
    xcp = lax.rem(cp + 2, 4)
    me = dp * 2 + ctx
    mine = z * 8 + me
    peers = everyone(4, 2, n_tensor)
    wide = a_spread.shape[1]
    part_width = wide // 3
    for i in range(3):
        w0[:, pl.ds(i * part_width, part_width)] = triple[i]
    w0[:, pl.ds(wide, merge.shape[0])] = merge[...].T
    w2[...] = shrink[...].T
    greet([at(*p) for p in peers])
    x_dev, y_dev, c_dev = at(xp, ctx, z), at(dp, yp, z), at(cp, ctx, z)
    x_slot, y_slot, d_slot = xp * 2 + ctx, dp * 2 + yp, xp * 2 + yp
    slots = (cp * 2 + ctx, xcp * 2 + ctx, cp * 2 + yp, xcp * 2 + yp)
    up_ok, down_ok = z < n_tensor - 1, z > 0

    def near(j):
        found = 0
        for there in range(n_tensor):
            order = sorted(range(n_tensor), key=lambda t: (abs(t - there), t))
            for n, t in enumerate(order):
                found = found + jnp.where((z == there) & (j == n), t, 0)
        return found

    def up(g, origin, src=None):
        block = outs[g].at[origin, me]
        return remote(block if src is None else src, block, z_up.at[g, origin], z_recv.at[g, origin],
                      at(dp, ctx, jnp.minimum(z + 1, n_tensor - 1)))

    def down(g, origin, src=None):
        block = outs[g].at[origin, me]
        return remote(block if src is None else src, block, z_down.at[g, origin], z_recv.at[g, origin],
                      at(dp, ctx, jnp.maximum(z - 1, 0)))

    def from_z(g, origin):
        block = outs[g].at[origin, me]
        return remote(block, block, z_up.at[g, origin], z_recv.at[g, origin], x_dev)

    def along(g, origin, slot, send, recv, dev, src=None):
        block = outs[g].at[origin, slot]
        return remote(block if src is None else src, block, send.at[g, origin], recv.at[g, origin], dev)

    def part(g, origin, slot, lo, send, recv, dev):
        block = outs[g].at[origin, slot, pl.ds(lo, half)]
        return remote(block, block, send.at[g, origin], recv.at[g, origin], dev)

    def core(g, origin, kind, slot, src=None):
        block = outs[g].at[origin, slot]
        return remote(
            block if src is None else src, block, c_send.at[g, kind, origin], c_recv.at[g, kind, origin], c_dev
        )

    own = [pltpu.make_async_copy(shards[g], outs[g].at[z, me], own_sem.at[g]) for g in range(3)]

    def begin(g):
        @pl.when(up_ok)
        def _():
            up(g, z, shards[g]).start()

        @pl.when(down_ok)
        def _():
            down(g, z, shards[g]).start()

        along(g, z, me, x_send, x_recv, x_dev, shards[g]).start()
        along(g, z, me, y_send, y_recv, y_dev, shards[g]).start()
        core(g, z, 0, me, shards[g]).start()
        own[g].start()

    def column(g, origin):
        from_z(g, origin).wait_recv()

        @pl.when((origin < z) & up_ok)
        def _():
            up(g, origin).start()

        @pl.when((origin > z) & down_ok)
        def _():
            down(g, origin).start()

        along(g, origin, me, x_send, x_recv, x_dev).start()
        along(g, origin, me, y_send, y_recv, y_dev).start()
        core(g, origin, 0, me).start()

    def sides(g, origin):
        along(g, origin, x_slot, x_send, x_recv, x_dev).wait_recv()
        part(g, origin, x_slot, 0, a_send, a_recv, y_dev).start()
        core(g, origin, 1, x_slot).start()
        along(g, origin, y_slot, y_send, y_recv, y_dev).wait_recv()
        part(g, origin, y_slot, half, b_send, b_recv, x_dev).start()
        core(g, origin, 2, y_slot).start()

    def corner(g, origin):
        part(g, origin, d_slot, 0, a_send, a_recv, y_dev).wait_recv()
        part(g, origin, d_slot, half, b_send, b_recv, x_dev).wait_recv()
        core(g, origin, 3, d_slot).start()

    def partner(g, origin):
        for kind in range(4):
            core(g, origin, kind, slots[kind]).wait_recv()

    begin(0)
    small_own = pltpu.make_async_copy(small, small_all.at[mine], s_send.at[0])
    small_own.start()
    for n, p in enumerate(peers):
        remote(small, small_all.at[mine], s_send.at[n + 1], s_recv.at[n], at(*p)).start()

    def to_heads(t, c):
        return remote(send_rows.at[t, c], rows.at[ctx * n_tensor + z], q_send.at[t, c],
                      q_recv.at[ctx * n_tensor + z], at(dp, c, t))

    def from_token(block):
        return remote(rows.at[block], rows.at[block], q_send.at[0, 0], q_recv.at[block], x_dev)

    count = x.shape[0]
    span = count // n_ctx
    width = x.shape[1]
    here = pltpu.make_async_copy(send_rows.at[z, ctx], rows.at[ctx * n_tensor + z], own_sem.at[3])

    def whole(ref, t):
        return ref[t].reshape(8 * n_rows, ref.shape[-1])

    def project(t):
        partner(0, t)
        bias = gathered(small_all[pl.ds(t * 8, 8), 0, :], a_spread, a_owned)
        value = jnp.dot(x[...], whole(f0, t), preferred_element_type=F32)[:, :wide] + bias
        send_rows[t] = value.astype(BF16).reshape(n_ctx, span, wide)
        to_heads(t, yp).start()

        @pl.when(t != z)
        def _():
            to_heads(t, ctx).start()

        @pl.when(t == z)
        def _():
            here.start()

    def first(j, carry):
        @pl.when((j >= 1) & (j < n_tensor))
        def _():
            column(0, near(j))

        @pl.when((j >= 1) & (j < n_tensor + 1))
        def _():
            sides(0, near(j - 1))

        @pl.when((j >= 2) & (j < n_tensor + 2))
        def _():
            corner(0, near(j - 2))

        @pl.when(j == 2)
        def _():
            own[0].wait()
            small_own.wait()
            for n, p in enumerate(peers):
                copy = remote(small, small_all.at[mine], s_send.at[n + 1], s_recv.at[n], at(*p))
                copy.wait_send()
                copy.wait_recv()

        @pl.when(j >= 3)
        def _():
            project(near(j - 3))

        return carry

    lax.fori_loop(0, n_tensor + 3, first, 0)
    for g in (1, 2):
        begin(g)
    for k in range(6):
        vectors[pl.ds(k, 1), :] = gathered(small_all[:, k + 1, :], v_spread, v_owned)
    for g in (1, 2):
        sides(g, z)
    for g in (1, 2):
        corner(g, z)
    here.wait()
    for j in range(n_ctx):
        for k in range(n_tensor):
            if j or k:
                from_token(lax.rem(ctx + j, n_ctx) * n_tensor + lax.rem(z + k, n_tensor)).wait_recv()

    n_blocks = n_ctx * n_tensor
    total_rows = n_blocks * span
    n_units = n_blocks // 2

    def to_tokens(block):
        c, t = lax.div(block, n_tensor), lax.rem(block, n_tensor)
        return remote(send_mixed.at[block], mixed.at[z * n_ctx + ctx], m_send.at[block],
                      m_recv.at[z * n_ctx + ctx], at(dp, c, t))

    def keep(i):
        return pltpu.make_async_copy(probs.at[:, pl.ds(i * 2 * span, 2 * span)],
                                     probs_out.at[:, pl.ds(i * 2 * span, 2 * span)], p_sem.at[i])

    own_block = ctx * n_tensor + z
    own_mixed = pltpu.make_async_copy(send_mixed.at[own_block], mixed.at[z * n_ctx + ctx], own_sem.at[4])

    def attend(i, carry):
        blocks = pl.ds(2 * i, 2)
        lines = pl.ds(pl.multiple_of(i * 2 * span, 2 * span), 2 * span)
        allowed = seg_col[lines, :] == seg_row[...]
        for h in range(heads):
            q = rows[blocks, :, pl.ds(HEAD_DIM * h, HEAD_DIM)].reshape(2 * span, HEAD_DIM)
            k = rows[:, :, pl.ds(HEAD_DIM * (heads + h), HEAD_DIM)].reshape(total_rows, HEAD_DIM)
            v = rows[:, :, pl.ds(HEAD_DIM * (2 * heads + h), HEAD_DIM)].reshape(total_rows, HEAD_DIM)
            scores = SCALE * lax.dot_general(q, k, (((1,), (1,)), ((), ())), preferred_element_type=F32)
            scores = jnp.where(allowed, scores, NEG)
            weights = jnp.exp(scores - jnp.max(scores, axis=-1, keepdims=True))
            low = (weights * (1.0 / jnp.sum(weights, axis=-1, keepdims=True))).astype(BF16)
            probs[h, lines, :] = low
            value = jnp.dot(low, v, preferred_element_type=F32)
            mixed_float[lines, pl.ds(HEAD_DIM * h, HEAD_DIM)] = value
            send_mixed[blocks, :, pl.ds(HEAD_DIM * h, HEAD_DIM)] = value.astype(BF16).reshape(2, span, HEAD_DIM)
        keep(i).start()
        for n in range(2):
            @pl.when(2 * i + n != own_block)
            def _():
                to_tokens(2 * i + n).start()

            @pl.when(2 * i + n == own_block)
            def _():
                own_mixed.start()

        return carry

    lax.fori_loop(0, n_units, attend, 0)

    def second(j, carry):
        @pl.when((j >= 1) & (j < n_tensor))
        def _():
            for g in (1, 2):
                column(g, near(j))

        @pl.when((j >= 2) & (j < n_tensor))
        def _():
            for g in (1, 2):
                sides(g, near(j - 1))

        return carry

    lax.fori_loop(1, n_tensor, second, 0)

    own_mixed.wait()
    for j in range(n_ctx):
        for k in range(n_tensor):
            if j or k:
                c, t = lax.rem(ctx + j, n_ctx), lax.rem(z + k, n_tensor)
                slot = t * n_ctx + c
                remote(mixed.at[slot], mixed.at[slot], m_send.at[0], m_recv.at[slot], x_dev).wait_recv()

    flip = (((1,), (1,)), ((), ()))
    total[...] = x[...].astype(F32) + vectors[pl.ds(0, 1), :]

    def add_merge(t, carry):
        value = mixed[pl.ds(t * n_ctx, n_ctx)].reshape(count, part_width)
        total[...] += lax.dot_general(value, whole(f0, t)[:, wide:], flip, preferred_element_type=F32)
        return carry

    lax.fori_loop(0, n_tensor, add_merge, 0)
    normal[0], scale[0] = normalize(total[...])
    value = normal[0] * vectors[pl.ds(1, 1), :] + vectors[pl.ds(2, 1), :]
    total[...] = value + vectors[pl.ds(3, 1), :]
    first_low[...] = value.astype(BF16)
    for g in (1, 2):
        own[g].wait()

    def units(t):
        for g in (1, 2):
            partner(g, t)
        bias = gathered(small_all[pl.ds(t * 8, 8), 7, :], e_spread, e_owned)
        before = jnp.dot(first_low[...], whole(f1, t), preferred_element_type=F32) + bias
        value, rise = gelu_exact(before)
        low = value.astype(BF16)
        active[t] = low
        slope[t] = rise
        total[...] += lax.dot_general(low, whole(f2, t), flip, preferred_element_type=F32)

    def third(j, carry):
        @pl.when(j == n_tensor)
        def _():
            for g in (1, 2):
                sides(g, near(j - 1))

        @pl.when(j < n_tensor + 2)
        def _():
            for g in (1, 2):
                corner(g, near(j - 2))

        units(near(j - 3))
        return carry

    lax.fori_loop(3, n_tensor + 3, third, 0)

    normal[1], scale[1] = normalize(total[...])
    gain = vectors[pl.ds(4, 1), :]
    outputs[...] = normal[1] * gain + vectors[pl.ds(5, 1), :]
    pull = cotangent[...].astype(F32)
    small_grads[:, 0, :] = jnp.zeros_like(small_grads[:, 0, :])
    small_grads[:, 5, :] = scattered(total_rows_of(pull * normal[1]), v_spread, v_owned)
    small_grads[:, 6, :] = scattered(total_rows_of(pull), v_spread, v_owned)
    second_grad = normalize_back(pull, normal[1], scale[1], gain)
    small_grads[:, 4, :] = scattered(total_rows_of(second_grad), v_spread, v_owned)
    total[...] = second_grad
    second_low[...] = second_grad.astype(BF16)
    turned[0] = second_low[...].T
    turned[1] = first_low[...].T
    blocked = (2, 2, 2, n_rows, g1.shape[-1])

    def store(which, t):
        grad, out = ((g1, g1_out), (g2, g2_out))[which]
        return pltpu.make_async_copy(grad.at[t], out.at[t], g_sem.at[which, t])

    def units_back(t, carry):
        low = active[t]
        g2[t] = jnp.dot(turned[0], low, preferred_element_type=F32).astype(BF16).reshape(blocked)
        store(1, t).start()
        back = jnp.dot(second_low[...], whole(f2, t), preferred_element_type=F32) * slope[t]
        back_low = back.astype(BF16)
        sums = total_rows_of(back_low.astype(F32))
        small_grads[pl.ds(t * 8, 8), 7, :] = scattered(sums, e_spread, e_owned)
        g1[t] = jnp.dot(turned[1], back_low, preferred_element_type=F32).astype(BF16).reshape(blocked)
        store(0, t).start()
        total[...] += lax.dot_general(back_low, whole(f1, t), flip, preferred_element_type=F32)
        return carry

    lax.fori_loop(0, n_tensor, units_back, 0)
    pull = total[...]
    small_grads[:, 2, :] = scattered(total_rows_of(pull * normal[0]), v_spread, v_owned)
    small_grads[:, 3, :] = scattered(total_rows_of(pull), v_spread, v_owned)
    value = normalize_back(pull, normal[0], scale[0], vectors[pl.ds(1, 1), :])
    small_grads[:, 1, :] = scattered(total_rows_of(value), v_spread, v_owned)
    first_grad[...] = value
    first_low_grad[...] = value.astype(BF16)

    for j in range(n_ctx):
        for k in range(n_tensor):
            if j or k:
                c, t = lax.rem(ctx + j, n_ctx), lax.rem(z + k, n_tensor)
                to_tokens(c * n_tensor + t).wait_send()
                to_heads(t, c).wait_send()
    for i in range(n_units):
        keep(i).wait()

    def finish(origin, carry):
        for g in range(3):
            for kind in range(4):
                core(g, origin, kind, slots[kind]).wait_send()
            along(g, origin, me, x_send, x_recv, x_dev).wait_send()
            along(g, origin, me, y_send, y_recv, y_dev).wait_send()
            part(g, origin, x_slot, 0, a_send, a_recv, y_dev).wait_send()
            part(g, origin, y_slot, half, b_send, b_recv, x_dev).wait_send()

            @pl.when((origin <= z) & up_ok)
            def _():
                up(g, origin).wait_send()

            @pl.when((origin >= z) & down_ok)
            def _():
                down(g, origin).wait_send()
        for which in range(2):
            store(which, origin).wait()
        return carry

    lax.fori_loop(0, n_tensor, finish, 0)


def forward_layer(n_tensor, heads, x, cotangent, triple, merge, w1, shrink, small, matrices, seg_row, seg_col):
    rows, cols = w1.shape
    count, width = x.shape
    n_small = 8 * n_tensor
    blocks = 2 * n_tensor
    span = count // 2
    length = blocks * span
    part = heads * HEAD_DIM
    dma = pltpu.SemaphoreType.DMA
    shape = jax.ShapeDtypeStruct
    full = (n_tensor, 8, rows, cols)
    split = (n_tensor, 2, 2, 2, rows, cols)
    pair = [dma((3, n_tensor)), dma((3, n_tensor))]
    vmem = pl.BlockSpec(memory_space=pltpu.VMEM)
    hbm = pl.BlockSpec(memory_space=pl.ANY)
    return pl.pallas_call(
        functools.partial(forward_kernel, n_tensor, heads),
        out_shape=(
            shape(full, BF16), shape((blocks, span, 3 * part), BF16),
            shape((length, part), F32), shape((heads, length, length), BF16), shape((blocks, span, part), BF16),
            shape((count, width), F32), shape((count, width), BF16), shape((count, width), BF16),
            shape((count, width), F32), shape((n_small,) + small.shape, F32), shape(split, BF16), shape(split, BF16),
        ),
        in_specs=[vmem] * 15,
        out_specs=(vmem, vmem, vmem, hbm) + (vmem,) * 6 + (hbm, hbm),
        scratch_shapes=[
            pltpu.VMEM((rows, cols), BF16),
            pltpu.VMEM((rows, cols), BF16),
            pltpu.VMEM(full, BF16),
            pltpu.VMEM(full, BF16),
            pltpu.VMEM((n_small,) + small.shape, F32),
            pltpu.VMEM((n_tensor, 2, span, 3 * part), BF16),
            pltpu.VMEM((blocks, span, part), BF16),
            pltpu.VMEM((heads, length, length), BF16),
            pltpu.VMEM((8, width), F32),
            pltpu.VMEM((2, count, width), F32),
            pltpu.VMEM((2, count, 1), F32),
            pltpu.VMEM((n_tensor, count, cols), BF16),
            pltpu.VMEM((n_tensor, count, cols), F32),
            pltpu.VMEM((count, width), F32),
            pltpu.VMEM((count, width), BF16),
            pltpu.VMEM((2, width, count), BF16),
            pltpu.VMEM(split, BF16),
            pltpu.VMEM(split, BF16),
            dma((5,)), dma((3, n_tensor)),
        ] + pair * 5 + [
            dma((3, 4, n_tensor)), dma((3, 4, n_tensor)), dma((n_small,)), dma((n_small,)),
            dma((n_tensor, 2)), dma((blocks,)), dma((blocks,)), dma((blocks,)), dma((blocks // 2,)),
            dma((2, n_tensor)),
        ],
        compiler_params=pltpu.CompilerParams(collective_id=0, has_side_effects=True, vmem_limit_bytes=60 << 20),
        cost_estimate=pl.CostEstimate(flops=0, bytes_accessed=w1.size * 400, transcendentals=0),
        name="forward_layer",
    )(x, cotangent, triple, merge, w1, shrink, small, *matrices, seg_row, seg_col)


def sum_steps(n_tensor, grads, acc, core_in, y1_in, x1_in, x2_in, y2_in, z_in, load_sem, c_send, c_recv,
              y1_send, y1_recv, x1_send, x1_recv, x2_send, x2_recv, y2_send, y2_recv, z_send, z_recv):
    dp, ctx, z = (lax.axis_index(a) for a in ALL)
    rows = acc.shape[-2]
    half = rows // 2
    core = lax.rem(dp, 2)
    x = lax.div(dp, 2)
    xp, yp = 1 - x, 1 - ctx
    x_dev, y_dev, c_dev = at(xp * 2 + core, ctx, z), at(dp, yp, z), at(x * 2 + 1 - core, ctx, z)
    low, high = pl.ds(0, half), pl.ds(half, half)
    count = range(len(grads))

    def load(g, t):
        return pltpu.make_async_copy(grads[g].at[t, :, core], acc.at[g, t], load_sem.at[g, t])

    def to_core(g, t):
        return remote(grads[g].at[t, :, 1 - core], core_in.at[g, t], c_send.at[g, t], c_recv.at[g, t], c_dev)

    def y1(g, t):
        return remote(acc.at[g, t, :, yp, low], y1_in.at[g, t], y1_send.at[g, t], y1_recv.at[g, t], y_dev)

    def x1(g, t):
        return remote(acc.at[g, t, xp, :, high], x1_in.at[g, t], x1_send.at[g, t], x1_recv.at[g, t], x_dev)

    def x2(g, t):
        return remote(acc.at[g, t, xp, ctx, low], x2_in.at[g, t], x2_send.at[g, t], x2_recv.at[g, t], x_dev)

    def y2(g, t):
        return remote(acc.at[g, t, x, yp, high], y2_in.at[g, t], y2_send.at[g, t], y2_recv.at[g, t], y_dev)

    def to_z(g, t):
        return remote(acc.at[g, t, x, ctx], z_in.at[g, z], z_send.at[g, t], z_recv.at[g, z], at(dp, ctx, t))

    def add(a, b):
        return (a.astype(F32) + b.astype(F32)).astype(BF16)

    def target(j):
        return lax.rem(z + 1 + j, n_tensor)

    def begin(j):
        t = target(j)
        for g in count:
            to_core(g, t).start()
            load(g, t).start()

    def core_step(j):
        t = target(j)
        for g in count:
            load(g, t).wait()
            to_core(g, t).wait_recv()
            acc[g, t] = add(acc[g, t], core_in[g, t])
            y1(g, t).start()
            x1(g, t).start()

    def first_step(j):
        t = target(j)
        for g in count:
            y1(g, t).wait_recv()
            for i in range(2):
                acc[g, t, i, ctx, low] = add(acc[g, t, i, ctx, low], y1_in[g, t, i])
            x2(g, t).start()
            x1(g, t).wait_recv()
            for i in range(2):
                acc[g, t, x, i, high] = add(acc[g, t, x, i, high], x1_in[g, t, i])
            y2(g, t).start()

    def second_step(j):
        t = target(j)
        for g in count:
            x2(g, t).wait_recv()
            acc[g, t, x, ctx, low] = add(acc[g, t, x, ctx, low], x2_in[g, t])
            y2(g, t).wait_recv()
            acc[g, t, x, ctx, high] = add(acc[g, t, x, ctx, high], y2_in[g, t])

            @pl.when(j < n_tensor - 1)
            def _():
                to_z(g, t).start()

    def step(j):
        @pl.when(j < n_tensor)
        def _():
            core_step(j)

        @pl.when((j >= 1) & (j < n_tensor + 1))
        def _():
            first_step(j - 1)

        @pl.when(j >= 2)
        def _():
            second_step(j - 2)

    def end(outs):
        for g in count:
            outs[g][...] = acc[g, z, x, ctx].astype(F32)
            for k in range(1, n_tensor):
                origin = lax.rem(z + n_tensor - k, n_tensor)
                block = z_in.at[g, origin]
                remote(block, block, z_send.at[g, origin], z_recv.at[g, origin], x_dev).wait_recv()
                outs[g][...] += z_in[g, origin].astype(F32)

        def finish(t, carry):
            for g in count:
                for copy in (to_core, y1, x1, x2, y2):
                    copy(g, t).wait_send()
            return carry

        lax.fori_loop(0, n_tensor, finish, 0)
        for g in count:
            for k in range(1, n_tensor):
                to_z(g, lax.rem(z + k, n_tensor)).wait_send()

    return begin, step, end


def sum_scratch(n_grads, n_tensor, rows, cols):
    dma = pltpu.SemaphoreType.DMA
    grid = (n_grads, n_tensor)
    half = rows // 2
    return [
        pltpu.VMEM(grid + (2, 2, rows, cols), BF16),
        pltpu.VMEM(grid + (2, 2, rows, cols), BF16),
        pltpu.VMEM(grid + (2, half, cols), BF16),
        pltpu.VMEM(grid + (2, half, cols), BF16),
        pltpu.VMEM(grid + (half, cols), BF16),
        pltpu.VMEM(grid + (half, cols), BF16),
        pltpu.VMEM(grid + (rows, cols), BF16),
    ] + [dma(grid)] * 13


def backward_kernel(n_tensor, heads, first_low, first_grad, x, f0, mixed, small, spread, owned, rows, mixed_float,
                    probs_in, g1, g2, input_grad, o0, o1, o2, small_out,
                    turned, g0, mixed_grad, grad, probs, send_rows, qkv_grad, key_sum, value_sum, small_send, small_in,
                    own_sem, g_send, g_recv, q_send, q_recv, p_sem, s_send, s_recv, *scratch):
    dp, ctx, z = (lax.axis_index(a) for a in ALL)
    n_ctx = 2
    n_blocks = n_ctx * n_tensor
    n_units = n_blocks // 2
    span = grad.shape[1]
    part = grad.shape[2]
    wide = 3 * part
    n_rows, width = f0.shape[-2:]
    total_rows = n_blocks * span
    own_block = ctx * n_tensor + z
    own_slot = z * n_ctx + ctx
    mine = z * 8 + dp * 2 + ctx
    peers = everyone(4, 2, n_tensor)
    greet([at(*p) for p in peers])
    others = [(lax.rem(ctx + j, n_ctx), lax.rem(z + k, n_tensor))
              for k in (2, 3, 1, 0) for j in range(n_ctx) if (j or k) and k < n_tensor]
    half = len(scratch) // 2
    begin, step, end = sum_steps(n_tensor, (g1, g2), *scratch[:half])
    begin_last, step_last, end_last = sum_steps(n_tensor, (g0,), *scratch[half:])

    def to_heads(c, t):
        return remote(mixed_grad.at[t * n_ctx + c], grad.at[own_block], g_send.at[t * n_ctx + c],
                      g_recv.at[own_block], at(dp, c, t))

    def load(i):
        lines = pl.ds(i * 2 * span, 2 * span)
        return pltpu.make_async_copy(probs_in.at[:, lines], probs.at[:, lines], p_sem.at[i])

    here = pltpu.make_async_copy(mixed_grad.at[own_slot], grad.at[own_block], own_sem.at[0])

    def begin_all(j, carry):
        begin(j)
        return carry

    lax.fori_loop(0, n_tensor, begin_all, 0)

    def spread_grad(j, carry):
        t = lax.rem(z + 1 + j, n_tensor)
        weight = f0[t].reshape(8 * n_rows, width)[:, wide:]
        value = jnp.dot(first_low[...], weight, preferred_element_type=F32).astype(BF16)
        mixed_grad[pl.ds(t * n_ctx, n_ctx)] = value.reshape(n_ctx, span, part)
        to_heads(1 - ctx, t).start()

        @pl.when(t != z)
        def _():
            to_heads(ctx, t).start()

        @pl.when(t == z)
        def _():
            here.start()

        return carry

    lax.fori_loop(0, n_tensor, spread_grad, 0)
    for i in range(n_units):
        load(i).start()
    turned[0] = first_low[...].T
    turned[1] = x[...].T
    small_send[...] = small[...]

    def merge_grad(t, carry):
        value = jnp.dot(turned[0], mixed[pl.ds(t * n_ctx, n_ctx)].reshape(n_ctx * span, part),
                        preferred_element_type=F32)
        g0[t, :, :, :, :, pl.ds(wide, part)] = value.astype(BF16).reshape(2, 2, 2, n_rows, part)
        return carry

    lax.fori_loop(0, n_tensor, merge_grad, 0)
    step(0)
    here.wait()
    for c, t in others:
        block = c * n_tensor + t
        remote(grad.at[block], grad.at[block], g_send.at[0], g_recv.at[block], at(dp, c, t)).wait_recv()
    for i in range(n_units):
        load(i).wait()

    def one_head(h):
        lanes = pl.ds(HEAD_DIM * h, HEAD_DIM)
        k_lanes = pl.ds(HEAD_DIM * (heads + h), HEAD_DIM)
        v_lanes = pl.ds(HEAD_DIM * (2 * heads + h), HEAD_DIM)
        key_sum[...] = jnp.zeros_like(key_sum)
        value_sum[...] = jnp.zeros_like(value_sum)

        def unit(i, carry):
            blocks = pl.ds(2 * i, 2)
            lines = pl.ds(pl.multiple_of(i * 2 * span, 2 * span), 2 * span)
            q = rows[blocks, :, lanes].reshape(2 * span, HEAD_DIM)
            k = rows[:, :, k_lanes].reshape(total_rows, HEAD_DIM)
            v = rows[:, :, v_lanes].reshape(total_rows, HEAD_DIM)
            up = grad[blocks, :, lanes].reshape(2 * span, HEAD_DIM)
            low = probs[h, lines, :]
            delta = jnp.sum(up.astype(F32) * mixed_float[lines, lanes], axis=-1, keepdims=True)
            pull = lax.dot_general(up, v, (((1,), (1,)), ((), ())), preferred_element_type=F32)
            score = (low.astype(F32) * (pull - delta)).astype(BF16)
            query = SCALE * jnp.dot(score, k, preferred_element_type=F32)
            send_rows[blocks, :, lanes] = query.astype(BF16).reshape(2, span, HEAD_DIM)
            key_sum[...] += lax.dot_general(q, score, (((0,), (0,)), ((), ())), preferred_element_type=F32)
            value_sum[...] += lax.dot_general(up, low, (((0,), (0,)), ((), ())), preferred_element_type=F32)
            return carry

        lax.fori_loop(0, n_units, unit, 0)
        key = (SCALE * key_sum[...]).T.astype(BF16)
        value = value_sum[...].T.astype(BF16)
        send_rows[:, :, k_lanes] = key.reshape(n_blocks, span, HEAD_DIM)
        send_rows[:, :, v_lanes] = value.reshape(n_blocks, span, HEAD_DIM)

    for h in range(heads):
        one_head(h)
        if h == 0:
            step(1)
        elif h == 1:
            step(2)

    def to_tokens(c, t):
        return remote(send_rows.at[c * n_tensor + t], qkv_grad.at[own_slot], q_send.at[c * n_tensor + t],
                      q_recv.at[own_slot], at(dp, c, t))

    there = pltpu.make_async_copy(send_rows.at[own_block], qkv_grad.at[own_slot], own_sem.at[1])
    for c, t in others:
        to_tokens(c, t).start()
    there.start()

    def one(j, carry):
        step(j)
        return carry

    lax.fori_loop(min(heads, 3), n_tensor + 2, one, 0)

    def arrived(t, c):
        slot = t * n_ctx + c
        remote(qkv_grad.at[slot], qkv_grad.at[slot], q_send.at[0], q_recv.at[slot], at(dp, c, t)).wait_recv()

    def weight_grad(j, carry):
        t = lax.rem(z + 1 + j, n_tensor)
        arrived(t, 1 - ctx)

        @pl.when(t != z)
        def _():
            arrived(t, ctx)

        @pl.when(t == z)
        def _():
            there.wait()

        pull = qkv_grad[pl.ds(t * n_ctx, n_ctx)].reshape(n_ctx * span, wide)
        value = jnp.dot(turned[1], pull, preferred_element_type=F32)
        g0[t, :, :, :, :, pl.ds(0, wide)] = value.astype(BF16).reshape(2, 2, 2, n_rows, wide)
        begin_last(j)
        small_send[pl.ds(t * 8, 8), 0, :] = scattered(total_rows_of(pull.astype(F32)), spread, owned)
        return carry

    lax.fori_loop(0, n_tensor, weight_grad, 0)
    small_copies = [
        remote(small_send.at[pt * 8 + pd * 2 + pc], small_in.at[n], s_send.at[n], s_recv.at[n], at(pd, pc, pt))
        for n, (pd, pc, pt) in enumerate(peers)
    ]
    for copy in small_copies:
        copy.start()
    input_grad[...] = first_grad[...]

    def last(j, carry):
        step_last(j)

        @pl.when(j < n_tensor)
        def _():
            pull = qkv_grad[pl.ds(j * n_ctx, n_ctx)].reshape(n_ctx * span, wide)
            weight = f0[j].reshape(8 * n_rows, width)[:, :wide]
            input_grad[...] += lax.dot_general(pull, weight, (((1,), (1,)), ((), ())), preferred_element_type=F32)

        return carry

    lax.fori_loop(0, n_tensor + 2, last, 0)
    end((o1, o2))
    end_last((o0,))
    total = small_send[mine]
    for n in range(len(peers)):
        small_copies[n].wait()
        total = total + small_in[n]
    small_out[...] = total
    for c, t in others:
        to_tokens(c, t).wait_send()
        to_heads(c, t).wait_send()


def backward_attention(n_tensor, heads, first_low, first_grad, x, f0, mixed, small, spread, owned, rows, mixed_float,
                       probs, g1, g2):
    blocks, span, wide = rows.shape
    part = heads * HEAD_DIM
    length = blocks * span
    n_rows, cols = g1.shape[-2:]
    n_small = 8 * n_tensor
    dma = pltpu.SemaphoreType.DMA
    vmem = pl.BlockSpec(memory_space=pltpu.VMEM)
    hbm = pl.BlockSpec(memory_space=pl.ANY)
    shape = jax.ShapeDtypeStruct
    out = shape((n_rows, cols), F32)
    return pl.pallas_call(
        functools.partial(backward_kernel, n_tensor, heads),
        out_shape=(shape(first_grad.shape, F32), out, out, out, shape(small.shape[1:], F32)),
        in_specs=[vmem] * 10 + [hbm] * 3,
        out_specs=(vmem,) * 5,
        scratch_shapes=[
            pltpu.VMEM((2,) + x.shape[::-1], BF16),
            pltpu.VMEM(g1.shape, BF16),
            pltpu.VMEM((blocks, span, part), BF16),
            pltpu.VMEM((blocks, span, part), BF16),
            pltpu.VMEM((heads, length, length), BF16),
            pltpu.VMEM((blocks, span, wide), BF16),
            pltpu.VMEM((blocks, span, wide), BF16),
            pltpu.VMEM((HEAD_DIM, length), F32),
            pltpu.VMEM((HEAD_DIM, length), F32),
            pltpu.VMEM(small.shape, F32),
            pltpu.VMEM((n_small - 1,) + small.shape[1:], F32),
            dma((2,)), dma((blocks,)), dma((blocks,)), dma((blocks,)), dma((blocks,)), dma((blocks // 2,)),
            dma((n_small - 1,)), dma((n_small - 1,)),
        ] + sum_scratch(2, n_tensor, n_rows, cols) + sum_scratch(1, n_tensor, n_rows, cols),
        compiler_params=pltpu.CompilerParams(collective_id=2, has_side_effects=True, vmem_limit_bytes=58 << 20),
        cost_estimate=pl.CostEstimate(flops=0, bytes_accessed=g1.size * 24, transcendentals=0),
        name="backward_attention",
    )(first_low, first_grad, x, f0, mixed, small, spread, owned, rows, mixed_float, probs, g1, g2)


def norm_rows(total, gain, shift):
    center = total - jnp.mean(total, axis=-1, keepdims=True)
    spread = jnp.mean(center * center, axis=-1, keepdims=True)
    return center * lax.rsqrt(spread + EPS) * gain + shift


def gelu_exact(before):
    share = 0.5 + 0.5 * lax.erf(before * 0.5**0.5)
    dense = (0.5 / np.pi) ** 0.5 * jnp.exp(-0.5 * before * before)
    return before * share, share + before * dense


def dot(spec, a, b):
    return jnp.einsum(spec, a, b, preferred_element_type=F32)


def add_up(spec, a, b):
    return sum(dot(spec, a[t], b[t]) for t in range(a.shape[0]))


def local(
    inputs,
    cotangent,
    segments,
    triple_weight,
    attend_bias,
    merge_weight,
    merge_bias,
    first_gain,
    first_shift,
    expand_weight,
    expand_bias,
    shrink_weight,
    shrink_bias,
    second_gain,
    second_shift,
):
    n_dp, n_ctx, n_tensor = (lax.axis_size(a) for a in ALL)
    span, batch, width = inputs.shape
    rows = triple_weight.shape[1]
    part = triple_weight.shape[2]
    units = expand_weight.shape[1]
    owners = n_dp * n_ctx
    heads = part // HEAD_DIM
    count = batch * span
    small_part = part // owners
    unit_part = units // owners
    own_kernels = n_dp == 4 and n_ctx == 2 and batch == 2 and n_tensor == 4 and rows % 32 == 0

    narrow_in = (merge_bias, first_gain, first_shift, shrink_bias, second_gain, second_shift)
    x_low = jnp.transpose(inputs, (1, 0, 2)).reshape(count, width)
    cotangent_rows = jnp.transpose(cotangent, (1, 0, 2)).reshape(count, width)
    here = lax.axis_index("ctx")
    if own_kernels:
        labels = lax.dynamic_slice_in_dim(segments, here, 1, 0)
        lines = [attend_bias.reshape(1, -1)] + list(narrow_in) + [expand_bias]
        small = sum(
            jnp.pad(v.astype(F32), ((n, 7 - n), (0, 128 - v.shape[1]))) for n, v in enumerate(lines)
        )
        matrices = tables(n_tensor, owners, part, units)
        (f0, rows_all, mixed_float, probs, mixed, outputs_rows, first_low, first_low_grad, first_grad, small_grads,
         expand_grad, shrink_grad) = forward_layer(
            n_tensor, heads, x_low, cotangent_rows, triple_weight, merge_weight, expand_weight, shrink_weight, small,
            matrices, labels, labels.reshape(-1, 1)
        )
        inputs_gradient, r0, r1, r2, small_sum = backward_attention(
            n_tensor, heads, first_low_grad, first_grad, x_low, f0, mixed, small_grads, *matrices[:2],
            rows_all, mixed_float, probs, expand_grad, shrink_grad
        )
        narrow_out = [small_sum[:1, :small_part], small_sum[:1, small_part : 2 * small_part]]
        narrow_out += [small_sum[n : n + 1, :small_part] for n in range(1, 7)]
        expand_out = small_sum[7:, :unit_part]
    else:
        pieces = [attend_bias[0, 0], attend_bias[1, 0]] + [v[0] for v in narrow_in] + [expand_bias[0]]
        w0 = jnp.concatenate(
            [jnp.transpose(triple_weight, (1, 0, 2)).reshape(rows, 3 * part), merge_weight.T], axis=1
        )
        small = jnp.concatenate(pieces).astype(F32)
        f0, f1, f2 = (
            lax.all_gather(lax.all_gather(w, ("dp", "ctx"), axis=0, tiled=True), "tensor", axis=0, tiled=False)
            for w in (w0, expand_weight, shrink_weight.T)
        )
        small_all = lax.all_gather(lax.all_gather(small, ("dp", "ctx")), "tensor")
        f0, w_expand, w_shrink = (w.reshape(n_tensor, width, -1) for w in (f0, f1, f2))
        w_qkv, w_merge = f0[:, :, : 3 * part], f0[:, :, 3 * part :]
        narrow = small_all[:, :, : 8 * small_part].reshape(n_tensor, owners, 8, small_part)
        narrow = jnp.transpose(narrow, (2, 0, 1, 3)).reshape(8, n_tensor, part)
        merge_vec, gain_one, shift_one, shrink_vec, gain_two, shift_two = narrow[2:].reshape(6, width)
        expand_vec = small_all[:, :, 8 * small_part :].reshape(n_tensor, 1, units)
        qkv_vec = jnp.concatenate([narrow[0], jnp.zeros_like(narrow[0]), narrow[1]], axis=-1)[:, None]
        x = x_low.astype(F32)
        upstream = cotangent_rows.astype(F32)

        def to_tokens(value):
            value = value.reshape(batch, n_tensor, span, -1)
            out = lax.all_to_all(jnp.transpose(value, (1, 0, 2, 3)), "tensor", split_axis=0, concat_axis=0)
            return out.reshape(n_tensor, count, -1)

        qkv = (dot("rd,tde->tre", x_low, w_qkv) + qkv_vec).astype(BF16)
        mine = lax.all_to_all(
            qkv.reshape(n_tensor, batch, span, 3 * part), "tensor", split_axis=0, concat_axis=0
        )
        mine = jnp.transpose(mine, (1, 0, 2, 3)).reshape(batch, n_tensor * span, 3 * part)
        n_query = n_tensor * span
        own_labels = lax.dynamic_slice_in_dim(segments, here * n_query, n_query, 1)
        kv_rows = lax.all_gather(mine[..., part:], "ctx", axis=1, tiled=True)
        n_key = kv_rows.shape[1]
        q_four = mine[..., :part].reshape(batch, n_query, heads, HEAD_DIM)
        k_four = kv_rows[..., :part].reshape(batch, n_key, heads, HEAD_DIM)
        v_four = kv_rows[..., part:].reshape(batch, n_key, heads, HEAD_DIM)
        allowed = own_labels[:, None, :, None] == segments[:, None, None, :]
        scores = jnp.where(allowed, SCALE * dot("sqhd,skhd->shqk", q_four, k_four), NEG)
        top = jnp.max(scores, axis=-1)
        weights = jnp.where(allowed, jnp.exp(scores - top[..., None]), 0.0)
        total = jnp.sum(weights, axis=-1)
        mixed_float = dot("shqk,skhd->shqd", weights.astype(BF16), v_four) / total[..., None]
        logsum = top + jnp.log(total)
        mixed = to_tokens(jnp.transpose(mixed_float, (0, 2, 1, 3)).reshape(batch, n_query, part).astype(BF16))
        first_sum = x + add_up("re,de->rd", mixed, w_merge) + merge_vec
        first_norm = norm_rows(first_sum, gain_one, shift_one)
        first_low = first_norm.astype(BF16)
        before = dot("rd,tdf->trf", first_low, w_expand) + expand_vec
        active, slope = gelu_exact(before)
        active = active.astype(BF16)
        second_sum = first_norm + add_up("rf,df->rd", active, w_shrink) + shrink_vec
        outputs_rows = norm_rows(second_sum, gain_two, shift_two)

        second_grad, gain_two_grad, shift_two_grad = jax.vjp(norm_rows, second_sum, gain_two, shift_two)[1](upstream)
        shrink_vec_grad = jnp.sum(second_grad, axis=0)
        second_low = second_grad.astype(BF16)
        shrink_grad = dot("rd,trf->tdf", second_low, active).astype(BF16)
        active_grad = dot("rd,tdf->trf", second_low, w_shrink)
        before_low = (active_grad * slope).astype(BF16)
        expand_vec_grad = jnp.sum(before_low.astype(F32), axis=1)
        expand_grad = dot("rd,trf->tdf", first_low, before_low).astype(BF16)
        norm_back = add_up("rf,df->rd", before_low, w_expand)
        first_grad, gain_one_grad, shift_one_grad = jax.vjp(norm_rows, first_sum, gain_one, shift_one)[1](
            second_grad + norm_back
        )
        merge_vec_grad = jnp.sum(first_grad, axis=0)
        first_low_grad = first_grad.astype(BF16)
        vec_grads = jnp.stack(
            [merge_vec_grad, gain_one_grad, shift_one_grad, shrink_vec_grad, gain_two_grad, shift_two_grad]
        ).reshape(6, n_tensor, owners, small_part)
        vec_grads = jnp.transpose(vec_grads, (1, 2, 0, 3)).reshape(n_tensor, owners, 6 * small_part)
        small_grads = jnp.concatenate([vec_grads, expand_vec_grad.reshape(n_tensor, owners, unit_part)], axis=-1)
        merge_grad = dot("rd,tre->tde", first_low_grad, mixed).astype(BF16)
        mixed_grad = dot("rd,tde->tre", first_low_grad, w_merge).astype(BF16)
        grad_rows = lax.all_to_all(
            mixed_grad.reshape(n_tensor, batch, span, part), "tensor", split_axis=0, concat_axis=0
        )
        grad_four = jnp.transpose(grad_rows, (1, 0, 2, 3)).reshape(batch, n_query, heads, HEAD_DIM)
        delta = jnp.sum(jnp.transpose(grad_four.astype(F32), (0, 2, 1, 3)) * mixed_float, axis=-1)
        back_scores = SCALE * dot("sqhd,skhd->shqk", q_four, k_four)
        probs = jnp.where(allowed, jnp.exp(back_scores - logsum[..., None]), 0.0)
        prob_grad = dot("sqhd,skhd->shqk", grad_four, v_four)
        score_low = (probs * (prob_grad - delta[..., None])).astype(BF16)
        value_part = dot("shqk,sqhd->skhd", probs.astype(BF16), grad_four)
        query_part = SCALE * dot("shqk,skhd->sqhd", score_low, k_four)
        key_part = SCALE * dot("shqk,sqhd->skhd", score_low, q_four)
        query_part, key_part, value_part = (
            v.reshape(batch, -1, part).astype(BF16) for v in (query_part, key_part, value_part)
        )
        key_part, value_part = (
            lax.psum_scatter(v, "ctx", scatter_dimension=1, tiled=True) for v in (key_part, value_part)
        )
        qkv_grad = to_tokens(jnp.concatenate([query_part, key_part, value_part], axis=-1))
        triple_grad = dot("rd,tre->tde", x_low, qkv_grad).astype(BF16)
        attend_grad = jnp.sum(qkv_grad.astype(F32), axis=1).reshape(n_tensor, 3, owners, small_part)
        inputs_gradient = first_grad + add_up("re,de->rd", qkv_grad, w_qkv)
        small_grads = jnp.concatenate([attend_grad[:, 0], attend_grad[:, 2], small_grads], axis=-1)
        grads = (jnp.concatenate([triple_grad, merge_grad], axis=-1), expand_grad, shrink_grad)
        r0, r1, r2 = (
            lax.psum_scatter(
                lax.psum_scatter(g, "tensor", scatter_dimension=0), ("dp", "ctx"), scatter_dimension=0, tiled=True
            ).astype(F32)
            for g in grads
        )
        small_sum = lax.psum_scatter(
            lax.psum_scatter(small_grads, "tensor", scatter_dimension=0), ("dp", "ctx"), scatter_dimension=0
        )
        narrow_out = list(small_sum[: 8 * small_part].reshape(8, 1, small_part))
        expand_out = small_sum[8 * small_part :].reshape(1, unit_part)
    triple_out = jnp.transpose(r0[:, : 3 * part].reshape(rows, 3, part), (1, 0, 2))
    outputs_rows, inputs_gradient = (
        jnp.transpose(v.reshape(batch, span, width), (1, 0, 2)) for v in (outputs_rows, inputs_gradient)
    )
    return (
        outputs_rows,
        inputs_gradient,
        triple_out,
        jnp.stack(narrow_out[:2]),
        r0[:, 3 * part :].T,
        narrow_out[2],
        narrow_out[3],
        narrow_out[4],
        r1,
        expand_out,
        r2.T,
        narrow_out[5],
        narrow_out[6],
        narrow_out[7],
    )


def solution(mesh):
    in_specs = (
        P(("ctx", "tensor"), "dp", None),
        P(("ctx", "tensor"), "dp", None),
        P("dp", None),
        P(None, ("dp", "ctx"), "tensor"),
        P(None, "tensor", ("dp", "ctx")),
        P("tensor", ("dp", "ctx")),
        P("tensor", ("dp", "ctx")),
        P("tensor", ("dp", "ctx")),
        P("tensor", ("dp", "ctx")),
        P(("dp", "ctx"), "tensor"),
        P("tensor", ("dp", "ctx")),
        P("tensor", ("dp", "ctx")),
        P("tensor", ("dp", "ctx")),
        P("tensor", ("dp", "ctx")),
        P("tensor", ("dp", "ctx")),
    )
    out_specs = (
        P(("ctx", "tensor"), "dp", None),
        P(("ctx", "tensor"), "dp", None),
        P(None, ("dp", "ctx"), "tensor"),
        P(None, "tensor", ("dp", "ctx")),
        P("tensor", ("dp", "ctx")),
        P("tensor", ("dp", "ctx")),
        P("tensor", ("dp", "ctx")),
        P("tensor", ("dp", "ctx")),
        P(("dp", "ctx"), "tensor"),
        P("tensor", ("dp", "ctx")),
        P("tensor", ("dp", "ctx")),
        P("tensor", ("dp", "ctx")),
        P("tensor", ("dp", "ctx")),
        P("tensor", ("dp", "ctx")),
    )
    return jax.shard_map(local, mesh=mesh, in_specs=in_specs, out_specs=out_specs, check_vma=False)
```

```python
import functools

import jax
import jax.numpy as jnp
import numpy as np
from jax import lax
from jax.experimental import pallas as pl
from jax.experimental.pallas import tpu as pltpu
from jax.sharding import PartitionSpec as P

HEAD_DIM = 64

EPS = 1e-12
NEG = -1e30
SCALE = 0.125
MESH = pl.DeviceIdType.MESH
BF16 = jnp.bfloat16
F32 = jnp.float32
ALL = ("dp", "ctx", "tensor")
TOKENS = ("ctx", "tensor")


def at(dp, ctx, tensor):
    return {"dp": dp, "ctx": ctx, "tensor": tensor}


def remote(src, dst, send, recv, where):
    return pltpu.make_async_remote_copy(
        src_ref=src, dst_ref=dst, send_sem=send, recv_sem=recv, device_id=where, device_id_type=MESH
    )


def greet(peers):
    barrier = pltpu.get_barrier_semaphore()
    for peer in peers:
        pl.semaphore_signal(barrier, inc=1, device_id=peer, device_id_type=MESH)
    pl.semaphore_wait(barrier, len(peers))


def everyone(n_dp, n_ctx, n_tensor):
    dp, ctx, tensor = (lax.axis_index(a) for a in ALL)
    peers = []
    for i in range(n_dp):
        for j in range(n_ctx):
            for k in range(n_tensor):
                if i or j or k:
                    peers.append(
                        (lax.rem(dp + i, n_dp), lax.rem(ctx + j, n_ctx), lax.rem(tensor + k, n_tensor))
                    )
    return peers


def in_order(key, n_tensor, j):
    z = lax.axis_index("tensor")
    found = 0
    for here in range(n_tensor):
        for n, there in enumerate(sorted(range(n_tensor), key=lambda t: key(t, here))):
            found = found + jnp.where((z == here) & (j == n), there, 0)
    return found


def one_hot(n_lanes, owners, picks, width):
    spread = np.zeros((n_lanes, width), np.float32)
    owned = np.zeros((owners, width), np.float32)
    for feature, (lane, owner) in picks.items():
        spread[lane, feature] = 1.0
        owned[owner, feature] = 1.0
    return jnp.asarray(spread, BF16), jnp.asarray(owned)


def tables(n_tensor, owners, part, units):
    piece, unit = part // owners, units // owners
    attend = {n: (n % piece, n // piece) for n in range(part)}
    attend.update({2 * part + n: (piece + n % piece, n // piece) for n in range(part)})
    whole = {t * part + n: (n % piece, t * owners + n // piece) for t in range(n_tensor) for n in range(part)}
    expand = {n: (n % unit, n // unit) for n in range(units)}
    return (
        one_hot(128, owners, attend, 3 * part)
        + one_hot(128, n_tensor * owners, whole, n_tensor * part)
        + one_hot(128, owners, expand, units)
    )


def gathered(pieces, spread, owned):
    value = jnp.dot(pieces.astype(BF16), spread[...], preferred_element_type=F32)
    return jnp.sum(value * owned[...], axis=0, keepdims=True)


def scattered(vector, spread, owned):
    total = vector * owned[...]
    upper = total.astype(BF16)
    lower = (total - upper.astype(F32)).astype(BF16)
    flip = (((1,), (1,)), ((), ()))
    return lax.dot_general(upper, spread[...], flip, preferred_element_type=F32) + lax.dot_general(
        lower, spread[...], flip, preferred_element_type=F32
    )


def normalize(total):
    center = total - jnp.mean(total, axis=-1, keepdims=True)
    spread = jnp.mean(center * center, axis=-1, keepdims=True)
    scale = lax.rsqrt(spread + EPS)
    return center * scale, scale


def normalize_back(up, normal, scale, gain):
    pull = up * gain
    return scale * (
        pull - jnp.mean(pull, axis=-1, keepdims=True) - normal * jnp.mean(pull * normal, axis=-1, keepdims=True)
    )


def total_rows_of(value):
    return jnp.sum(value, axis=0, keepdims=True)


def forward_kernel(n_tensor, heads, x, cotangent, triple, merge, w1, shrink, small, a_spread, a_owned, v_spread,
                   v_owned, e_spread, e_owned, seg_row, seg_col,
                   f0, rows, mixed_float, probs_out, mixed, outputs, first_low, first_low_grad, first_grad,
                   small_grads, g1_out, g2_out,
                   w0, w2, f1, f2, small_all, send_rows, send_mixed, probs, vectors, normal, scale, active, slope,
                   total, second_low, turned, g1, g2,
                   own_sem, z_up, z_down, z_recv, x_send, x_recv, y_send, y_recv, a_send, a_recv, b_send, b_recv,
                   c_send, c_recv, s_send, s_recv, q_send, q_recv, m_send, m_recv, p_sem, g_sem):
    shards, outs = (w0, w1, w2), (f0, f1, f2)
    dp, ctx, z = (lax.axis_index(a) for a in ALL)
    n_ctx = 2
    n_rows = w0.shape[0]
    half = n_rows // 2
    xp = lax.rem(dp + 2, 4)
    cp = dp + 1 - 2 * lax.rem(dp, 2)
    yp = 1 - ctx
    xcp = lax.rem(cp + 2, 4)
    me = dp * 2 + ctx
    mine = z * 8 + me
    peers = everyone(4, 2, n_tensor)
    wide = a_spread.shape[1]
    part_width = wide // 3
    for i in range(3):
        w0[:, pl.ds(i * part_width, part_width)] = triple[i]
    w0[:, pl.ds(wide, merge.shape[0])] = merge[...].T
    w2[...] = shrink[...].T
    greet([at(*p) for p in peers])
    x_dev, y_dev, c_dev = at(xp, ctx, z), at(dp, yp, z), at(cp, ctx, z)
    x_slot, y_slot, d_slot = xp * 2 + ctx, dp * 2 + yp, xp * 2 + yp
    slots = (cp * 2 + ctx, xcp * 2 + ctx, cp * 2 + yp, xcp * 2 + yp)
    up_ok, down_ok = z < n_tensor - 1, z > 0

    def near(j):
        middle = (n_tensor - 1) / 2
        return in_order(lambda t, here: (abs(t - here), abs(t - middle)), n_tensor, j)

    def up(g, origin, src=None):
        block = outs[g].at[origin, me]
        return remote(block if src is None else src, block, z_up.at[g, origin], z_recv.at[g, origin],
                      at(dp, ctx, jnp.minimum(z + 1, n_tensor - 1)))

    def down(g, origin, src=None):
        block = outs[g].at[origin, me]
        return remote(block if src is None else src, block, z_down.at[g, origin], z_recv.at[g, origin],
                      at(dp, ctx, jnp.maximum(z - 1, 0)))

    def from_z(g, origin):
        block = outs[g].at[origin, me]
        return remote(block, block, z_up.at[g, origin], z_recv.at[g, origin], x_dev)

    def along(g, origin, slot, send, recv, dev, src=None):
        block = outs[g].at[origin, slot]
        return remote(block if src is None else src, block, send.at[g, origin], recv.at[g, origin], dev)

    def part(g, origin, slot, lo, send, recv, dev):
        block = outs[g].at[origin, slot, pl.ds(lo, half)]
        return remote(block, block, send.at[g, origin], recv.at[g, origin], dev)

    def core(g, origin, kind, slot, src=None):
        block = outs[g].at[origin, slot]
        return remote(
            block if src is None else src, block, c_send.at[g, kind, origin], c_recv.at[g, kind, origin], c_dev
        )

    own = [pltpu.make_async_copy(shards[g], outs[g].at[z, me], own_sem.at[g]) for g in range(3)]

    def begin(g):
        @pl.when(up_ok)
        def _():
            up(g, z, shards[g]).start()

        @pl.when(down_ok)
        def _():
            down(g, z, shards[g]).start()

        along(g, z, me, x_send, x_recv, x_dev, shards[g]).start()
        along(g, z, me, y_send, y_recv, y_dev, shards[g]).start()
        core(g, z, 0, me, shards[g]).start()
        own[g].start()

    def column(g, origin):
        from_z(g, origin).wait_recv()

        @pl.when((origin < z) & up_ok)
        def _():
            up(g, origin).start()

        @pl.when((origin > z) & down_ok)
        def _():
            down(g, origin).start()

        along(g, origin, me, x_send, x_recv, x_dev).start()
        along(g, origin, me, y_send, y_recv, y_dev).start()
        core(g, origin, 0, me).start()

    def sides(g, origin):
        along(g, origin, x_slot, x_send, x_recv, x_dev).wait_recv()
        part(g, origin, x_slot, 0, a_send, a_recv, y_dev).start()
        core(g, origin, 1, x_slot).start()
        along(g, origin, y_slot, y_send, y_recv, y_dev).wait_recv()
        part(g, origin, y_slot, half, b_send, b_recv, x_dev).start()
        core(g, origin, 2, y_slot).start()

    def corner(g, origin):
        part(g, origin, d_slot, 0, a_send, a_recv, y_dev).wait_recv()
        part(g, origin, d_slot, half, b_send, b_recv, x_dev).wait_recv()
        core(g, origin, 3, d_slot).start()

    def partner(g, origin):
        for kind in range(4):
            core(g, origin, kind, slots[kind]).wait_recv()

    begin(0)
    small_own = pltpu.make_async_copy(small, small_all.at[mine], s_send.at[0])
    small_own.start()
    for n, p in enumerate(peers):
        remote(small, small_all.at[mine], s_send.at[n + 1], s_recv.at[n], at(*p)).start()

    def to_heads(t, c):
        return remote(send_rows.at[t, c], rows.at[ctx * n_tensor + z], q_send.at[t, c],
                      q_recv.at[ctx * n_tensor + z], at(dp, c, t))

    def from_token(block):
        return remote(rows.at[block], rows.at[block], q_send.at[0, 0], q_recv.at[block], x_dev)

    count = x.shape[0]
    span = count // n_ctx
    width = x.shape[1]
    here = pltpu.make_async_copy(send_rows.at[z, ctx], rows.at[ctx * n_tensor + z], own_sem.at[3])

    def whole(ref, t):
        return ref[t].reshape(8 * n_rows, ref.shape[-1])

    def project(t):
        partner(0, t)
        bias = gathered(small_all[pl.ds(t * 8, 8), 0, :], a_spread, a_owned)
        value = jnp.dot(x[...], whole(f0, t), preferred_element_type=F32)[:, :wide] + bias
        send_rows[t] = value.astype(BF16).reshape(n_ctx, span, wide)
        to_heads(t, yp).start()

        @pl.when(t != z)
        def _():
            to_heads(t, ctx).start()

        @pl.when(t == z)
        def _():
            here.start()

    def first(j, carry):
        @pl.when(j < n_tensor - 1)
        def _():
            column(0, near(j + 1))

        @pl.when(j < n_tensor)
        def _():
            sides(0, near(j))

        @pl.when(j >= 1)
        def _():
            corner(0, near(j - 1))

        @pl.when(j == 1)
        def _():
            own[0].wait()
            small_own.wait()
            for n, p in enumerate(peers):
                copy = remote(small, small_all.at[mine], s_send.at[n + 1], s_recv.at[n], at(*p))
                copy.wait_send()
                copy.wait_recv()

        @pl.when(j >= 1)
        def _():
            project(near(j - 1))

        return carry

    lax.fori_loop(0, n_tensor + 1, first, 0)
    for g in (1, 2):
        begin(g)
    for k in range(6):
        vectors[pl.ds(k, 1), :] = gathered(small_all[:, k + 1, :], v_spread, v_owned)
    for g in (1, 2):
        sides(g, z)
    for g in (1, 2):
        corner(g, z)
    here.wait()
    for j in range(n_ctx):
        for k in range(n_tensor):
            if j or k:
                from_token(lax.rem(ctx + j, n_ctx) * n_tensor + lax.rem(z + k, n_tensor)).wait_recv()

    n_blocks = n_ctx * n_tensor
    total_rows = n_blocks * span
    n_units = n_blocks // 2

    def to_tokens(block):
        c, t = lax.div(block, n_tensor), lax.rem(block, n_tensor)
        return remote(send_mixed.at[block], mixed.at[z * n_ctx + ctx], m_send.at[block],
                      m_recv.at[z * n_ctx + ctx], at(dp, c, t))

    def keep(i):
        return pltpu.make_async_copy(probs.at[:, pl.ds(i * 2 * span, 2 * span)],
                                     probs_out.at[:, pl.ds(i * 2 * span, 2 * span)], p_sem.at[i])

    own_block = ctx * n_tensor + z
    own_mixed = pltpu.make_async_copy(send_mixed.at[own_block], mixed.at[z * n_ctx + ctx], own_sem.at[4])

    def attend(i, carry):
        blocks = pl.ds(2 * i, 2)
        lines = pl.ds(pl.multiple_of(i * 2 * span, 2 * span), 2 * span)
        allowed = seg_col[lines, :] == seg_row[...]
        for h in range(heads):
            q = rows[blocks, :, pl.ds(HEAD_DIM * h, HEAD_DIM)].reshape(2 * span, HEAD_DIM)
            k = rows[:, :, pl.ds(HEAD_DIM * (heads + h), HEAD_DIM)].reshape(total_rows, HEAD_DIM)
            v = rows[:, :, pl.ds(HEAD_DIM * (2 * heads + h), HEAD_DIM)].reshape(total_rows, HEAD_DIM)
            scores = SCALE * lax.dot_general(q, k, (((1,), (1,)), ((), ())), preferred_element_type=F32)
            scores = jnp.where(allowed, scores, NEG)
            weights = jnp.exp(scores - jnp.max(scores, axis=-1, keepdims=True))
            low = (weights * (1.0 / jnp.sum(weights, axis=-1, keepdims=True))).astype(BF16)
            probs[h, lines, :] = low
            value = jnp.dot(low, v, preferred_element_type=F32)
            mixed_float[lines, pl.ds(HEAD_DIM * h, HEAD_DIM)] = value
            send_mixed[blocks, :, pl.ds(HEAD_DIM * h, HEAD_DIM)] = value.astype(BF16).reshape(2, span, HEAD_DIM)
        keep(i).start()
        for n in range(2):
            @pl.when(2 * i + n != own_block)
            def _():
                to_tokens(2 * i + n).start()

            @pl.when(2 * i + n == own_block)
            def _():
                own_mixed.start()

        return carry

    lax.fori_loop(0, n_units, attend, 0)

    def second(j, carry):
        @pl.when((j >= 1) & (j < n_tensor))
        def _():
            for g in (1, 2):
                column(g, near(j))

        @pl.when((j >= 2) & (j < n_tensor))
        def _():
            for g in (1, 2):
                sides(g, near(j - 1))

        return carry

    lax.fori_loop(1, n_tensor, second, 0)

    own_mixed.wait()
    for j in range(n_ctx):
        for k in range(n_tensor):
            if j or k:
                c, t = lax.rem(ctx + j, n_ctx), lax.rem(z + k, n_tensor)
                slot = t * n_ctx + c
                remote(mixed.at[slot], mixed.at[slot], m_send.at[0], m_recv.at[slot], x_dev).wait_recv()

    flip = (((1,), (1,)), ((), ()))
    total[...] = x[...].astype(F32) + vectors[pl.ds(0, 1), :]

    def add_merge(t, carry):
        value = mixed[pl.ds(t * n_ctx, n_ctx)].reshape(count, part_width)
        total[...] += lax.dot_general(value, whole(f0, t)[:, wide:], flip, preferred_element_type=F32)
        return carry

    lax.fori_loop(0, n_tensor, add_merge, 0)
    normal[0], scale[0] = normalize(total[...])
    value = normal[0] * vectors[pl.ds(1, 1), :] + vectors[pl.ds(2, 1), :]
    total[...] = value + vectors[pl.ds(3, 1), :]
    first_low[...] = value.astype(BF16)
    for g in (1, 2):
        own[g].wait()

    def units(t):
        for g in (1, 2):
            partner(g, t)
        bias = gathered(small_all[pl.ds(t * 8, 8), 7, :], e_spread, e_owned)
        before = jnp.dot(first_low[...], whole(f1, t), preferred_element_type=F32) + bias
        value, rise = gelu_exact(before)
        low = value.astype(BF16)
        active[t] = low
        slope[t] = rise
        total[...] += lax.dot_general(low, whole(f2, t), flip, preferred_element_type=F32)

    def third(j, carry):
        @pl.when(j == n_tensor)
        def _():
            for g in (1, 2):
                sides(g, near(j - 1))

        @pl.when(j < n_tensor + 2)
        def _():
            for g in (1, 2):
                corner(g, near(j - 2))

        units(near(j - 3))
        return carry

    lax.fori_loop(3, n_tensor + 3, third, 0)

    normal[1], scale[1] = normalize(total[...])
    gain = vectors[pl.ds(4, 1), :]
    outputs[...] = normal[1] * gain + vectors[pl.ds(5, 1), :]
    pull = cotangent[...].astype(F32)
    small_grads[:, 0, :] = jnp.zeros_like(small_grads[:, 0, :])
    small_grads[:, 5, :] = scattered(total_rows_of(pull * normal[1]), v_spread, v_owned)
    small_grads[:, 6, :] = scattered(total_rows_of(pull), v_spread, v_owned)
    second_grad = normalize_back(pull, normal[1], scale[1], gain)
    small_grads[:, 4, :] = scattered(total_rows_of(second_grad), v_spread, v_owned)
    total[...] = second_grad
    second_low[...] = second_grad.astype(BF16)
    turned[0] = second_low[...].T
    turned[1] = first_low[...].T
    blocked = (2, 2, 2, n_rows, g1.shape[-1])

    def store(which, t):
        grad, out = ((g1, g1_out), (g2, g2_out))[which]
        return pltpu.make_async_copy(grad.at[t], out.at[t], g_sem.at[which, t])

    def units_back(t, carry):
        low = active[t]
        g2[t] = jnp.dot(turned[0], low, preferred_element_type=F32).astype(BF16).reshape(blocked)
        store(1, t).start()
        back = jnp.dot(second_low[...], whole(f2, t), preferred_element_type=F32) * slope[t]
        back_low = back.astype(BF16)
        sums = total_rows_of(back_low.astype(F32))
        small_grads[pl.ds(t * 8, 8), 7, :] = scattered(sums, e_spread, e_owned)
        g1[t] = jnp.dot(turned[1], back_low, preferred_element_type=F32).astype(BF16).reshape(blocked)
        store(0, t).start()
        total[...] += lax.dot_general(back_low, whole(f1, t), flip, preferred_element_type=F32)
        return carry

    lax.fori_loop(0, n_tensor, units_back, 0)
    pull = total[...]
    small_grads[:, 2, :] = scattered(total_rows_of(pull * normal[0]), v_spread, v_owned)
    small_grads[:, 3, :] = scattered(total_rows_of(pull), v_spread, v_owned)
    value = normalize_back(pull, normal[0], scale[0], vectors[pl.ds(1, 1), :])
    small_grads[:, 1, :] = scattered(total_rows_of(value), v_spread, v_owned)
    first_grad[...] = value
    first_low_grad[...] = value.astype(BF16)

    for j in range(n_ctx):
        for k in range(n_tensor):
            if j or k:
                c, t = lax.rem(ctx + j, n_ctx), lax.rem(z + k, n_tensor)
                to_tokens(c * n_tensor + t).wait_send()
                to_heads(t, c).wait_send()
    for i in range(n_units):
        keep(i).wait()

    def finish(origin, carry):
        for g in range(3):
            for kind in range(4):
                core(g, origin, kind, slots[kind]).wait_send()
            along(g, origin, me, x_send, x_recv, x_dev).wait_send()
            along(g, origin, me, y_send, y_recv, y_dev).wait_send()
            part(g, origin, x_slot, 0, a_send, a_recv, y_dev).wait_send()
            part(g, origin, y_slot, half, b_send, b_recv, x_dev).wait_send()

            @pl.when((origin <= z) & up_ok)
            def _():
                up(g, origin).wait_send()

            @pl.when((origin >= z) & down_ok)
            def _():
                down(g, origin).wait_send()
        for which in range(2):
            store(which, origin).wait()
        return carry

    lax.fori_loop(0, n_tensor, finish, 0)


def forward_layer(n_tensor, heads, x, cotangent, triple, merge, w1, shrink, small, matrices, seg_row, seg_col):
    rows, cols = w1.shape
    count, width = x.shape
    n_small = 8 * n_tensor
    blocks = 2 * n_tensor
    span = count // 2
    length = blocks * span
    part = heads * HEAD_DIM
    dma = pltpu.SemaphoreType.DMA
    shape = jax.ShapeDtypeStruct
    full = (n_tensor, 8, rows, cols)
    split = (n_tensor, 2, 2, 2, rows, cols)
    pair = [dma((3, n_tensor)), dma((3, n_tensor))]
    vmem = pl.BlockSpec(memory_space=pltpu.VMEM)
    hbm = pl.BlockSpec(memory_space=pl.ANY)
    return pl.pallas_call(
        functools.partial(forward_kernel, n_tensor, heads),
        out_shape=(
            shape(full, BF16), shape((blocks, span, 3 * part), BF16),
            shape((length, part), F32), shape((heads, length, length), BF16), shape((blocks, span, part), BF16),
            shape((count, width), F32), shape((count, width), BF16), shape((count, width), BF16),
            shape((count, width), F32), shape((n_small,) + small.shape, F32), shape(split, BF16), shape(split, BF16),
        ),
        in_specs=[vmem] * 15,
        out_specs=(vmem, vmem, vmem, hbm) + (vmem,) * 6 + (hbm, hbm),
        scratch_shapes=[
            pltpu.VMEM((rows, cols), BF16),
            pltpu.VMEM((rows, cols), BF16),
            pltpu.VMEM(full, BF16),
            pltpu.VMEM(full, BF16),
            pltpu.VMEM((n_small,) + small.shape, F32),
            pltpu.VMEM((n_tensor, 2, span, 3 * part), BF16),
            pltpu.VMEM((blocks, span, part), BF16),
            pltpu.VMEM((heads, length, length), BF16),
            pltpu.VMEM((8, width), F32),
            pltpu.VMEM((2, count, width), F32),
            pltpu.VMEM((2, count, 1), F32),
            pltpu.VMEM((n_tensor, count, cols), BF16),
            pltpu.VMEM((n_tensor, count, cols), F32),
            pltpu.VMEM((count, width), F32),
            pltpu.VMEM((count, width), BF16),
            pltpu.VMEM((2, width, count), BF16),
            pltpu.VMEM(split, BF16),
            pltpu.VMEM(split, BF16),
            dma((5,)), dma((3, n_tensor)),
        ] + pair * 5 + [
            dma((3, 4, n_tensor)), dma((3, 4, n_tensor)), dma((n_small,)), dma((n_small,)),
            dma((n_tensor, 2)), dma((blocks,)), dma((blocks,)), dma((blocks,)), dma((blocks // 2,)),
            dma((2, n_tensor)),
        ],
        compiler_params=pltpu.CompilerParams(collective_id=0, has_side_effects=True, vmem_limit_bytes=60 << 20),
        cost_estimate=pl.CostEstimate(flops=0, bytes_accessed=w1.size * 400, transcendentals=0),
        name="forward_layer",
    )(x, cotangent, triple, merge, w1, shrink, small, *matrices, seg_row, seg_col)


def far(n_tensor, j):
    return in_order(lambda t, here: (-abs(t - here), t), n_tensor, j)


def sum_steps(n_tensor, grads, acc, core_in, y1_in, x1_in, x2_in, y2_in, up_in, down_in, load_sem, c_send, c_recv,
              y1_send, y1_recv, x1_send, x1_recv, x2_send, x2_recv, y2_send, y2_recv, up_send, up_recv, down_send, down_recv):
    dp, ctx, z = (lax.axis_index(a) for a in ALL)
    rows = acc.shape[-2]
    half = rows // 2
    core = lax.rem(dp, 2)
    x = lax.div(dp, 2)
    xp, yp = 1 - x, 1 - ctx
    x_dev, y_dev, c_dev = at(xp * 2 + core, ctx, z), at(dp, yp, z), at(x * 2 + 1 - core, ctx, z)
    low, high = pl.ds(0, half), pl.ds(half, half)
    count = range(len(grads))

    def load(g, t):
        return pltpu.make_async_copy(grads[g].at[t, :, core], acc.at[g, t], load_sem.at[g, t])

    def to_core(g, t):
        return remote(grads[g].at[t, :, 1 - core], core_in.at[g, t], c_send.at[g, t], c_recv.at[g, t], c_dev)

    def y1(g, t):
        return remote(acc.at[g, t, :, yp, low], y1_in.at[g, t], y1_send.at[g, t], y1_recv.at[g, t], y_dev)

    def x1(g, t):
        return remote(acc.at[g, t, xp, :, high], x1_in.at[g, t], x1_send.at[g, t], x1_recv.at[g, t], x_dev)

    def x2(g, t):
        return remote(acc.at[g, t, xp, ctx, low], x2_in.at[g, t], x2_send.at[g, t], x2_recv.at[g, t], x_dev)

    def y2(g, t):
        return remote(acc.at[g, t, x, yp, high], y2_in.at[g, t], y2_send.at[g, t], y2_recv.at[g, t], y_dev)

    up_dev, down_dev = at(dp, ctx, jnp.minimum(z + 1, n_tensor - 1)), at(dp, ctx, jnp.maximum(z - 1, 0))

    def up(g, t):
        return remote(acc.at[g, t, x, ctx], up_in.at[g, t], up_send.at[g, t], up_recv.at[g, t], up_dev)

    def down(g, t):
        return remote(acc.at[g, t, x, ctx], down_in.at[g, t], down_send.at[g, t], down_recv.at[g, t], down_dev)

    def add(a, b):
        return (a.astype(F32) + b.astype(F32)).astype(BF16)

    def target(j):
        return far(n_tensor, j)

    def begin(j):
        t = target(j)
        for g in count:
            to_core(g, t).start()
            load(g, t).start()

    def core_step(j):
        t = target(j)
        for g in count:
            load(g, t).wait()
            to_core(g, t).wait_recv()
            acc[g, t] = add(acc[g, t], core_in[g, t])
            y1(g, t).start()
            x1(g, t).start()

    def first_step(j):
        t = target(j)
        for g in count:
            y1(g, t).wait_recv()
            for i in range(2):
                acc[g, t, i, ctx, low] = add(acc[g, t, i, ctx, low], y1_in[g, t, i])
            x2(g, t).start()
            x1(g, t).wait_recv()
            for i in range(2):
                acc[g, t, x, i, high] = add(acc[g, t, x, i, high], x1_in[g, t, i])
            y2(g, t).start()

    def second_step(j):
        t = target(j)
        for g in count:
            x2(g, t).wait_recv()
            acc[g, t, x, ctx, low] = add(acc[g, t, x, ctx, low], x2_in[g, t])
            y2(g, t).wait_recv()
            acc[g, t, x, ctx, high] = add(acc[g, t, x, ctx, high], y2_in[g, t])

    def third_step(j):
        t = target(j)
        for g in count:
            @pl.when((t >= z) & (z > 0))
            def _():
                up(g, t).wait_recv()
                acc[g, t, x, ctx] = add(acc[g, t, x, ctx], up_in[g, t])

            @pl.when((t <= z) & (z < n_tensor - 1))
            def _():
                down(g, t).wait_recv()
                acc[g, t, x, ctx] = add(acc[g, t, x, ctx], down_in[g, t])

            @pl.when(t > z)
            def _():
                up(g, t).start()

            @pl.when(t < z)
            def _():
                down(g, t).start()

    def step(j):
        @pl.when(j < n_tensor)
        def _():
            core_step(j)

        @pl.when((j >= 1) & (j < n_tensor + 1))
        def _():
            first_step(j - 1)

        @pl.when((j >= 2) & (j < n_tensor + 2))
        def _():
            second_step(j - 2)

        @pl.when(j >= 3)
        def _():
            third_step(j - 3)

    def end(outs):
        for g in count:
            outs[g][...] = acc[g, z, x, ctx].astype(F32)

        def finish(t, carry):
            for g in count:
                for copy in (to_core, y1, x1, x2, y2):
                    copy(g, t).wait_send()

                @pl.when(t > z)
                def _():
                    up(g, t).wait_send()

                @pl.when(t < z)
                def _():
                    down(g, t).wait_send()
            return carry

        lax.fori_loop(0, n_tensor, finish, 0)

    return begin, step, end


def sum_scratch(n_grads, n_tensor, rows, cols):
    dma = pltpu.SemaphoreType.DMA
    grid = (n_grads, n_tensor)
    half = rows // 2
    return [
        pltpu.VMEM(grid + (2, 2, rows, cols), BF16),
        pltpu.VMEM(grid + (2, 2, rows, cols), BF16),
        pltpu.VMEM(grid + (2, half, cols), BF16),
        pltpu.VMEM(grid + (2, half, cols), BF16),
        pltpu.VMEM(grid + (half, cols), BF16),
        pltpu.VMEM(grid + (half, cols), BF16),
        pltpu.VMEM(grid + (rows, cols), BF16),
        pltpu.VMEM(grid + (rows, cols), BF16),
    ] + [dma(grid)] * 15


def backward_kernel(n_tensor, heads, first_low, first_grad, x, f0, mixed, small, spread, owned, rows, mixed_float,
                    probs_in, g1, g2, input_grad, o0, o1, o2, small_out,
                    turned, g0, mixed_grad, grad, probs, send_rows, qkv_grad, key_sum, value_sum, small_send, small_in,
                    own_sem, g_send, g_recv, q_send, q_recv, p_sem, s_send, s_recv, *scratch):
    dp, ctx, z = (lax.axis_index(a) for a in ALL)
    n_ctx = 2
    n_blocks = n_ctx * n_tensor
    n_units = n_blocks // 2
    span = grad.shape[1]
    part = grad.shape[2]
    wide = 3 * part
    n_rows, width = f0.shape[-2:]
    total_rows = n_blocks * span
    own_block = ctx * n_tensor + z
    own_slot = z * n_ctx + ctx
    mine = z * 8 + dp * 2 + ctx
    peers = everyone(4, 2, n_tensor)
    greet([at(*p) for p in peers])
    others = [(lax.rem(ctx + j, n_ctx), lax.rem(z + k, n_tensor))
              for k in (2, 3, 1, 0) for j in range(n_ctx) if (j or k) and k < n_tensor]
    half = len(scratch) // 2
    begin, step, end = sum_steps(n_tensor, (g1, g2), *scratch[:half])
    begin_last, step_last, end_last = sum_steps(n_tensor, (g0,), *scratch[half:])

    def to_heads(c, t):
        return remote(mixed_grad.at[t * n_ctx + c], grad.at[own_block], g_send.at[t * n_ctx + c],
                      g_recv.at[own_block], at(dp, c, t))

    def load(i):
        lines = pl.ds(i * 2 * span, 2 * span)
        return pltpu.make_async_copy(probs_in.at[:, lines], probs.at[:, lines], p_sem.at[i])

    here = pltpu.make_async_copy(mixed_grad.at[own_slot], grad.at[own_block], own_sem.at[0])

    def begin_all(j, carry):
        begin(j)
        return carry

    lax.fori_loop(0, n_tensor, begin_all, 0)

    def spread_grad(j, carry):
        t = far(n_tensor, j)
        weight = f0[t].reshape(8 * n_rows, width)[:, wide:]
        value = jnp.dot(first_low[...], weight, preferred_element_type=F32).astype(BF16)
        mixed_grad[pl.ds(t * n_ctx, n_ctx)] = value.reshape(n_ctx, span, part)
        to_heads(1 - ctx, t).start()

        @pl.when(t != z)
        def _():
            to_heads(ctx, t).start()

        @pl.when(t == z)
        def _():
            here.start()

        return carry

    lax.fori_loop(0, n_tensor, spread_grad, 0)
    for i in range(n_units):
        load(i).start()
    turned[0] = first_low[...].T
    turned[1] = x[...].T
    small_send[...] = small[...]

    def merge_grad(t, carry):
        value = jnp.dot(turned[0], mixed[pl.ds(t * n_ctx, n_ctx)].reshape(n_ctx * span, part),
                        preferred_element_type=F32)
        g0[t, :, :, :, :, pl.ds(wide, part)] = value.astype(BF16).reshape(2, 2, 2, n_rows, part)
        return carry

    lax.fori_loop(0, n_tensor, merge_grad, 0)
    step(0)
    step(1)
    here.wait()
    for c, t in others:
        block = c * n_tensor + t
        remote(grad.at[block], grad.at[block], g_send.at[0], g_recv.at[block], at(dp, c, t)).wait_recv()
    for i in range(n_units):
        load(i).wait()

    def one_head(h):
        lanes = pl.ds(HEAD_DIM * h, HEAD_DIM)
        k_lanes = pl.ds(HEAD_DIM * (heads + h), HEAD_DIM)
        v_lanes = pl.ds(HEAD_DIM * (2 * heads + h), HEAD_DIM)
        key_sum[...] = jnp.zeros_like(key_sum)
        value_sum[...] = jnp.zeros_like(value_sum)

        def unit(i, carry):
            blocks = pl.ds(2 * i, 2)
            lines = pl.ds(pl.multiple_of(i * 2 * span, 2 * span), 2 * span)
            q = rows[blocks, :, lanes].reshape(2 * span, HEAD_DIM)
            k = rows[:, :, k_lanes].reshape(total_rows, HEAD_DIM)
            v = rows[:, :, v_lanes].reshape(total_rows, HEAD_DIM)
            up = grad[blocks, :, lanes].reshape(2 * span, HEAD_DIM)
            low = probs[h, lines, :]
            delta = jnp.sum(up.astype(F32) * mixed_float[lines, lanes], axis=-1, keepdims=True)
            pull = lax.dot_general(up, v, (((1,), (1,)), ((), ())), preferred_element_type=F32)
            score = (low.astype(F32) * (pull - delta)).astype(BF16)
            query = SCALE * jnp.dot(score, k, preferred_element_type=F32)
            send_rows[blocks, :, lanes] = query.astype(BF16).reshape(2, span, HEAD_DIM)
            key_sum[...] += lax.dot_general(q, score, (((0,), (0,)), ((), ())), preferred_element_type=F32)
            value_sum[...] += lax.dot_general(up, low, (((0,), (0,)), ((), ())), preferred_element_type=F32)
            return carry

        lax.fori_loop(0, n_units, unit, 0)
        key = (SCALE * key_sum[...]).T.astype(BF16)
        value = value_sum[...].T.astype(BF16)
        send_rows[:, :, k_lanes] = key.reshape(n_blocks, span, HEAD_DIM)
        send_rows[:, :, v_lanes] = value.reshape(n_blocks, span, HEAD_DIM)

    for h in range(heads):
        one_head(h)
        if h < 2:
            step(h + 2)

    def to_tokens(c, t):
        return remote(send_rows.at[c * n_tensor + t], qkv_grad.at[own_slot], q_send.at[c * n_tensor + t],
                      q_recv.at[own_slot], at(dp, c, t))

    there = pltpu.make_async_copy(send_rows.at[own_block], qkv_grad.at[own_slot], own_sem.at[1])

    def send_back(j, carry):
        t = far(n_tensor, j)
        to_tokens(1 - ctx, t).start()

        @pl.when(t != z)
        def _():
            to_tokens(ctx, t).start()

        @pl.when(t == z)
        def _():
            there.start()

        return carry

    lax.fori_loop(0, n_tensor, send_back, 0)

    def one(j, carry):
        step(j)
        return carry

    lax.fori_loop(2 + min(heads, 2), n_tensor + 3, one, 0)

    def arrived(t, c):
        slot = t * n_ctx + c
        remote(qkv_grad.at[slot], qkv_grad.at[slot], q_send.at[0], q_recv.at[slot], at(dp, c, t)).wait_recv()

    def weight_grad(j):
        t = far(n_tensor, j)
        arrived(t, 1 - ctx)

        @pl.when(t != z)
        def _():
            arrived(t, ctx)

        @pl.when(t == z)
        def _():
            there.wait()

        pull = qkv_grad[pl.ds(t * n_ctx, n_ctx)].reshape(n_ctx * span, wide)
        value = jnp.dot(turned[1], pull, preferred_element_type=F32)
        g0[t, :, :, :, :, pl.ds(0, wide)] = value.astype(BF16).reshape(2, 2, 2, n_rows, wide)
        begin_last(j)
        small_send[pl.ds(t * 8, 8), 0, :] = scattered(total_rows_of(pull.astype(F32)), spread, owned)

    def weight_grads(j, carry):
        @pl.when(j < n_tensor)
        def _():
            weight_grad(j)

        @pl.when(j >= 1)
        def _():
            step_last(j - 1)

        return carry

    lax.fori_loop(0, n_tensor + 1, weight_grads, 0)
    small_copies = [
        remote(small_send.at[pt * 8 + pd * 2 + pc], small_in.at[n], s_send.at[n], s_recv.at[n], at(pd, pc, pt))
        for n, (pd, pc, pt) in enumerate(peers)
    ]
    for copy in small_copies:
        copy.start()
    input_grad[...] = first_grad[...]

    def add_input(j):
        pull = qkv_grad[pl.ds(j * n_ctx, n_ctx)].reshape(n_ctx * span, wide)
        weight = f0[j].reshape(8 * n_rows, width)[:, :wide]
        input_grad[...] += lax.dot_general(pull, weight, (((1,), (1,)), ((), ())), preferred_element_type=F32)

    for j in range(n_tensor):
        if j < 3:
            step_last(n_tensor + j)
        add_input(j)
    end((o1, o2))
    end_last((o0,))
    total = small_send[mine]
    for n in range(len(peers)):
        small_copies[n].wait()
        total = total + small_in[n]
    small_out[...] = total
    for c, t in others:
        to_tokens(c, t).wait_send()
        to_heads(c, t).wait_send()


def backward_attention(n_tensor, heads, first_low, first_grad, x, f0, mixed, small, spread, owned, rows, mixed_float,
                       probs, g1, g2):
    blocks, span, wide = rows.shape
    part = heads * HEAD_DIM
    length = blocks * span
    n_rows, cols = g1.shape[-2:]
    n_small = 8 * n_tensor
    dma = pltpu.SemaphoreType.DMA
    vmem = pl.BlockSpec(memory_space=pltpu.VMEM)
    hbm = pl.BlockSpec(memory_space=pl.ANY)
    shape = jax.ShapeDtypeStruct
    out = shape((n_rows, cols), F32)
    return pl.pallas_call(
        functools.partial(backward_kernel, n_tensor, heads),
        out_shape=(shape(first_grad.shape, F32), out, out, out, shape(small.shape[1:], F32)),
        in_specs=[vmem] * 10 + [hbm] * 3,
        out_specs=(vmem,) * 5,
        scratch_shapes=[
            pltpu.VMEM((2,) + x.shape[::-1], BF16),
            pltpu.VMEM(g1.shape, BF16),
            pltpu.VMEM((blocks, span, part), BF16),
            pltpu.VMEM((blocks, span, part), BF16),
            pltpu.VMEM((heads, length, length), BF16),
            pltpu.VMEM((blocks, span, wide), BF16),
            pltpu.VMEM((blocks, span, wide), BF16),
            pltpu.VMEM((HEAD_DIM, length), F32),
            pltpu.VMEM((HEAD_DIM, length), F32),
            pltpu.VMEM(small.shape, F32),
            pltpu.VMEM((n_small - 1,) + small.shape[1:], F32),
            dma((2,)), dma((blocks,)), dma((blocks,)), dma((blocks,)), dma((blocks,)), dma((blocks // 2,)),
            dma((n_small - 1,)), dma((n_small - 1,)),
        ] + sum_scratch(2, n_tensor, n_rows, cols) + sum_scratch(1, n_tensor, n_rows, cols),
        compiler_params=pltpu.CompilerParams(collective_id=2, has_side_effects=True, vmem_limit_bytes=58 << 20),
        cost_estimate=pl.CostEstimate(flops=0, bytes_accessed=g1.size * 24, transcendentals=0),
        name="backward_attention",
    )(first_low, first_grad, x, f0, mixed, small, spread, owned, rows, mixed_float, probs, g1, g2)


def norm_rows(total, gain, shift):
    center = total - jnp.mean(total, axis=-1, keepdims=True)
    spread = jnp.mean(center * center, axis=-1, keepdims=True)
    return center * lax.rsqrt(spread + EPS) * gain + shift


def gelu_exact(before):
    share = 0.5 + 0.5 * lax.erf(before * 0.5**0.5)
    dense = (0.5 / np.pi) ** 0.5 * jnp.exp(-0.5 * before * before)
    return before * share, share + before * dense


def dot(spec, a, b):
    return jnp.einsum(spec, a, b, preferred_element_type=F32)


def add_up(spec, a, b):
    return sum(dot(spec, a[t], b[t]) for t in range(a.shape[0]))


def local(
    inputs,
    cotangent,
    segments,
    triple_weight,
    attend_bias,
    merge_weight,
    merge_bias,
    first_gain,
    first_shift,
    expand_weight,
    expand_bias,
    shrink_weight,
    shrink_bias,
    second_gain,
    second_shift,
):
    n_dp, n_ctx, n_tensor = (lax.axis_size(a) for a in ALL)
    span, batch, width = inputs.shape
    rows = triple_weight.shape[1]
    part = triple_weight.shape[2]
    units = expand_weight.shape[1]
    owners = n_dp * n_ctx
    heads = part // HEAD_DIM
    count = batch * span
    small_part = part // owners
    unit_part = units // owners
    own_kernels = n_dp == 4 and n_ctx == 2 and batch == 2 and n_tensor == 4 and rows % 32 == 0

    narrow_in = (merge_bias, first_gain, first_shift, shrink_bias, second_gain, second_shift)
    x_low = jnp.transpose(inputs, (1, 0, 2)).reshape(count, width)
    cotangent_rows = jnp.transpose(cotangent, (1, 0, 2)).reshape(count, width)
    here = lax.axis_index("ctx")
    if own_kernels:
        labels = lax.dynamic_slice_in_dim(segments, here, 1, 0)
        lines = [attend_bias.reshape(1, -1)] + list(narrow_in) + [expand_bias]
        small = sum(
            jnp.pad(v.astype(F32), ((n, 7 - n), (0, 128 - v.shape[1]))) for n, v in enumerate(lines)
        )
        matrices = tables(n_tensor, owners, part, units)
        (f0, rows_all, mixed_float, probs, mixed, outputs_rows, first_low, first_low_grad, first_grad, small_grads,
         expand_grad, shrink_grad) = forward_layer(
            n_tensor, heads, x_low, cotangent_rows, triple_weight, merge_weight, expand_weight, shrink_weight, small,
            matrices, labels, labels.reshape(-1, 1)
        )
        inputs_gradient, r0, r1, r2, small_sum = backward_attention(
            n_tensor, heads, first_low_grad, first_grad, x_low, f0, mixed, small_grads, *matrices[:2],
            rows_all, mixed_float, probs, expand_grad, shrink_grad
        )
        narrow_out = [small_sum[:1, :small_part], small_sum[:1, small_part : 2 * small_part]]
        narrow_out += [small_sum[n : n + 1, :small_part] for n in range(1, 7)]
        expand_out = small_sum[7:, :unit_part]
    else:
        pieces = [attend_bias[0, 0], attend_bias[1, 0]] + [v[0] for v in narrow_in] + [expand_bias[0]]
        w0 = jnp.concatenate(
            [jnp.transpose(triple_weight, (1, 0, 2)).reshape(rows, 3 * part), merge_weight.T], axis=1
        )
        small = jnp.concatenate(pieces).astype(F32)
        f0, f1, f2 = (
            lax.all_gather(lax.all_gather(w, ("dp", "ctx"), axis=0, tiled=True), "tensor", axis=0, tiled=False)
            for w in (w0, expand_weight, shrink_weight.T)
        )
        small_all = lax.all_gather(lax.all_gather(small, ("dp", "ctx")), "tensor")
        f0, w_expand, w_shrink = (w.reshape(n_tensor, width, -1) for w in (f0, f1, f2))
        w_qkv, w_merge = f0[:, :, : 3 * part], f0[:, :, 3 * part :]
        narrow = small_all[:, :, : 8 * small_part].reshape(n_tensor, owners, 8, small_part)
        narrow = jnp.transpose(narrow, (2, 0, 1, 3)).reshape(8, n_tensor, part)
        merge_vec, gain_one, shift_one, shrink_vec, gain_two, shift_two = narrow[2:].reshape(6, width)
        expand_vec = small_all[:, :, 8 * small_part :].reshape(n_tensor, 1, units)
        qkv_vec = jnp.concatenate([narrow[0], jnp.zeros_like(narrow[0]), narrow[1]], axis=-1)[:, None]
        x = x_low.astype(F32)
        upstream = cotangent_rows.astype(F32)

        def to_tokens(value):
            value = value.reshape(batch, n_tensor, span, -1)
            out = lax.all_to_all(jnp.transpose(value, (1, 0, 2, 3)), "tensor", split_axis=0, concat_axis=0)
            return out.reshape(n_tensor, count, -1)

        qkv = (dot("rd,tde->tre", x_low, w_qkv) + qkv_vec).astype(BF16)
        mine = lax.all_to_all(
            qkv.reshape(n_tensor, batch, span, 3 * part), "tensor", split_axis=0, concat_axis=0
        )
        mine = jnp.transpose(mine, (1, 0, 2, 3)).reshape(batch, n_tensor * span, 3 * part)
        n_query = n_tensor * span
        own_labels = lax.dynamic_slice_in_dim(segments, here * n_query, n_query, 1)
        kv_rows = lax.all_gather(mine[..., part:], "ctx", axis=1, tiled=True)
        n_key = kv_rows.shape[1]
        q_four = mine[..., :part].reshape(batch, n_query, heads, HEAD_DIM)
        k_four = kv_rows[..., :part].reshape(batch, n_key, heads, HEAD_DIM)
        v_four = kv_rows[..., part:].reshape(batch, n_key, heads, HEAD_DIM)
        allowed = own_labels[:, None, :, None] == segments[:, None, None, :]
        scores = jnp.where(allowed, SCALE * dot("sqhd,skhd->shqk", q_four, k_four), NEG)
        top = jnp.max(scores, axis=-1)
        weights = jnp.where(allowed, jnp.exp(scores - top[..., None]), 0.0)
        total = jnp.sum(weights, axis=-1)
        mixed_float = dot("shqk,skhd->shqd", weights.astype(BF16), v_four) / total[..., None]
        logsum = top + jnp.log(total)
        mixed = to_tokens(jnp.transpose(mixed_float, (0, 2, 1, 3)).reshape(batch, n_query, part).astype(BF16))
        first_sum = x + add_up("re,de->rd", mixed, w_merge) + merge_vec
        first_norm = norm_rows(first_sum, gain_one, shift_one)
        first_low = first_norm.astype(BF16)
        before = dot("rd,tdf->trf", first_low, w_expand) + expand_vec
        active, slope = gelu_exact(before)
        active = active.astype(BF16)
        second_sum = first_norm + add_up("rf,df->rd", active, w_shrink) + shrink_vec
        outputs_rows = norm_rows(second_sum, gain_two, shift_two)

        second_grad, gain_two_grad, shift_two_grad = jax.vjp(norm_rows, second_sum, gain_two, shift_two)[1](upstream)
        shrink_vec_grad = jnp.sum(second_grad, axis=0)
        second_low = second_grad.astype(BF16)
        shrink_grad = dot("rd,trf->tdf", second_low, active).astype(BF16)
        active_grad = dot("rd,tdf->trf", second_low, w_shrink)
        before_low = (active_grad * slope).astype(BF16)
        expand_vec_grad = jnp.sum(before_low.astype(F32), axis=1)
        expand_grad = dot("rd,trf->tdf", first_low, before_low).astype(BF16)
        norm_back = add_up("rf,df->rd", before_low, w_expand)
        first_grad, gain_one_grad, shift_one_grad = jax.vjp(norm_rows, first_sum, gain_one, shift_one)[1](
            second_grad + norm_back
        )
        merge_vec_grad = jnp.sum(first_grad, axis=0)
        first_low_grad = first_grad.astype(BF16)
        vec_grads = jnp.stack(
            [merge_vec_grad, gain_one_grad, shift_one_grad, shrink_vec_grad, gain_two_grad, shift_two_grad]
        ).reshape(6, n_tensor, owners, small_part)
        vec_grads = jnp.transpose(vec_grads, (1, 2, 0, 3)).reshape(n_tensor, owners, 6 * small_part)
        small_grads = jnp.concatenate([vec_grads, expand_vec_grad.reshape(n_tensor, owners, unit_part)], axis=-1)
        merge_grad = dot("rd,tre->tde", first_low_grad, mixed).astype(BF16)
        mixed_grad = dot("rd,tde->tre", first_low_grad, w_merge).astype(BF16)
        grad_rows = lax.all_to_all(
            mixed_grad.reshape(n_tensor, batch, span, part), "tensor", split_axis=0, concat_axis=0
        )
        grad_four = jnp.transpose(grad_rows, (1, 0, 2, 3)).reshape(batch, n_query, heads, HEAD_DIM)
        delta = jnp.sum(jnp.transpose(grad_four.astype(F32), (0, 2, 1, 3)) * mixed_float, axis=-1)
        back_scores = SCALE * dot("sqhd,skhd->shqk", q_four, k_four)
        probs = jnp.where(allowed, jnp.exp(back_scores - logsum[..., None]), 0.0)
        prob_grad = dot("sqhd,skhd->shqk", grad_four, v_four)
        score_low = (probs * (prob_grad - delta[..., None])).astype(BF16)
        value_part = dot("shqk,sqhd->skhd", probs.astype(BF16), grad_four)
        query_part = SCALE * dot("shqk,skhd->sqhd", score_low, k_four)
        key_part = SCALE * dot("shqk,sqhd->skhd", score_low, q_four)
        query_part, key_part, value_part = (
            v.reshape(batch, -1, part).astype(BF16) for v in (query_part, key_part, value_part)
        )
        key_part, value_part = (
            lax.psum_scatter(v, "ctx", scatter_dimension=1, tiled=True) for v in (key_part, value_part)
        )
        qkv_grad = to_tokens(jnp.concatenate([query_part, key_part, value_part], axis=-1))
        triple_grad = dot("rd,tre->tde", x_low, qkv_grad).astype(BF16)
        attend_grad = jnp.sum(qkv_grad.astype(F32), axis=1).reshape(n_tensor, 3, owners, small_part)
        inputs_gradient = first_grad + add_up("re,de->rd", qkv_grad, w_qkv)
        small_grads = jnp.concatenate([attend_grad[:, 0], attend_grad[:, 2], small_grads], axis=-1)
        grads = (jnp.concatenate([triple_grad, merge_grad], axis=-1), expand_grad, shrink_grad)
        r0, r1, r2 = (
            lax.psum_scatter(
                lax.psum_scatter(g, "tensor", scatter_dimension=0), ("dp", "ctx"), scatter_dimension=0, tiled=True
            ).astype(F32)
            for g in grads
        )
        small_sum = lax.psum_scatter(
            lax.psum_scatter(small_grads, "tensor", scatter_dimension=0), ("dp", "ctx"), scatter_dimension=0
        )
        narrow_out = list(small_sum[: 8 * small_part].reshape(8, 1, small_part))
        expand_out = small_sum[8 * small_part :].reshape(1, unit_part)
    triple_out = jnp.transpose(r0[:, : 3 * part].reshape(rows, 3, part), (1, 0, 2))
    outputs_rows, inputs_gradient = (
        jnp.transpose(v.reshape(batch, span, width), (1, 0, 2)) for v in (outputs_rows, inputs_gradient)
    )
    return (
        outputs_rows,
        inputs_gradient,
        triple_out,
        jnp.stack(narrow_out[:2]),
        r0[:, 3 * part :].T,
        narrow_out[2],
        narrow_out[3],
        narrow_out[4],
        r1,
        expand_out,
        r2.T,
        narrow_out[5],
        narrow_out[6],
        narrow_out[7],
    )


def solution(mesh):
    in_specs = (
        P(("ctx", "tensor"), "dp", None),
        P(("ctx", "tensor"), "dp", None),
        P("dp", None),
        P(None, ("dp", "ctx"), "tensor"),
        P(None, "tensor", ("dp", "ctx")),
        P("tensor", ("dp", "ctx")),
        P("tensor", ("dp", "ctx")),
        P("tensor", ("dp", "ctx")),
        P("tensor", ("dp", "ctx")),
        P(("dp", "ctx"), "tensor"),
        P("tensor", ("dp", "ctx")),
        P("tensor", ("dp", "ctx")),
        P("tensor", ("dp", "ctx")),
        P("tensor", ("dp", "ctx")),
        P("tensor", ("dp", "ctx")),
    )
    out_specs = (
        P(("ctx", "tensor"), "dp", None),
        P(("ctx", "tensor"), "dp", None),
        P(None, ("dp", "ctx"), "tensor"),
        P(None, "tensor", ("dp", "ctx")),
        P("tensor", ("dp", "ctx")),
        P("tensor", ("dp", "ctx")),
        P("tensor", ("dp", "ctx")),
        P("tensor", ("dp", "ctx")),
        P(("dp", "ctx"), "tensor"),
        P("tensor", ("dp", "ctx")),
        P("tensor", ("dp", "ctx")),
        P("tensor", ("dp", "ctx")),
        P("tensor", ("dp", "ctx")),
        P("tensor", ("dp", "ctx")),
    )
    return jax.shard_map(local, mesh=mesh, in_specs=in_specs, out_specs=out_specs, check_vma=False)
```

```python
import functools

import jax
import jax.numpy as jnp
import numpy as np
from jax import lax
from jax.experimental import pallas as pl
from jax.experimental.pallas import tpu as pltpu
from jax.sharding import PartitionSpec as P

HEAD_DIM = 64

EPS = 1e-12
NEG = -1e30
SCALE = 0.125
MESH = pl.DeviceIdType.MESH
BF16 = jnp.bfloat16
F32 = jnp.float32
ALL = ("dp", "ctx", "tensor")
TOKENS = ("ctx", "tensor")


def at(dp, ctx, tensor):
    return {"dp": dp, "ctx": ctx, "tensor": tensor}


def remote(src, dst, send, recv, where):
    return pltpu.make_async_remote_copy(
        src_ref=src, dst_ref=dst, send_sem=send, recv_sem=recv, device_id=where, device_id_type=MESH
    )


def greet(peers):
    barrier = pltpu.get_barrier_semaphore()
    for peer in peers:
        pl.semaphore_signal(barrier, inc=1, device_id=peer, device_id_type=MESH)
    pl.semaphore_wait(barrier, len(peers))


def everyone(n_dp, n_ctx, n_tensor):
    dp, ctx, tensor = (lax.axis_index(a) for a in ALL)
    peers = []
    for i in range(n_dp):
        for j in range(n_ctx):
            for k in range(n_tensor):
                if i or j or k:
                    peers.append(
                        (lax.rem(dp + i, n_dp), lax.rem(ctx + j, n_ctx), lax.rem(tensor + k, n_tensor))
                    )
    return peers


def in_order(key, n_tensor, j):
    z = lax.axis_index("tensor")
    found = 0
    for here in range(n_tensor):
        for n, there in enumerate(sorted(range(n_tensor), key=lambda t: key(t, here))):
            found = found + jnp.where((z == here) & (j == n), there, 0)
    return found


def one_hot(n_lanes, owners, picks, width):
    spread = np.zeros((n_lanes, width), np.float32)
    owned = np.zeros((owners, width), np.float32)
    for feature, (lane, owner) in picks.items():
        spread[lane, feature] = 1.0
        owned[owner, feature] = 1.0
    return jnp.asarray(spread, BF16), jnp.asarray(owned)


def tables(n_tensor, owners, part, units):
    piece, unit = part // owners, units // owners
    attend = {n: (n % piece, n // piece) for n in range(part)}
    attend.update({2 * part + n: (piece + n % piece, n // piece) for n in range(part)})
    whole = {t * part + n: (n % piece, t * owners + n // piece) for t in range(n_tensor) for n in range(part)}
    expand = {n: (n % unit, n // unit) for n in range(units)}
    return (
        one_hot(128, owners, attend, 3 * part)
        + one_hot(128, n_tensor * owners, whole, n_tensor * part)
        + one_hot(128, owners, expand, units)
    )


def gathered(pieces, spread, owned):
    value = jnp.dot(pieces.astype(BF16), spread[...], preferred_element_type=F32)
    return jnp.sum(value * owned[...], axis=0, keepdims=True)


def scattered(vector, spread, owned):
    total = vector * owned[...]
    upper = total.astype(BF16)
    lower = (total - upper.astype(F32)).astype(BF16)
    flip = (((1,), (1,)), ((), ()))
    return lax.dot_general(upper, spread[...], flip, preferred_element_type=F32) + lax.dot_general(
        lower, spread[...], flip, preferred_element_type=F32
    )


def normalize(total):
    center = total - jnp.mean(total, axis=-1, keepdims=True)
    spread = jnp.mean(center * center, axis=-1, keepdims=True)
    scale = lax.rsqrt(spread + EPS)
    return center * scale, scale


def normalize_back(up, normal, scale, gain):
    pull = up * gain
    return scale * (
        pull - jnp.mean(pull, axis=-1, keepdims=True) - normal * jnp.mean(pull * normal, axis=-1, keepdims=True)
    )


def total_rows_of(value):
    return jnp.sum(value, axis=0, keepdims=True)


def forward_kernel(n_tensor, heads, x, cotangent, triple, merge, w1, shrink, small, a_spread, a_owned, v_spread,
                   v_owned, e_spread, e_owned, seg_row, seg_col,
                   f0, rows, mixed_float, probs_out, mixed, outputs, first_low, first_low_grad, first_grad,
                   small_grads, g1_out, g2_out,
                   w0, w2, f1, f2, small_all, send_rows, send_mixed, probs, vectors, normal, scale, active, slope,
                   total, second_low, turned, g1, g2,
                   own_sem, z_up, z_down, z_recv, x_send, x_recv, y_send, y_recv, a_send, a_recv, b_send, b_recv,
                   c_send, c_recv, s_send, s_recv, q_send, q_recv, m_send, m_recv, p_sem, g_sem):
    shards, outs = (w0, w1, w2), (f0, f1, f2)
    dp, ctx, z = (lax.axis_index(a) for a in ALL)
    n_ctx = 2
    n_rows = w0.shape[0]
    half = n_rows // 2
    xp = lax.rem(dp + 2, 4)
    cp = dp + 1 - 2 * lax.rem(dp, 2)
    yp = 1 - ctx
    xcp = lax.rem(cp + 2, 4)
    me = dp * 2 + ctx
    mine = z * 8 + me
    peers = everyone(4, 2, n_tensor)
    wide = a_spread.shape[1]
    part_width = wide // 3
    for i in range(3):
        w0[:, pl.ds(i * part_width, part_width)] = triple[i]
    w0[:, pl.ds(wide, merge.shape[0])] = merge[...].T
    w2[...] = shrink[...].T
    greet([at(*p) for p in peers])
    x_dev, y_dev, c_dev = at(xp, ctx, z), at(dp, yp, z), at(cp, ctx, z)
    x_slot, y_slot, d_slot = xp * 2 + ctx, dp * 2 + yp, xp * 2 + yp
    slots = (cp * 2 + ctx, xcp * 2 + ctx, cp * 2 + yp, xcp * 2 + yp)
    up_ok, down_ok = z < n_tensor - 1, z > 0

    def near(j):
        middle = (n_tensor - 1) / 2
        return in_order(lambda t, here: (abs(t - here), abs(t - middle)), n_tensor, j)

    def up(g, origin, src=None):
        block = outs[g].at[origin, me]
        return remote(block if src is None else src, block, z_up.at[g, origin], z_recv.at[g, origin],
                      at(dp, ctx, jnp.minimum(z + 1, n_tensor - 1)))

    def down(g, origin, src=None):
        block = outs[g].at[origin, me]
        return remote(block if src is None else src, block, z_down.at[g, origin], z_recv.at[g, origin],
                      at(dp, ctx, jnp.maximum(z - 1, 0)))

    def from_z(g, origin):
        block = outs[g].at[origin, me]
        return remote(block, block, z_up.at[g, origin], z_recv.at[g, origin], x_dev)

    def along(g, origin, slot, send, recv, dev, src=None):
        block = outs[g].at[origin, slot]
        return remote(block if src is None else src, block, send.at[g, origin], recv.at[g, origin], dev)

    def part(g, origin, slot, lo, send, recv, dev):
        block = outs[g].at[origin, slot, pl.ds(lo, half)]
        return remote(block, block, send.at[g, origin], recv.at[g, origin], dev)

    def core(g, origin, kind, slot, src=None):
        block = outs[g].at[origin, slot]
        return remote(
            block if src is None else src, block, c_send.at[g, kind, origin], c_recv.at[g, kind, origin], c_dev
        )

    own = [pltpu.make_async_copy(shards[g], outs[g].at[z, me], own_sem.at[g]) for g in range(3)]

    def begin(g):
        @pl.when(up_ok)
        def _():
            up(g, z, shards[g]).start()

        @pl.when(down_ok)
        def _():
            down(g, z, shards[g]).start()

        along(g, z, me, x_send, x_recv, x_dev, shards[g]).start()
        along(g, z, me, y_send, y_recv, y_dev, shards[g]).start()
        core(g, z, 0, me, shards[g]).start()
        own[g].start()

    def column(g, origin):
        from_z(g, origin).wait_recv()

        @pl.when((origin < z) & up_ok)
        def _():
            up(g, origin).start()

        @pl.when((origin > z) & down_ok)
        def _():
            down(g, origin).start()

        along(g, origin, me, x_send, x_recv, x_dev).start()
        along(g, origin, me, y_send, y_recv, y_dev).start()
        core(g, origin, 0, me).start()

    def sides(g, origin):
        along(g, origin, x_slot, x_send, x_recv, x_dev).wait_recv()
        part(g, origin, x_slot, 0, a_send, a_recv, y_dev).start()
        core(g, origin, 1, x_slot).start()
        along(g, origin, y_slot, y_send, y_recv, y_dev).wait_recv()
        part(g, origin, y_slot, half, b_send, b_recv, x_dev).start()
        core(g, origin, 2, y_slot).start()

    def corner(g, origin):
        part(g, origin, d_slot, 0, a_send, a_recv, y_dev).wait_recv()
        part(g, origin, d_slot, half, b_send, b_recv, x_dev).wait_recv()
        core(g, origin, 3, d_slot).start()

    def partner(g, origin):
        for kind in range(4):
            core(g, origin, kind, slots[kind]).wait_recv()

    begin(0)
    small_own = pltpu.make_async_copy(small, small_all.at[mine], s_send.at[0])
    small_own.start()
    for n, p in enumerate(peers):
        remote(small, small_all.at[mine], s_send.at[n + 1], s_recv.at[n], at(*p)).start()

    def to_heads(t, c):
        return remote(send_rows.at[t, c], rows.at[ctx * n_tensor + z], q_send.at[t, c],
                      q_recv.at[ctx * n_tensor + z], at(dp, c, t))

    def from_token(block):
        return remote(rows.at[block], rows.at[block], q_send.at[0, 0], q_recv.at[block], x_dev)

    count = x.shape[0]
    span = count // n_ctx
    width = x.shape[1]
    here = pltpu.make_async_copy(send_rows.at[z, ctx], rows.at[ctx * n_tensor + z], own_sem.at[3])

    def whole(ref, t):
        return ref[t].reshape(8 * n_rows, ref.shape[-1])

    def project(t):
        partner(0, t)
        bias = gathered(small_all[pl.ds(t * 8, 8), 0, :], a_spread, a_owned)
        value = jnp.dot(x[...], whole(f0, t), preferred_element_type=F32)[:, :wide] + bias
        send_rows[t] = value.astype(BF16).reshape(n_ctx, span, wide)
        to_heads(t, yp).start()

        @pl.when(t != z)
        def _():
            to_heads(t, ctx).start()

        @pl.when(t == z)
        def _():
            here.start()

    def first(j, carry):
        @pl.when(j < n_tensor - 1)
        def _():
            column(0, near(j + 1))

        @pl.when(j < n_tensor)
        def _():
            sides(0, near(j))

        @pl.when(j == n_tensor - 1)
        def _():
            for g in (1, 2):
                begin(g)

        @pl.when(j >= 1)
        def _():
            corner(0, near(j - 1))

        @pl.when(j == 1)
        def _():
            own[0].wait()
            small_own.wait()
            for n, p in enumerate(peers):
                copy = remote(small, small_all.at[mine], s_send.at[n + 1], s_recv.at[n], at(*p))
                copy.wait_send()
                copy.wait_recv()

        @pl.when(j >= 1)
        def _():
            project(near(j - 1))

        return carry

    lax.fori_loop(0, n_tensor + 1, first, 0)
    for k in range(6):
        vectors[pl.ds(k, 1), :] = gathered(small_all[:, k + 1, :], v_spread, v_owned)

    def second(j, carry):
        @pl.when(j < n_tensor - 1)
        def _():
            for g in (1, 2):
                column(g, near(j + 1))

        @pl.when(j < n_tensor - 1)
        def _():
            for g in (1, 2):
                sides(g, near(j))

        @pl.when((j >= 1) & (j < n_tensor - 1))
        def _():
            for g in (1, 2):
                corner(g, near(j - 1))

        return carry

    lax.fori_loop(0, n_tensor - 1, second, 0)
    here.wait()
    for j in range(n_ctx):
        for k in range(n_tensor):
            if j or k:
                from_token(lax.rem(ctx + j, n_ctx) * n_tensor + lax.rem(z + k, n_tensor)).wait_recv()

    n_blocks = n_ctx * n_tensor
    total_rows = n_blocks * span
    n_units = n_blocks // 2

    def to_tokens(block):
        c, t = lax.div(block, n_tensor), lax.rem(block, n_tensor)
        return remote(send_mixed.at[block], mixed.at[z * n_ctx + ctx], m_send.at[block],
                      m_recv.at[z * n_ctx + ctx], at(dp, c, t))

    def keep(i):
        return pltpu.make_async_copy(probs.at[:, pl.ds(i * 2 * span, 2 * span)],
                                     probs_out.at[:, pl.ds(i * 2 * span, 2 * span)], p_sem.at[i])

    own_block = ctx * n_tensor + z
    own_mixed = pltpu.make_async_copy(send_mixed.at[own_block], mixed.at[z * n_ctx + ctx], own_sem.at[4])

    def attend(i, carry):
        blocks = pl.ds(2 * i, 2)
        lines = pl.ds(pl.multiple_of(i * 2 * span, 2 * span), 2 * span)
        allowed = seg_col[lines, :] == seg_row[...]
        for h in range(heads):
            q = rows[blocks, :, pl.ds(HEAD_DIM * h, HEAD_DIM)].reshape(2 * span, HEAD_DIM)
            k = rows[:, :, pl.ds(HEAD_DIM * (heads + h), HEAD_DIM)].reshape(total_rows, HEAD_DIM)
            v = rows[:, :, pl.ds(HEAD_DIM * (2 * heads + h), HEAD_DIM)].reshape(total_rows, HEAD_DIM)
            scores = SCALE * lax.dot_general(q, k, (((1,), (1,)), ((), ())), preferred_element_type=F32)
            scores = jnp.where(allowed, scores, NEG)
            weights = jnp.exp(scores - jnp.max(scores, axis=-1, keepdims=True))
            low = (weights * (1.0 / jnp.sum(weights, axis=-1, keepdims=True))).astype(BF16)
            probs[h, lines, :] = low
            value = jnp.dot(low, v, preferred_element_type=F32)
            mixed_float[lines, pl.ds(HEAD_DIM * h, HEAD_DIM)] = value
            send_mixed[blocks, :, pl.ds(HEAD_DIM * h, HEAD_DIM)] = value.astype(BF16).reshape(2, span, HEAD_DIM)
        keep(i).start()
        for n in range(2):
            @pl.when(2 * i + n != own_block)
            def _():
                to_tokens(2 * i + n).start()

            @pl.when(2 * i + n == own_block)
            def _():
                own_mixed.start()

        return carry

    lax.fori_loop(0, n_units, attend, 0)

    last = n_tensor - 1
    for g in (1, 2):
        sides(g, near(last))
    for g in (1, 2):
        corner(g, near(last - 1))

    own_mixed.wait()
    for j in range(n_ctx):
        for k in range(n_tensor):
            if j or k:
                c, t = lax.rem(ctx + j, n_ctx), lax.rem(z + k, n_tensor)
                slot = t * n_ctx + c
                remote(mixed.at[slot], mixed.at[slot], m_send.at[0], m_recv.at[slot], x_dev).wait_recv()

    flip = (((1,), (1,)), ((), ()))
    total[...] = x[...].astype(F32) + vectors[pl.ds(0, 1), :]

    def add_merge(t, carry):
        value = mixed[pl.ds(t * n_ctx, n_ctx)].reshape(count, part_width)
        total[...] += lax.dot_general(value, whole(f0, t)[:, wide:], flip, preferred_element_type=F32)
        return carry

    lax.fori_loop(0, n_tensor, add_merge, 0)
    normal[0], scale[0] = normalize(total[...])
    value = normal[0] * vectors[pl.ds(1, 1), :] + vectors[pl.ds(2, 1), :]
    total[...] = value + vectors[pl.ds(3, 1), :]
    first_low[...] = value.astype(BF16)
    for g in (1, 2):
        corner(g, near(last))
        own[g].wait()

    def units(t):
        for g in (1, 2):
            partner(g, t)
        bias = gathered(small_all[pl.ds(t * 8, 8), 7, :], e_spread, e_owned)
        before = jnp.dot(first_low[...], whole(f1, t), preferred_element_type=F32) + bias
        value, rise = gelu_exact(before)
        low = value.astype(BF16)
        active[t] = low
        slope[t] = rise
        total[...] += lax.dot_general(low, whole(f2, t), flip, preferred_element_type=F32)

    def third(j, carry):
        units(near(j))
        return carry

    lax.fori_loop(0, n_tensor, third, 0)

    normal[1], scale[1] = normalize(total[...])
    gain = vectors[pl.ds(4, 1), :]
    outputs[...] = normal[1] * gain + vectors[pl.ds(5, 1), :]
    pull = cotangent[...].astype(F32)
    small_grads[:, 0, :] = jnp.zeros_like(small_grads[:, 0, :])
    small_grads[:, 5, :] = scattered(total_rows_of(pull * normal[1]), v_spread, v_owned)
    small_grads[:, 6, :] = scattered(total_rows_of(pull), v_spread, v_owned)
    second_grad = normalize_back(pull, normal[1], scale[1], gain)
    small_grads[:, 4, :] = scattered(total_rows_of(second_grad), v_spread, v_owned)
    total[...] = second_grad
    second_low[...] = second_grad.astype(BF16)
    turned[0] = second_low[...].T
    turned[1] = first_low[...].T
    blocked = (2, 2, 2, n_rows, g1.shape[-1])

    def store(which, t):
        grad, out = ((g1, g1_out), (g2, g2_out))[which]
        return pltpu.make_async_copy(grad.at[t], out.at[t], g_sem.at[which, t])

    def units_back(t, carry):
        low = active[t]
        g2[t] = jnp.dot(turned[0], low, preferred_element_type=F32).astype(BF16).reshape(blocked)
        store(1, t).start()
        back = jnp.dot(second_low[...], whole(f2, t), preferred_element_type=F32) * slope[t]
        back_low = back.astype(BF16)
        sums = total_rows_of(back_low.astype(F32))
        small_grads[pl.ds(t * 8, 8), 7, :] = scattered(sums, e_spread, e_owned)
        g1[t] = jnp.dot(turned[1], back_low, preferred_element_type=F32).astype(BF16).reshape(blocked)
        store(0, t).start()
        total[...] += lax.dot_general(back_low, whole(f1, t), flip, preferred_element_type=F32)
        return carry

    lax.fori_loop(0, n_tensor, units_back, 0)
    pull = total[...]
    small_grads[:, 2, :] = scattered(total_rows_of(pull * normal[0]), v_spread, v_owned)
    small_grads[:, 3, :] = scattered(total_rows_of(pull), v_spread, v_owned)
    value = normalize_back(pull, normal[0], scale[0], vectors[pl.ds(1, 1), :])
    small_grads[:, 1, :] = scattered(total_rows_of(value), v_spread, v_owned)
    first_grad[...] = value
    first_low_grad[...] = value.astype(BF16)

    for j in range(n_ctx):
        for k in range(n_tensor):
            if j or k:
                c, t = lax.rem(ctx + j, n_ctx), lax.rem(z + k, n_tensor)
                to_tokens(c * n_tensor + t).wait_send()
                to_heads(t, c).wait_send()
    for i in range(n_units):
        keep(i).wait()

    def finish(origin, carry):
        for g in range(3):
            for kind in range(4):
                core(g, origin, kind, slots[kind]).wait_send()
            along(g, origin, me, x_send, x_recv, x_dev).wait_send()
            along(g, origin, me, y_send, y_recv, y_dev).wait_send()
            part(g, origin, x_slot, 0, a_send, a_recv, y_dev).wait_send()
            part(g, origin, y_slot, half, b_send, b_recv, x_dev).wait_send()

            @pl.when((origin <= z) & up_ok)
            def _():
                up(g, origin).wait_send()

            @pl.when((origin >= z) & down_ok)
            def _():
                down(g, origin).wait_send()
        for which in range(2):
            store(which, origin).wait()
        return carry

    lax.fori_loop(0, n_tensor, finish, 0)


def forward_layer(n_tensor, heads, x, cotangent, triple, merge, w1, shrink, small, matrices, seg_row, seg_col):
    rows, cols = w1.shape
    count, width = x.shape
    n_small = 8 * n_tensor
    blocks = 2 * n_tensor
    span = count // 2
    length = blocks * span
    part = heads * HEAD_DIM
    dma = pltpu.SemaphoreType.DMA
    shape = jax.ShapeDtypeStruct
    full = (n_tensor, 8, rows, cols)
    split = (n_tensor, 2, 2, 2, rows, cols)
    pair = [dma((3, n_tensor)), dma((3, n_tensor))]
    vmem = pl.BlockSpec(memory_space=pltpu.VMEM)
    hbm = pl.BlockSpec(memory_space=pl.ANY)
    return pl.pallas_call(
        functools.partial(forward_kernel, n_tensor, heads),
        out_shape=(
            shape(full, BF16), shape((blocks, span, 3 * part), BF16),
            shape((length, part), F32), shape((heads, length, length), BF16), shape((blocks, span, part), BF16),
            shape((count, width), F32), shape((count, width), BF16), shape((count, width), BF16),
            shape((count, width), F32), shape((n_small,) + small.shape, F32), shape(split, BF16), shape(split, BF16),
        ),
        in_specs=[vmem] * 15,
        out_specs=(vmem, vmem, vmem, hbm) + (vmem,) * 6 + (hbm, hbm),
        scratch_shapes=[
            pltpu.VMEM((rows, cols), BF16),
            pltpu.VMEM((rows, cols), BF16),
            pltpu.VMEM(full, BF16),
            pltpu.VMEM(full, BF16),
            pltpu.VMEM((n_small,) + small.shape, F32),
            pltpu.VMEM((n_tensor, 2, span, 3 * part), BF16),
            pltpu.VMEM((blocks, span, part), BF16),
            pltpu.VMEM((heads, length, length), BF16),
            pltpu.VMEM((8, width), F32),
            pltpu.VMEM((2, count, width), F32),
            pltpu.VMEM((2, count, 1), F32),
            pltpu.VMEM((n_tensor, count, cols), BF16),
            pltpu.VMEM((n_tensor, count, cols), F32),
            pltpu.VMEM((count, width), F32),
            pltpu.VMEM((count, width), BF16),
            pltpu.VMEM((2, width, count), BF16),
            pltpu.VMEM(split, BF16),
            pltpu.VMEM(split, BF16),
            dma((5,)), dma((3, n_tensor)),
        ] + pair * 5 + [
            dma((3, 4, n_tensor)), dma((3, 4, n_tensor)), dma((n_small,)), dma((n_small,)),
            dma((n_tensor, 2)), dma((blocks,)), dma((blocks,)), dma((blocks,)), dma((blocks // 2,)),
            dma((2, n_tensor)),
        ],
        compiler_params=pltpu.CompilerParams(collective_id=0, has_side_effects=True, vmem_limit_bytes=60 << 20),
        cost_estimate=pl.CostEstimate(flops=0, bytes_accessed=w1.size * 400, transcendentals=0),
        name="forward_layer",
    )(x, cotangent, triple, merge, w1, shrink, small, *matrices, seg_row, seg_col)


def far(n_tensor, j):
    return in_order(lambda t, here: (-abs(t - here), t), n_tensor, j)


def sum_steps(n_tensor, grads, acc, core_in, y1_in, x1_in, x2_in, y2_in, up_in, down_in, load_sem, c_send, c_recv,
              y1_send, y1_recv, x1_send, x1_recv, x2_send, x2_recv, y2_send, y2_recv, up_send, up_recv, down_send, down_recv):
    dp, ctx, z = (lax.axis_index(a) for a in ALL)
    rows = acc.shape[-2]
    half = rows // 2
    core = lax.rem(dp, 2)
    x = lax.div(dp, 2)
    xp, yp = 1 - x, 1 - ctx
    x_dev, y_dev, c_dev = at(xp * 2 + core, ctx, z), at(dp, yp, z), at(x * 2 + 1 - core, ctx, z)
    low, high = pl.ds(0, half), pl.ds(half, half)
    count = range(len(grads))

    def load(g, t):
        return pltpu.make_async_copy(grads[g].at[t, :, core], acc.at[g, t], load_sem.at[g, t])

    def to_core(g, t):
        return remote(grads[g].at[t, :, 1 - core], core_in.at[g, t], c_send.at[g, t], c_recv.at[g, t], c_dev)

    def y1(g, t):
        return remote(acc.at[g, t, :, yp, low], y1_in.at[g, t], y1_send.at[g, t], y1_recv.at[g, t], y_dev)

    def x1(g, t):
        return remote(acc.at[g, t, xp, :, high], x1_in.at[g, t], x1_send.at[g, t], x1_recv.at[g, t], x_dev)

    def x2(g, t):
        return remote(acc.at[g, t, xp, ctx, low], x2_in.at[g, t], x2_send.at[g, t], x2_recv.at[g, t], x_dev)

    def y2(g, t):
        return remote(acc.at[g, t, x, yp, high], y2_in.at[g, t], y2_send.at[g, t], y2_recv.at[g, t], y_dev)

    up_dev, down_dev = at(dp, ctx, jnp.minimum(z + 1, n_tensor - 1)), at(dp, ctx, jnp.maximum(z - 1, 0))

    def up(g, t):
        return remote(acc.at[g, t, x, ctx], up_in.at[g, t], up_send.at[g, t], up_recv.at[g, t], up_dev)

    def down(g, t):
        return remote(acc.at[g, t, x, ctx], down_in.at[g, t], down_send.at[g, t], down_recv.at[g, t], down_dev)

    def add(a, b):
        return (a.astype(F32) + b.astype(F32)).astype(BF16)

    def target(j):
        return far(n_tensor, j)

    def begin(j):
        t = target(j)
        for g in count:
            to_core(g, t).start()
            load(g, t).start()

    def core_step(j):
        t = target(j)
        for g in count:
            load(g, t).wait()
            to_core(g, t).wait_recv()
            acc[g, t] = add(acc[g, t], core_in[g, t])
            y1(g, t).start()
            x1(g, t).start()

    def first_step(j):
        t = target(j)
        for g in count:
            y1(g, t).wait_recv()
            for i in range(2):
                acc[g, t, i, ctx, low] = add(acc[g, t, i, ctx, low], y1_in[g, t, i])
            x2(g, t).start()
            x1(g, t).wait_recv()
            for i in range(2):
                acc[g, t, x, i, high] = add(acc[g, t, x, i, high], x1_in[g, t, i])
            y2(g, t).start()

    def second_step(j):
        t = target(j)
        for g in count:
            x2(g, t).wait_recv()
            acc[g, t, x, ctx, low] = add(acc[g, t, x, ctx, low], x2_in[g, t])
            y2(g, t).wait_recv()
            acc[g, t, x, ctx, high] = add(acc[g, t, x, ctx, high], y2_in[g, t])

    def third_step(j):
        t = target(j)
        for g in count:
            @pl.when((t >= z) & (z > 0))
            def _():
                up(g, t).wait_recv()
                acc[g, t, x, ctx] = add(acc[g, t, x, ctx], up_in[g, t])

            @pl.when((t <= z) & (z < n_tensor - 1))
            def _():
                down(g, t).wait_recv()
                acc[g, t, x, ctx] = add(acc[g, t, x, ctx], down_in[g, t])

            @pl.when(t > z)
            def _():
                up(g, t).start()

            @pl.when(t < z)
            def _():
                down(g, t).start()

    def end(outs):
        for g in count:
            outs[g][...] = acc[g, z, x, ctx].astype(F32)

        def finish(t, carry):
            for g in count:
                for copy in (to_core, y1, x1, x2, y2):
                    copy(g, t).wait_send()

                @pl.when(t > z)
                def _():
                    up(g, t).wait_send()

                @pl.when(t < z)
                def _():
                    down(g, t).wait_send()
            return carry

        lax.fori_loop(0, n_tensor, finish, 0)

    return begin, core_step, first_step, second_step, third_step, end


def sum_scratch(n_grads, n_tensor, rows, cols):
    dma = pltpu.SemaphoreType.DMA
    grid = (n_grads, n_tensor)
    half = rows // 2
    return [
        pltpu.VMEM(grid + (2, 2, rows, cols), BF16),
        pltpu.VMEM(grid + (2, 2, rows, cols), BF16),
        pltpu.VMEM(grid + (2, half, cols), BF16),
        pltpu.VMEM(grid + (2, half, cols), BF16),
        pltpu.VMEM(grid + (half, cols), BF16),
        pltpu.VMEM(grid + (half, cols), BF16),
        pltpu.VMEM(grid + (rows, cols), BF16),
        pltpu.VMEM(grid + (rows, cols), BF16),
    ] + [dma(grid)] * 15


def backward_kernel(n_tensor, heads, first_low, first_grad, x, f0, mixed, small, spread, owned, rows, mixed_float,
                    probs_in, g1, g2, input_grad, o0, o1, o2, small_out,
                    turned, g0, mixed_grad, grad, probs, send_rows, qkv_grad, key_sum, value_sum, small_send, small_in,
                    own_sem, g_send, g_recv, q_send, q_recv, p_sem, s_send, s_recv, *scratch):
    dp, ctx, z = (lax.axis_index(a) for a in ALL)
    n_ctx = 2
    n_blocks = n_ctx * n_tensor
    n_units = n_blocks // 2
    span = grad.shape[1]
    part = grad.shape[2]
    wide = 3 * part
    n_rows, width = f0.shape[-2:]
    total_rows = n_blocks * span
    own_block = ctx * n_tensor + z
    own_slot = z * n_ctx + ctx
    mine = z * 8 + dp * 2 + ctx
    peers = everyone(4, 2, n_tensor)
    greet([at(*p) for p in peers])
    others = [(lax.rem(ctx + j, n_ctx), lax.rem(z + k, n_tensor))
              for k in (2, 3, 1, 0) for j in range(n_ctx) if (j or k) and k < n_tensor]
    half = len(scratch) // 2
    begin, core_step, first_step, second_step, third_step, end = sum_steps(n_tensor, (g1, g2), *scratch[:half])
    begin_last, core_last, first_last, second_last, third_last, end_last = sum_steps(n_tensor, (g0,), *scratch[half:])

    def to_heads(c, t):
        return remote(mixed_grad.at[t * n_ctx + c], grad.at[own_block], g_send.at[t * n_ctx + c],
                      g_recv.at[own_block], at(dp, c, t))

    def load(i):
        lines = pl.ds(i * 2 * span, 2 * span)
        return pltpu.make_async_copy(probs_in.at[:, lines], probs.at[:, lines], p_sem.at[i])

    here = pltpu.make_async_copy(mixed_grad.at[own_slot], grad.at[own_block], own_sem.at[0])

    def begin_all(j, carry):
        begin(j)
        return carry

    lax.fori_loop(0, n_tensor, begin_all, 0)

    def spread_grad(j, carry):
        t = far(n_tensor, j)
        weight = f0[t].reshape(8 * n_rows, width)[:, wide:]
        value = jnp.dot(first_low[...], weight, preferred_element_type=F32).astype(BF16)
        mixed_grad[pl.ds(t * n_ctx, n_ctx)] = value.reshape(n_ctx, span, part)
        to_heads(1 - ctx, t).start()

        @pl.when(t != z)
        def _():
            to_heads(ctx, t).start()

        @pl.when(t == z)
        def _():
            here.start()

        return carry

    lax.fori_loop(0, n_tensor, spread_grad, 0)
    for i in range(n_units):
        load(i).start()

    def core_steps(j, carry):
        core_step(j)
        return carry

    lax.fori_loop(0, n_tensor, core_steps, 0)
    turned[0] = first_low[...].T
    turned[1] = x[...].T
    small_send[...] = small[...]

    def merge_grad(t, carry):
        value = jnp.dot(turned[0], mixed[pl.ds(t * n_ctx, n_ctx)].reshape(n_ctx * span, part),
                        preferred_element_type=F32)
        g0[t, :, :, :, :, pl.ds(wide, part)] = value.astype(BF16).reshape(2, 2, 2, n_rows, part)
        return carry

    lax.fori_loop(0, n_tensor, merge_grad, 0)
    first_step(0)
    here.wait()
    for c, t in others:
        block = c * n_tensor + t
        remote(grad.at[block], grad.at[block], g_send.at[0], g_recv.at[block], at(dp, c, t)).wait_recv()
    for i in range(n_units):
        load(i).wait()

    def one_head(h):
        lanes = pl.ds(HEAD_DIM * h, HEAD_DIM)
        k_lanes = pl.ds(HEAD_DIM * (heads + h), HEAD_DIM)
        v_lanes = pl.ds(HEAD_DIM * (2 * heads + h), HEAD_DIM)
        key_sum[...] = jnp.zeros_like(key_sum)
        value_sum[...] = jnp.zeros_like(value_sum)

        def unit(i, carry):
            blocks = pl.ds(2 * i, 2)
            lines = pl.ds(pl.multiple_of(i * 2 * span, 2 * span), 2 * span)
            q = rows[blocks, :, lanes].reshape(2 * span, HEAD_DIM)
            k = rows[:, :, k_lanes].reshape(total_rows, HEAD_DIM)
            v = rows[:, :, v_lanes].reshape(total_rows, HEAD_DIM)
            up = grad[blocks, :, lanes].reshape(2 * span, HEAD_DIM)
            low = probs[h, lines, :]
            delta = jnp.sum(up.astype(F32) * mixed_float[lines, lanes], axis=-1, keepdims=True)
            pull = lax.dot_general(up, v, (((1,), (1,)), ((), ())), preferred_element_type=F32)
            score = (low.astype(F32) * (pull - delta)).astype(BF16)
            query = SCALE * jnp.dot(score, k, preferred_element_type=F32)
            send_rows[blocks, :, lanes] = query.astype(BF16).reshape(2, span, HEAD_DIM)
            key_sum[...] += lax.dot_general(q, score, (((0,), (0,)), ((), ())), preferred_element_type=F32)
            value_sum[...] += lax.dot_general(up, low, (((0,), (0,)), ((), ())), preferred_element_type=F32)
            return carry

        lax.fori_loop(0, n_units, unit, 0)
        key = (SCALE * key_sum[...]).T.astype(BF16)
        value = value_sum[...].T.astype(BF16)
        send_rows[:, :, k_lanes] = key.reshape(n_blocks, span, HEAD_DIM)
        send_rows[:, :, v_lanes] = value.reshape(n_blocks, span, HEAD_DIM)

    for h in range(heads):
        one_head(h)
        if h < 2:
            first_step(h + 1)

    def to_tokens(c, t):
        return remote(send_rows.at[c * n_tensor + t], qkv_grad.at[own_slot], q_send.at[c * n_tensor + t],
                      q_recv.at[own_slot], at(dp, c, t))

    there = pltpu.make_async_copy(send_rows.at[own_block], qkv_grad.at[own_slot], own_sem.at[1])

    def send_back(j, carry):
        t = far(n_tensor, j)
        to_tokens(1 - ctx, t).start()

        @pl.when(t != z)
        def _():
            to_tokens(ctx, t).start()

        @pl.when(t == z)
        def _():
            there.start()

        return carry

    lax.fori_loop(0, n_tensor, send_back, 0)

    def rest(j, carry):
        @pl.when((j >= 3) & (j < n_tensor))
        def _():
            first_step(j)

        @pl.when((j >= 3) & (j < n_tensor + 3))
        def _():
            second_step(j - 3)

        @pl.when(j >= 4)
        def _():
            third_step(j - 4)

        return carry

    lax.fori_loop(1 + min(heads, 2), n_tensor + 4, rest, 0)

    def arrived(t, c):
        slot = t * n_ctx + c
        remote(qkv_grad.at[slot], qkv_grad.at[slot], q_send.at[0], q_recv.at[slot], at(dp, c, t)).wait_recv()

    def weight_grad(j):
        t = far(n_tensor, j)
        arrived(t, 1 - ctx)

        @pl.when(t != z)
        def _():
            arrived(t, ctx)

        @pl.when(t == z)
        def _():
            there.wait()

        pull = qkv_grad[pl.ds(t * n_ctx, n_ctx)].reshape(n_ctx * span, wide)
        value = jnp.dot(turned[1], pull, preferred_element_type=F32)
        g0[t, :, :, :, :, pl.ds(0, wide)] = value.astype(BF16).reshape(2, 2, 2, n_rows, wide)
        begin_last(j)
        small_send[pl.ds(t * 8, 8), 0, :] = scattered(total_rows_of(pull.astype(F32)), spread, owned)

    def weight_grads(j, carry):
        @pl.when(j < n_tensor)
        def _():
            weight_grad(j)

        @pl.when(j >= 1)
        def _():
            core_last(j - 1)

        return carry

    lax.fori_loop(0, n_tensor + 1, weight_grads, 0)
    small_copies = [
        remote(small_send.at[pt * 8 + pd * 2 + pc], small_in.at[n], s_send.at[n], s_recv.at[n], at(pd, pc, pt))
        for n, (pd, pc, pt) in enumerate(peers)
    ]
    for copy in small_copies:
        copy.start()
    input_grad[...] = first_grad[...]

    def add_input(j):
        pull = qkv_grad[pl.ds(j * n_ctx, n_ctx)].reshape(n_ctx * span, wide)
        weight = f0[j].reshape(8 * n_rows, width)[:, :wide]
        input_grad[...] += lax.dot_general(pull, weight, (((1,), (1,)), ((), ())), preferred_element_type=F32)

    def last(j, carry):
        @pl.when(j < n_tensor)
        def _():
            first_last(j)

        @pl.when((j >= 1) & (j < n_tensor + 1))
        def _():
            second_last(j - 1)

        @pl.when(j >= 2)
        def _():
            third_last(j - 2)

        @pl.when(j < n_tensor)
        def _():
            add_input(j)

        return carry

    lax.fori_loop(0, n_tensor + 2, last, 0)
    end((o1, o2))
    end_last((o0,))
    total = small_send[mine]
    for n in range(len(peers)):
        small_copies[n].wait()
        total = total + small_in[n]
    small_out[...] = total
    for c, t in others:
        to_tokens(c, t).wait_send()
        to_heads(c, t).wait_send()


def backward_attention(n_tensor, heads, first_low, first_grad, x, f0, mixed, small, spread, owned, rows, mixed_float,
                       probs, g1, g2):
    blocks, span, wide = rows.shape
    part = heads * HEAD_DIM
    length = blocks * span
    n_rows, cols = g1.shape[-2:]
    n_small = 8 * n_tensor
    dma = pltpu.SemaphoreType.DMA
    vmem = pl.BlockSpec(memory_space=pltpu.VMEM)
    hbm = pl.BlockSpec(memory_space=pl.ANY)
    shape = jax.ShapeDtypeStruct
    out = shape((n_rows, cols), F32)
    return pl.pallas_call(
        functools.partial(backward_kernel, n_tensor, heads),
        out_shape=(shape(first_grad.shape, F32), out, out, out, shape(small.shape[1:], F32)),
        in_specs=[vmem] * 10 + [hbm] * 3,
        out_specs=(vmem,) * 5,
        scratch_shapes=[
            pltpu.VMEM((2,) + x.shape[::-1], BF16),
            pltpu.VMEM(g1.shape, BF16),
            pltpu.VMEM((blocks, span, part), BF16),
            pltpu.VMEM((blocks, span, part), BF16),
            pltpu.VMEM((heads, length, length), BF16),
            pltpu.VMEM((blocks, span, wide), BF16),
            pltpu.VMEM((blocks, span, wide), BF16),
            pltpu.VMEM((HEAD_DIM, length), F32),
            pltpu.VMEM((HEAD_DIM, length), F32),
            pltpu.VMEM(small.shape, F32),
            pltpu.VMEM((n_small - 1,) + small.shape[1:], F32),
            dma((2,)), dma((blocks,)), dma((blocks,)), dma((blocks,)), dma((blocks,)), dma((blocks // 2,)),
            dma((n_small - 1,)), dma((n_small - 1,)),
        ] + sum_scratch(2, n_tensor, n_rows, cols) + sum_scratch(1, n_tensor, n_rows, cols),
        compiler_params=pltpu.CompilerParams(collective_id=2, has_side_effects=True, vmem_limit_bytes=58 << 20),
        cost_estimate=pl.CostEstimate(flops=0, bytes_accessed=g1.size * 24, transcendentals=0),
        name="backward_attention",
    )(first_low, first_grad, x, f0, mixed, small, spread, owned, rows, mixed_float, probs, g1, g2)


def norm_rows(total, gain, shift):
    center = total - jnp.mean(total, axis=-1, keepdims=True)
    spread = jnp.mean(center * center, axis=-1, keepdims=True)
    return center * lax.rsqrt(spread + EPS) * gain + shift


def gelu_exact(before):
    share = 0.5 + 0.5 * lax.erf(before * 0.5**0.5)
    dense = (0.5 / np.pi) ** 0.5 * jnp.exp(-0.5 * before * before)
    return before * share, share + before * dense


def dot(spec, a, b):
    return jnp.einsum(spec, a, b, preferred_element_type=F32)


def add_up(spec, a, b):
    return sum(dot(spec, a[t], b[t]) for t in range(a.shape[0]))


def local(
    inputs,
    cotangent,
    segments,
    triple_weight,
    attend_bias,
    merge_weight,
    merge_bias,
    first_gain,
    first_shift,
    expand_weight,
    expand_bias,
    shrink_weight,
    shrink_bias,
    second_gain,
    second_shift,
):
    n_dp, n_ctx, n_tensor = (lax.axis_size(a) for a in ALL)
    span, batch, width = inputs.shape
    rows = triple_weight.shape[1]
    part = triple_weight.shape[2]
    units = expand_weight.shape[1]
    owners = n_dp * n_ctx
    heads = part // HEAD_DIM
    count = batch * span
    small_part = part // owners
    unit_part = units // owners
    own_kernels = n_dp == 4 and n_ctx == 2 and batch == 2 and n_tensor == 4 and rows % 32 == 0

    narrow_in = (merge_bias, first_gain, first_shift, shrink_bias, second_gain, second_shift)
    x_low = jnp.transpose(inputs, (1, 0, 2)).reshape(count, width)
    cotangent_rows = jnp.transpose(cotangent, (1, 0, 2)).reshape(count, width)
    here = lax.axis_index("ctx")
    if own_kernels:
        labels = lax.dynamic_slice_in_dim(segments, here, 1, 0)
        lines = [attend_bias.reshape(1, -1)] + list(narrow_in) + [expand_bias]
        small = sum(
            jnp.pad(v.astype(F32), ((n, 7 - n), (0, 128 - v.shape[1]))) for n, v in enumerate(lines)
        )
        matrices = tables(n_tensor, owners, part, units)
        (f0, rows_all, mixed_float, probs, mixed, outputs_rows, first_low, first_low_grad, first_grad, small_grads,
         expand_grad, shrink_grad) = forward_layer(
            n_tensor, heads, x_low, cotangent_rows, triple_weight, merge_weight, expand_weight, shrink_weight, small,
            matrices, labels, labels.reshape(-1, 1)
        )
        inputs_gradient, r0, r1, r2, small_sum = backward_attention(
            n_tensor, heads, first_low_grad, first_grad, x_low, f0, mixed, small_grads, *matrices[:2],
            rows_all, mixed_float, probs, expand_grad, shrink_grad
        )
        narrow_out = [small_sum[:1, :small_part], small_sum[:1, small_part : 2 * small_part]]
        narrow_out += [small_sum[n : n + 1, :small_part] for n in range(1, 7)]
        expand_out = small_sum[7:, :unit_part]
    else:
        pieces = [attend_bias[0, 0], attend_bias[1, 0]] + [v[0] for v in narrow_in] + [expand_bias[0]]
        w0 = jnp.concatenate(
            [jnp.transpose(triple_weight, (1, 0, 2)).reshape(rows, 3 * part), merge_weight.T], axis=1
        )
        small = jnp.concatenate(pieces).astype(F32)
        f0, f1, f2 = (
            lax.all_gather(lax.all_gather(w, ("dp", "ctx"), axis=0, tiled=True), "tensor", axis=0, tiled=False)
            for w in (w0, expand_weight, shrink_weight.T)
        )
        small_all = lax.all_gather(lax.all_gather(small, ("dp", "ctx")), "tensor")
        f0, w_expand, w_shrink = (w.reshape(n_tensor, width, -1) for w in (f0, f1, f2))
        w_qkv, w_merge = f0[:, :, : 3 * part], f0[:, :, 3 * part :]
        narrow = small_all[:, :, : 8 * small_part].reshape(n_tensor, owners, 8, small_part)
        narrow = jnp.transpose(narrow, (2, 0, 1, 3)).reshape(8, n_tensor, part)
        merge_vec, gain_one, shift_one, shrink_vec, gain_two, shift_two = narrow[2:].reshape(6, width)
        expand_vec = small_all[:, :, 8 * small_part :].reshape(n_tensor, 1, units)
        qkv_vec = jnp.concatenate([narrow[0], jnp.zeros_like(narrow[0]), narrow[1]], axis=-1)[:, None]
        x = x_low.astype(F32)
        upstream = cotangent_rows.astype(F32)

        def to_tokens(value):
            value = value.reshape(batch, n_tensor, span, -1)
            out = lax.all_to_all(jnp.transpose(value, (1, 0, 2, 3)), "tensor", split_axis=0, concat_axis=0)
            return out.reshape(n_tensor, count, -1)

        qkv = (dot("rd,tde->tre", x_low, w_qkv) + qkv_vec).astype(BF16)
        mine = lax.all_to_all(
            qkv.reshape(n_tensor, batch, span, 3 * part), "tensor", split_axis=0, concat_axis=0
        )
        mine = jnp.transpose(mine, (1, 0, 2, 3)).reshape(batch, n_tensor * span, 3 * part)
        n_query = n_tensor * span
        own_labels = lax.dynamic_slice_in_dim(segments, here * n_query, n_query, 1)
        kv_rows = lax.all_gather(mine[..., part:], "ctx", axis=1, tiled=True)
        n_key = kv_rows.shape[1]
        q_four = mine[..., :part].reshape(batch, n_query, heads, HEAD_DIM)
        k_four = kv_rows[..., :part].reshape(batch, n_key, heads, HEAD_DIM)
        v_four = kv_rows[..., part:].reshape(batch, n_key, heads, HEAD_DIM)
        allowed = own_labels[:, None, :, None] == segments[:, None, None, :]
        scores = jnp.where(allowed, SCALE * dot("sqhd,skhd->shqk", q_four, k_four), NEG)
        top = jnp.max(scores, axis=-1)
        weights = jnp.where(allowed, jnp.exp(scores - top[..., None]), 0.0)
        total = jnp.sum(weights, axis=-1)
        mixed_float = dot("shqk,skhd->shqd", weights.astype(BF16), v_four) / total[..., None]
        logsum = top + jnp.log(total)
        mixed = to_tokens(jnp.transpose(mixed_float, (0, 2, 1, 3)).reshape(batch, n_query, part).astype(BF16))
        first_sum = x + add_up("re,de->rd", mixed, w_merge) + merge_vec
        first_norm = norm_rows(first_sum, gain_one, shift_one)
        first_low = first_norm.astype(BF16)
        before = dot("rd,tdf->trf", first_low, w_expand) + expand_vec
        active, slope = gelu_exact(before)
        active = active.astype(BF16)
        second_sum = first_norm + add_up("rf,df->rd", active, w_shrink) + shrink_vec
        outputs_rows = norm_rows(second_sum, gain_two, shift_two)

        second_grad, gain_two_grad, shift_two_grad = jax.vjp(norm_rows, second_sum, gain_two, shift_two)[1](upstream)
        shrink_vec_grad = jnp.sum(second_grad, axis=0)
        second_low = second_grad.astype(BF16)
        shrink_grad = dot("rd,trf->tdf", second_low, active).astype(BF16)
        active_grad = dot("rd,tdf->trf", second_low, w_shrink)
        before_low = (active_grad * slope).astype(BF16)
        expand_vec_grad = jnp.sum(before_low.astype(F32), axis=1)
        expand_grad = dot("rd,trf->tdf", first_low, before_low).astype(BF16)
        norm_back = add_up("rf,df->rd", before_low, w_expand)
        first_grad, gain_one_grad, shift_one_grad = jax.vjp(norm_rows, first_sum, gain_one, shift_one)[1](
            second_grad + norm_back
        )
        merge_vec_grad = jnp.sum(first_grad, axis=0)
        first_low_grad = first_grad.astype(BF16)
        vec_grads = jnp.stack(
            [merge_vec_grad, gain_one_grad, shift_one_grad, shrink_vec_grad, gain_two_grad, shift_two_grad]
        ).reshape(6, n_tensor, owners, small_part)
        vec_grads = jnp.transpose(vec_grads, (1, 2, 0, 3)).reshape(n_tensor, owners, 6 * small_part)
        small_grads = jnp.concatenate([vec_grads, expand_vec_grad.reshape(n_tensor, owners, unit_part)], axis=-1)
        merge_grad = dot("rd,tre->tde", first_low_grad, mixed).astype(BF16)
        mixed_grad = dot("rd,tde->tre", first_low_grad, w_merge).astype(BF16)
        grad_rows = lax.all_to_all(
            mixed_grad.reshape(n_tensor, batch, span, part), "tensor", split_axis=0, concat_axis=0
        )
        grad_four = jnp.transpose(grad_rows, (1, 0, 2, 3)).reshape(batch, n_query, heads, HEAD_DIM)
        delta = jnp.sum(jnp.transpose(grad_four.astype(F32), (0, 2, 1, 3)) * mixed_float, axis=-1)
        back_scores = SCALE * dot("sqhd,skhd->shqk", q_four, k_four)
        probs = jnp.where(allowed, jnp.exp(back_scores - logsum[..., None]), 0.0)
        prob_grad = dot("sqhd,skhd->shqk", grad_four, v_four)
        score_low = (probs * (prob_grad - delta[..., None])).astype(BF16)
        value_part = dot("shqk,sqhd->skhd", probs.astype(BF16), grad_four)
        query_part = SCALE * dot("shqk,skhd->sqhd", score_low, k_four)
        key_part = SCALE * dot("shqk,sqhd->skhd", score_low, q_four)
        query_part, key_part, value_part = (
            v.reshape(batch, -1, part).astype(BF16) for v in (query_part, key_part, value_part)
        )
        key_part, value_part = (
            lax.psum_scatter(v, "ctx", scatter_dimension=1, tiled=True) for v in (key_part, value_part)
        )
        qkv_grad = to_tokens(jnp.concatenate([query_part, key_part, value_part], axis=-1))
        triple_grad = dot("rd,tre->tde", x_low, qkv_grad).astype(BF16)
        attend_grad = jnp.sum(qkv_grad.astype(F32), axis=1).reshape(n_tensor, 3, owners, small_part)
        inputs_gradient = first_grad + add_up("re,de->rd", qkv_grad, w_qkv)
        small_grads = jnp.concatenate([attend_grad[:, 0], attend_grad[:, 2], small_grads], axis=-1)
        grads = (jnp.concatenate([triple_grad, merge_grad], axis=-1), expand_grad, shrink_grad)
        r0, r1, r2 = (
            lax.psum_scatter(
                lax.psum_scatter(g, "tensor", scatter_dimension=0), ("dp", "ctx"), scatter_dimension=0, tiled=True
            ).astype(F32)
            for g in grads
        )
        small_sum = lax.psum_scatter(
            lax.psum_scatter(small_grads, "tensor", scatter_dimension=0), ("dp", "ctx"), scatter_dimension=0
        )
        narrow_out = list(small_sum[: 8 * small_part].reshape(8, 1, small_part))
        expand_out = small_sum[8 * small_part :].reshape(1, unit_part)
    triple_out = jnp.transpose(r0[:, : 3 * part].reshape(rows, 3, part), (1, 0, 2))
    outputs_rows, inputs_gradient = (
        jnp.transpose(v.reshape(batch, span, width), (1, 0, 2)) for v in (outputs_rows, inputs_gradient)
    )
    return (
        outputs_rows,
        inputs_gradient,
        triple_out,
        jnp.stack(narrow_out[:2]),
        r0[:, 3 * part :].T,
        narrow_out[2],
        narrow_out[3],
        narrow_out[4],
        r1,
        expand_out,
        r2.T,
        narrow_out[5],
        narrow_out[6],
        narrow_out[7],
    )


def solution(mesh):
    in_specs = (
        P(("ctx", "tensor"), "dp", None),
        P(("ctx", "tensor"), "dp", None),
        P("dp", None),
        P(None, ("dp", "ctx"), "tensor"),
        P(None, "tensor", ("dp", "ctx")),
        P("tensor", ("dp", "ctx")),
        P("tensor", ("dp", "ctx")),
        P("tensor", ("dp", "ctx")),
        P("tensor", ("dp", "ctx")),
        P(("dp", "ctx"), "tensor"),
        P("tensor", ("dp", "ctx")),
        P("tensor", ("dp", "ctx")),
        P("tensor", ("dp", "ctx")),
        P("tensor", ("dp", "ctx")),
        P("tensor", ("dp", "ctx")),
    )
    out_specs = (
        P(("ctx", "tensor"), "dp", None),
        P(("ctx", "tensor"), "dp", None),
        P(None, ("dp", "ctx"), "tensor"),
        P(None, "tensor", ("dp", "ctx")),
        P("tensor", ("dp", "ctx")),
        P("tensor", ("dp", "ctx")),
        P("tensor", ("dp", "ctx")),
        P("tensor", ("dp", "ctx")),
        P(("dp", "ctx"), "tensor"),
        P("tensor", ("dp", "ctx")),
        P("tensor", ("dp", "ctx")),
        P("tensor", ("dp", "ctx")),
        P("tensor", ("dp", "ctx")),
        P("tensor", ("dp", "ctx")),
    )
    return jax.shard_map(local, mesh=mesh, in_specs=in_specs, out_specs=out_specs, check_vma=False)
```

```python
import functools

import jax
import jax.numpy as jnp
import numpy as np
from jax import lax
from jax.experimental import pallas as pl
from jax.experimental.pallas import tpu as pltpu
from jax.sharding import PartitionSpec as P

HEAD_DIM = 64

EPS = 1e-12
NEG = -1e30
SCALE = 0.125
MESH = pl.DeviceIdType.MESH
BF16 = jnp.bfloat16
F32 = jnp.float32
ALL = ("dp", "ctx", "tensor")
TOKENS = ("ctx", "tensor")


def at(dp, ctx, tensor):
    return {"dp": dp, "ctx": ctx, "tensor": tensor}


def remote(src, dst, send, recv, where):
    return pltpu.make_async_remote_copy(
        src_ref=src, dst_ref=dst, send_sem=send, recv_sem=recv, device_id=where, device_id_type=MESH
    )


def greet(peers):
    barrier = pltpu.get_barrier_semaphore()
    for peer in peers:
        pl.semaphore_signal(barrier, inc=1, device_id=peer, device_id_type=MESH)
    pl.semaphore_wait(barrier, len(peers))


def everyone(n_dp, n_ctx, n_tensor):
    dp, ctx, tensor = (lax.axis_index(a) for a in ALL)
    peers = []
    for i in range(n_dp):
        for j in range(n_ctx):
            for k in range(n_tensor):
                if i or j or k:
                    peers.append(
                        (lax.rem(dp + i, n_dp), lax.rem(ctx + j, n_ctx), lax.rem(tensor + k, n_tensor))
                    )
    return peers


def in_order(key, n_tensor, j):
    z = lax.axis_index("tensor")
    found = 0
    for here in range(n_tensor):
        for n, there in enumerate(sorted(range(n_tensor), key=lambda t: key(t, here))):
            found = found + jnp.where((z == here) & (j == n), there, 0)
    return found


def one_hot(n_lanes, owners, picks, width):
    spread = np.zeros((n_lanes, width), np.float32)
    owned = np.zeros((owners, width), np.float32)
    for feature, (lane, owner) in picks.items():
        spread[lane, feature] = 1.0
        owned[owner, feature] = 1.0
    return jnp.asarray(spread, BF16), jnp.asarray(owned)


def tables(n_tensor, owners, part, units):
    piece, unit = part // owners, units // owners
    attend = {n: (n % piece, n // piece) for n in range(part)}
    attend.update({2 * part + n: (piece + n % piece, n // piece) for n in range(part)})
    whole = {t * part + n: (n % piece, t * owners + n // piece) for t in range(n_tensor) for n in range(part)}
    expand = {n: (n % unit, n // unit) for n in range(units)}
    return (
        one_hot(128, owners, attend, 3 * part)
        + one_hot(128, n_tensor * owners, whole, n_tensor * part)
        + one_hot(128, owners, expand, units)
    )


def gathered(pieces, spread, owned):
    value = jnp.dot(pieces.astype(BF16), spread[...], preferred_element_type=F32)
    return jnp.sum(value * owned[...], axis=0, keepdims=True)


def scattered(vector, spread, owned):
    total = vector * owned[...]
    upper = total.astype(BF16)
    lower = (total - upper.astype(F32)).astype(BF16)
    flip = (((1,), (1,)), ((), ()))
    return lax.dot_general(upper, spread[...], flip, preferred_element_type=F32) + lax.dot_general(
        lower, spread[...], flip, preferred_element_type=F32
    )


def normalize(total):
    center = total - jnp.mean(total, axis=-1, keepdims=True)
    spread = jnp.mean(center * center, axis=-1, keepdims=True)
    scale = lax.rsqrt(spread + EPS)
    return center * scale, scale


def normalize_back(up, normal, scale, gain):
    pull = up * gain
    return scale * (
        pull - jnp.mean(pull, axis=-1, keepdims=True) - normal * jnp.mean(pull * normal, axis=-1, keepdims=True)
    )


def total_rows_of(value):
    return jnp.sum(value, axis=0, keepdims=True)


def forward_kernel(n_tensor, heads, x, cotangent, triple, merge, w1, shrink, small, a_spread, a_owned, v_spread,
                   v_owned, e_spread, e_owned, seg_row, seg_col,
                   f0, rows, mixed_float, probs_out, mixed, outputs, first_low, first_low_grad, first_grad,
                   small_grads, g1_out, g2_out,
                   w0, w2, f1, f2, small_all, send_rows, send_mixed, probs, vectors, normal, scale, active, slope,
                   total, second_low, turned, g1, g2,
                   own_sem, z_up, z_down, z_recv, x_send, x_recv, y_send, y_recv, a_send, a_recv, b_send, b_recv,
                   c_send, c_recv, s_send, s_recv, q_send, q_recv, m_send, m_recv, p_sem, g_sem):
    shards, outs = (w0, w1, w2), (f0, f1, f2)
    dp, ctx, z = (lax.axis_index(a) for a in ALL)
    n_ctx = 2
    n_rows = w0.shape[0]
    half = n_rows // 2
    xp = lax.rem(dp + 2, 4)
    cp = dp + 1 - 2 * lax.rem(dp, 2)
    yp = 1 - ctx
    xcp = lax.rem(cp + 2, 4)
    me = dp * 2 + ctx
    mine = z * 8 + me
    peers = everyone(4, 2, n_tensor)
    wide = a_spread.shape[1]
    part_width = wide // 3
    for i in range(3):
        w0[:, pl.ds(i * part_width, part_width)] = triple[i]
    w0[:, pl.ds(wide, merge.shape[0])] = merge[...].T
    w2[...] = shrink[...].T
    greet([at(*p) for p in peers])
    x_dev, y_dev, c_dev = at(xp, ctx, z), at(dp, yp, z), at(cp, ctx, z)
    x_slot, y_slot, d_slot = xp * 2 + ctx, dp * 2 + yp, xp * 2 + yp
    slots = (cp * 2 + ctx, xcp * 2 + ctx, cp * 2 + yp, xcp * 2 + yp)
    up_ok, down_ok = z < n_tensor - 1, z > 0

    def near(j):
        middle = (n_tensor - 1) / 2
        return in_order(lambda t, here: (abs(t - here), abs(t - middle)), n_tensor, j)

    def up(g, origin, src=None):
        block = outs[g].at[origin, me]
        return remote(block if src is None else src, block, z_up.at[g, origin], z_recv.at[g, origin],
                      at(dp, ctx, jnp.minimum(z + 1, n_tensor - 1)))

    def down(g, origin, src=None):
        block = outs[g].at[origin, me]
        return remote(block if src is None else src, block, z_down.at[g, origin], z_recv.at[g, origin],
                      at(dp, ctx, jnp.maximum(z - 1, 0)))

    def from_z(g, origin):
        block = outs[g].at[origin, me]
        return remote(block, block, z_up.at[g, origin], z_recv.at[g, origin], x_dev)

    def along(g, origin, slot, send, recv, dev, src=None):
        block = outs[g].at[origin, slot]
        return remote(block if src is None else src, block, send.at[g, origin], recv.at[g, origin], dev)

    def part(g, origin, slot, lo, send, recv, dev):
        block = outs[g].at[origin, slot, pl.ds(lo, half)]
        return remote(block, block, send.at[g, origin], recv.at[g, origin], dev)

    def core(g, origin, kind, slot, src=None):
        block = outs[g].at[origin, slot]
        return remote(
            block if src is None else src, block, c_send.at[g, kind, origin], c_recv.at[g, kind, origin], c_dev
        )

    own = [pltpu.make_async_copy(shards[g], outs[g].at[z, me], own_sem.at[g]) for g in range(3)]

    def begin_z(g):
        @pl.when(up_ok)
        def _():
            up(g, z, shards[g]).start()

        @pl.when(down_ok)
        def _():
            down(g, z, shards[g]).start()

    def begin(g):
        along(g, z, me, x_send, x_recv, x_dev, shards[g]).start()
        along(g, z, me, y_send, y_recv, y_dev, shards[g]).start()
        core(g, z, 0, me, shards[g]).start()
        own[g].start()

    def column_z(g, origin):
        from_z(g, origin).wait_recv()

        @pl.when((origin < z) & up_ok)
        def _():
            up(g, origin).start()

        @pl.when((origin > z) & down_ok)
        def _():
            down(g, origin).start()

    def column(g, origin):
        along(g, origin, me, x_send, x_recv, x_dev).start()
        along(g, origin, me, y_send, y_recv, y_dev).start()
        core(g, origin, 0, me).start()

    def sides(g, origin):
        along(g, origin, x_slot, x_send, x_recv, x_dev).wait_recv()
        part(g, origin, x_slot, 0, a_send, a_recv, y_dev).start()
        core(g, origin, 1, x_slot).start()
        along(g, origin, y_slot, y_send, y_recv, y_dev).wait_recv()
        part(g, origin, y_slot, half, b_send, b_recv, x_dev).start()
        core(g, origin, 2, y_slot).start()

    def corner(g, origin):
        part(g, origin, d_slot, 0, a_send, a_recv, y_dev).wait_recv()
        part(g, origin, d_slot, half, b_send, b_recv, x_dev).wait_recv()
        core(g, origin, 3, d_slot).start()

    def partner(g, origin):
        for kind in range(4):
            core(g, origin, kind, slots[kind]).wait_recv()

    begin_z(0)
    begin(0)
    for g in (1, 2):
        begin_z(g)
    small_own = pltpu.make_async_copy(small, small_all.at[mine], s_send.at[0])
    small_own.start()
    for n, p in enumerate(peers):
        remote(small, small_all.at[mine], s_send.at[n + 1], s_recv.at[n], at(*p)).start()

    def to_heads(t, c):
        return remote(send_rows.at[t, c], rows.at[ctx * n_tensor + z], q_send.at[t, c],
                      q_recv.at[ctx * n_tensor + z], at(dp, c, t))

    def from_token(block):
        return remote(rows.at[block], rows.at[block], q_send.at[0, 0], q_recv.at[block], x_dev)

    count = x.shape[0]
    span = count // n_ctx
    width = x.shape[1]
    here = pltpu.make_async_copy(send_rows.at[z, ctx], rows.at[ctx * n_tensor + z], own_sem.at[3])

    def whole(ref, t):
        return ref[t].reshape(8 * n_rows, ref.shape[-1])

    def project(t):
        partner(0, t)
        bias = gathered(small_all[pl.ds(t * 8, 8), 0, :], a_spread, a_owned)
        value = jnp.dot(x[...], whole(f0, t), preferred_element_type=F32)[:, :wide] + bias
        send_rows[t] = value.astype(BF16).reshape(n_ctx, span, wide)
        to_heads(t, yp).start()

        @pl.when(t != z)
        def _():
            to_heads(t, ctx).start()

        @pl.when(t == z)
        def _():
            here.start()

    def first(j, carry):
        @pl.when(j < n_tensor - 1)
        def _():
            column_z(0, near(j + 1))
            column(0, near(j + 1))

        @pl.when(j < n_tensor)
        def _():
            sides(0, near(j))

        @pl.when(j == n_tensor - 1)
        def _():
            for g in (1, 2):
                begin(g)

        @pl.when(j >= 1)
        def _():
            corner(0, near(j - 1))

        @pl.when(j == 1)
        def _():
            own[0].wait()
            small_own.wait()
            for n, p in enumerate(peers):
                copy = remote(small, small_all.at[mine], s_send.at[n + 1], s_recv.at[n], at(*p))
                copy.wait_send()
                copy.wait_recv()

        @pl.when(j >= 1)
        def _():
            project(near(j - 1))

        @pl.when(j == n_tensor - 2)
        def _():
            for g in (1, 2):
                column_z(g, near(1))

        @pl.when(j == n_tensor - 1)
        def _():
            for g in (1, 2):
                column(g, near(1))

        return carry

    lax.fori_loop(0, n_tensor + 1, first, 0)
    for k in range(6):
        vectors[pl.ds(k, 1), :] = gathered(small_all[:, k + 1, :], v_spread, v_owned)

    for g in (1, 2):
        column_z(g, near(2))
        column(g, near(2))
    for g in (1, 2):
        sides(g, z)
    for g in (1, 2):
        corner(g, z)
    for g in (1, 2):
        column_z(g, near(3))
        column(g, near(3))

    def second(j, carry):
        for g in (1, 2):
            sides(g, near(j))

        @pl.when(j == 1)
        def _():
            for g in (1, 2):
                corner(g, near(1))

        return carry

    lax.fori_loop(1, n_tensor - 1, second, 0)
    here.wait()
    for j in range(n_ctx):
        for k in range(n_tensor):
            if j or k:
                from_token(lax.rem(ctx + j, n_ctx) * n_tensor + lax.rem(z + k, n_tensor)).wait_recv()

    n_blocks = n_ctx * n_tensor
    total_rows = n_blocks * span
    n_units = n_blocks // 2

    def to_tokens(block):
        c, t = lax.div(block, n_tensor), lax.rem(block, n_tensor)
        return remote(send_mixed.at[block], mixed.at[z * n_ctx + ctx], m_send.at[block],
                      m_recv.at[z * n_ctx + ctx], at(dp, c, t))

    def keep(i):
        return pltpu.make_async_copy(probs.at[:, pl.ds(i * 2 * span, 2 * span)],
                                     probs_out.at[:, pl.ds(i * 2 * span, 2 * span)], p_sem.at[i])

    own_block = ctx * n_tensor + z
    own_mixed = pltpu.make_async_copy(send_mixed.at[own_block], mixed.at[z * n_ctx + ctx], own_sem.at[4])

    def attend(i, carry):
        blocks = pl.ds(2 * i, 2)
        lines = pl.ds(pl.multiple_of(i * 2 * span, 2 * span), 2 * span)
        allowed = seg_col[lines, :] == seg_row[...]
        for h in range(heads):
            q = rows[blocks, :, pl.ds(HEAD_DIM * h, HEAD_DIM)].reshape(2 * span, HEAD_DIM)
            k = rows[:, :, pl.ds(HEAD_DIM * (heads + h), HEAD_DIM)].reshape(total_rows, HEAD_DIM)
            v = rows[:, :, pl.ds(HEAD_DIM * (2 * heads + h), HEAD_DIM)].reshape(total_rows, HEAD_DIM)
            scores = SCALE * lax.dot_general(q, k, (((1,), (1,)), ((), ())), preferred_element_type=F32)
            scores = jnp.where(allowed, scores, NEG)
            weights = jnp.exp(scores - jnp.max(scores, axis=-1, keepdims=True))
            low = (weights * (1.0 / jnp.sum(weights, axis=-1, keepdims=True))).astype(BF16)
            probs[h, lines, :] = low
            value = jnp.dot(low, v, preferred_element_type=F32)
            mixed_float[lines, pl.ds(HEAD_DIM * h, HEAD_DIM)] = value
            send_mixed[blocks, :, pl.ds(HEAD_DIM * h, HEAD_DIM)] = value.astype(BF16).reshape(2, span, HEAD_DIM)
        keep(i).start()
        for n in range(2):
            @pl.when(2 * i + n != own_block)
            def _():
                to_tokens(2 * i + n).start()

            @pl.when(2 * i + n == own_block)
            def _():
                own_mixed.start()

        return carry

    lax.fori_loop(0, n_units, attend, 0)

    last = n_tensor - 1
    for g in (1, 2):
        sides(g, near(last))
    for g in (1, 2):
        corner(g, near(last - 1))

    own_mixed.wait()
    for j in range(n_ctx):
        for k in range(n_tensor):
            if j or k:
                c, t = lax.rem(ctx + j, n_ctx), lax.rem(z + k, n_tensor)
                slot = t * n_ctx + c
                remote(mixed.at[slot], mixed.at[slot], m_send.at[0], m_recv.at[slot], x_dev).wait_recv()

    flip = (((1,), (1,)), ((), ()))
    total[...] = x[...].astype(F32) + vectors[pl.ds(0, 1), :]

    def add_merge(t, carry):
        value = mixed[pl.ds(t * n_ctx, n_ctx)].reshape(count, part_width)
        total[...] += lax.dot_general(value, whole(f0, t)[:, wide:], flip, preferred_element_type=F32)
        return carry

    lax.fori_loop(0, n_tensor, add_merge, 0)
    normal[0], scale[0] = normalize(total[...])
    value = normal[0] * vectors[pl.ds(1, 1), :] + vectors[pl.ds(2, 1), :]
    total[...] = value + vectors[pl.ds(3, 1), :]
    first_low[...] = value.astype(BF16)
    for g in (1, 2):
        corner(g, near(last))
        own[g].wait()

    def units(t):
        for g in (1, 2):
            partner(g, t)
        bias = gathered(small_all[pl.ds(t * 8, 8), 7, :], e_spread, e_owned)
        before = jnp.dot(first_low[...], whole(f1, t), preferred_element_type=F32) + bias
        value, rise = gelu_exact(before)
        low = value.astype(BF16)
        active[t] = low
        slope[t] = rise
        total[...] += lax.dot_general(low, whole(f2, t), flip, preferred_element_type=F32)

    def third(j, carry):
        units(near(j))
        return carry

    lax.fori_loop(0, n_tensor, third, 0)

    normal[1], scale[1] = normalize(total[...])
    gain = vectors[pl.ds(4, 1), :]
    outputs[...] = normal[1] * gain + vectors[pl.ds(5, 1), :]
    pull = cotangent[...].astype(F32)
    small_grads[:, 0, :] = jnp.zeros_like(small_grads[:, 0, :])
    small_grads[:, 5, :] = scattered(total_rows_of(pull * normal[1]), v_spread, v_owned)
    small_grads[:, 6, :] = scattered(total_rows_of(pull), v_spread, v_owned)
    second_grad = normalize_back(pull, normal[1], scale[1], gain)
    small_grads[:, 4, :] = scattered(total_rows_of(second_grad), v_spread, v_owned)
    total[...] = second_grad
    second_low[...] = second_grad.astype(BF16)
    turned[0] = second_low[...].T
    turned[1] = first_low[...].T
    blocked = (2, 2, 2, n_rows, g1.shape[-1])

    def store(which, t):
        grad, out = ((g1, g1_out), (g2, g2_out))[which]
        return pltpu.make_async_copy(grad.at[t], out.at[t], g_sem.at[which, t])

    def units_back(t, carry):
        low = active[t]
        g2[t] = jnp.dot(turned[0], low, preferred_element_type=F32).astype(BF16).reshape(blocked)
        store(1, t).start()
        back = jnp.dot(second_low[...], whole(f2, t), preferred_element_type=F32) * slope[t]
        back_low = back.astype(BF16)
        sums = total_rows_of(back_low.astype(F32))
        small_grads[pl.ds(t * 8, 8), 7, :] = scattered(sums, e_spread, e_owned)
        g1[t] = jnp.dot(turned[1], back_low, preferred_element_type=F32).astype(BF16).reshape(blocked)
        store(0, t).start()
        total[...] += lax.dot_general(back_low, whole(f1, t), flip, preferred_element_type=F32)
        return carry

    lax.fori_loop(0, n_tensor, units_back, 0)
    pull = total[...]
    small_grads[:, 2, :] = scattered(total_rows_of(pull * normal[0]), v_spread, v_owned)
    small_grads[:, 3, :] = scattered(total_rows_of(pull), v_spread, v_owned)
    value = normalize_back(pull, normal[0], scale[0], vectors[pl.ds(1, 1), :])
    small_grads[:, 1, :] = scattered(total_rows_of(value), v_spread, v_owned)
    first_grad[...] = value
    first_low_grad[...] = value.astype(BF16)

    for j in range(n_ctx):
        for k in range(n_tensor):
            if j or k:
                c, t = lax.rem(ctx + j, n_ctx), lax.rem(z + k, n_tensor)
                to_tokens(c * n_tensor + t).wait_send()
                to_heads(t, c).wait_send()
    for i in range(n_units):
        keep(i).wait()

    def finish(origin, carry):
        for g in range(3):
            for kind in range(4):
                core(g, origin, kind, slots[kind]).wait_send()
            along(g, origin, me, x_send, x_recv, x_dev).wait_send()
            along(g, origin, me, y_send, y_recv, y_dev).wait_send()
            part(g, origin, x_slot, 0, a_send, a_recv, y_dev).wait_send()
            part(g, origin, y_slot, half, b_send, b_recv, x_dev).wait_send()

            @pl.when((origin <= z) & up_ok)
            def _():
                up(g, origin).wait_send()

            @pl.when((origin >= z) & down_ok)
            def _():
                down(g, origin).wait_send()
        for which in range(2):
            store(which, origin).wait()
        return carry

    lax.fori_loop(0, n_tensor, finish, 0)


def forward_layer(n_tensor, heads, x, cotangent, triple, merge, w1, shrink, small, matrices, seg_row, seg_col):
    rows, cols = w1.shape
    count, width = x.shape
    n_small = 8 * n_tensor
    blocks = 2 * n_tensor
    span = count // 2
    length = blocks * span
    part = heads * HEAD_DIM
    dma = pltpu.SemaphoreType.DMA
    shape = jax.ShapeDtypeStruct
    full = (n_tensor, 8, rows, cols)
    split = (n_tensor, 2, 2, 2, rows, cols)
    pair = [dma((3, n_tensor)), dma((3, n_tensor))]
    vmem = pl.BlockSpec(memory_space=pltpu.VMEM)
    hbm = pl.BlockSpec(memory_space=pl.ANY)
    return pl.pallas_call(
        functools.partial(forward_kernel, n_tensor, heads),
        out_shape=(
            shape(full, BF16), shape((blocks, span, 3 * part), BF16),
            shape((length, part), F32), shape((heads, length, length), BF16), shape((blocks, span, part), BF16),
            shape((count, width), F32), shape((count, width), BF16), shape((count, width), BF16),
            shape((count, width), F32), shape((n_small,) + small.shape, F32), shape(split, BF16), shape(split, BF16),
        ),
        in_specs=[vmem] * 15,
        out_specs=(vmem, vmem, vmem, hbm) + (vmem,) * 6 + (hbm, hbm),
        scratch_shapes=[
            pltpu.VMEM((rows, cols), BF16),
            pltpu.VMEM((rows, cols), BF16),
            pltpu.VMEM(full, BF16),
            pltpu.VMEM(full, BF16),
            pltpu.VMEM((n_small,) + small.shape, F32),
            pltpu.VMEM((n_tensor, 2, span, 3 * part), BF16),
            pltpu.VMEM((blocks, span, part), BF16),
            pltpu.VMEM((heads, length, length), BF16),
            pltpu.VMEM((8, width), F32),
            pltpu.VMEM((2, count, width), F32),
            pltpu.VMEM((2, count, 1), F32),
            pltpu.VMEM((n_tensor, count, cols), BF16),
            pltpu.VMEM((n_tensor, count, cols), F32),
            pltpu.VMEM((count, width), F32),
            pltpu.VMEM((count, width), BF16),
            pltpu.VMEM((2, width, count), BF16),
            pltpu.VMEM(split, BF16),
            pltpu.VMEM(split, BF16),
            dma((5,)), dma((3, n_tensor)),
        ] + pair * 5 + [
            dma((3, 4, n_tensor)), dma((3, 4, n_tensor)), dma((n_small,)), dma((n_small,)),
            dma((n_tensor, 2)), dma((blocks,)), dma((blocks,)), dma((blocks,)), dma((blocks // 2,)),
            dma((2, n_tensor)),
        ],
        compiler_params=pltpu.CompilerParams(collective_id=0, has_side_effects=True, vmem_limit_bytes=60 << 20),
        cost_estimate=pl.CostEstimate(flops=0, bytes_accessed=w1.size * 400, transcendentals=0),
        name="forward_layer",
    )(x, cotangent, triple, merge, w1, shrink, small, *matrices, seg_row, seg_col)


def far(n_tensor, j):
    return in_order(lambda t, here: (-abs(t - here), t), n_tensor, j)


def sum_steps(n_tensor, grads, acc, core_in, y1_in, x1_in, x2_in, y2_in, up_in, down_in, load_sem, c_send, c_recv,
              y1_send, y1_recv, x1_send, x1_recv, x2_send, x2_recv, y2_send, y2_recv, up_send, up_recv, down_send, down_recv):
    dp, ctx, z = (lax.axis_index(a) for a in ALL)
    rows = acc.shape[-2]
    half = rows // 2
    core = lax.rem(dp, 2)
    x = lax.div(dp, 2)
    xp, yp = 1 - x, 1 - ctx
    x_dev, y_dev, c_dev = at(xp * 2 + core, ctx, z), at(dp, yp, z), at(x * 2 + 1 - core, ctx, z)
    low, high = pl.ds(0, half), pl.ds(half, half)
    count = range(len(grads))

    def load(g, t):
        return pltpu.make_async_copy(grads[g].at[t, :, core], acc.at[g, t], load_sem.at[g, t])

    def to_core(g, t):
        return remote(grads[g].at[t, :, 1 - core], core_in.at[g, t], c_send.at[g, t], c_recv.at[g, t], c_dev)

    def y1(g, t):
        return remote(acc.at[g, t, :, yp, low], y1_in.at[g, t], y1_send.at[g, t], y1_recv.at[g, t], y_dev)

    def x1(g, t):
        return remote(acc.at[g, t, xp, :, high], x1_in.at[g, t], x1_send.at[g, t], x1_recv.at[g, t], x_dev)

    def x2(g, t):
        return remote(acc.at[g, t, xp, ctx, low], x2_in.at[g, t], x2_send.at[g, t], x2_recv.at[g, t], x_dev)

    def y2(g, t):
        return remote(acc.at[g, t, x, yp, high], y2_in.at[g, t], y2_send.at[g, t], y2_recv.at[g, t], y_dev)

    up_dev, down_dev = at(dp, ctx, jnp.minimum(z + 1, n_tensor - 1)), at(dp, ctx, jnp.maximum(z - 1, 0))

    def up(g, t):
        return remote(acc.at[g, t, x, ctx], up_in.at[g, t], up_send.at[g, t], up_recv.at[g, t], up_dev)

    def down(g, t):
        return remote(acc.at[g, t, x, ctx], down_in.at[g, t], down_send.at[g, t], down_recv.at[g, t], down_dev)

    def add(a, b):
        return (a.astype(F32) + b.astype(F32)).astype(BF16)

    def target(j):
        return far(n_tensor, j)

    def begin(j):
        t = target(j)
        for g in count:
            to_core(g, t).start()
            load(g, t).start()

    def core_step(j):
        t = target(j)
        for g in count:
            load(g, t).wait()
            to_core(g, t).wait_recv()
            acc[g, t] = add(acc[g, t], core_in[g, t])
            y1(g, t).start()
            x1(g, t).start()

    def first_step(j):
        t = target(j)
        for g in count:
            y1(g, t).wait_recv()
            for i in range(2):
                acc[g, t, i, ctx, low] = add(acc[g, t, i, ctx, low], y1_in[g, t, i])
            x2(g, t).start()
            x1(g, t).wait_recv()
            for i in range(2):
                acc[g, t, x, i, high] = add(acc[g, t, x, i, high], x1_in[g, t, i])
            y2(g, t).start()

    def second_step(j):
        t = target(j)
        for g in count:
            x2(g, t).wait_recv()
            acc[g, t, x, ctx, low] = add(acc[g, t, x, ctx, low], x2_in[g, t])
            y2(g, t).wait_recv()
            acc[g, t, x, ctx, high] = add(acc[g, t, x, ctx, high], y2_in[g, t])

    def third_step(j):
        t = target(j)
        for g in count:
            @pl.when((t >= z) & (z > 0))
            def _():
                up(g, t).wait_recv()
                acc[g, t, x, ctx] = add(acc[g, t, x, ctx], up_in[g, t])

            @pl.when((t <= z) & (z < n_tensor - 1))
            def _():
                down(g, t).wait_recv()
                acc[g, t, x, ctx] = add(acc[g, t, x, ctx], down_in[g, t])

            @pl.when(t > z)
            def _():
                up(g, t).start()

            @pl.when(t < z)
            def _():
                down(g, t).start()

    def end(outs):
        for g in count:
            outs[g][...] = acc[g, z, x, ctx].astype(F32)

        def finish(t, carry):
            for g in count:
                for copy in (to_core, y1, x1, x2, y2):
                    copy(g, t).wait_send()

                @pl.when(t > z)
                def _():
                    up(g, t).wait_send()

                @pl.when(t < z)
                def _():
                    down(g, t).wait_send()
            return carry

        lax.fori_loop(0, n_tensor, finish, 0)

    return begin, core_step, first_step, second_step, third_step, end


def sum_scratch(n_grads, n_tensor, rows, cols):
    dma = pltpu.SemaphoreType.DMA
    grid = (n_grads, n_tensor)
    half = rows // 2
    return [
        pltpu.VMEM(grid + (2, 2, rows, cols), BF16),
        pltpu.VMEM(grid + (2, 2, rows, cols), BF16),
        pltpu.VMEM(grid + (2, half, cols), BF16),
        pltpu.VMEM(grid + (2, half, cols), BF16),
        pltpu.VMEM(grid + (half, cols), BF16),
        pltpu.VMEM(grid + (half, cols), BF16),
        pltpu.VMEM(grid + (rows, cols), BF16),
        pltpu.VMEM(grid + (rows, cols), BF16),
    ] + [dma(grid)] * 15


def backward_kernel(n_tensor, heads, first_low, first_grad, x, f0, mixed, small, spread, owned, rows, mixed_float,
                    probs_in, g1, g2, input_grad, o0, o1, o2, small_out,
                    turned, g0, mixed_grad, grad, probs, send_rows, qkv_grad, key_sum, value_sum, small_send, small_in,
                    own_sem, g_send, g_recv, q_send, q_recv, p_sem, s_send, s_recv, *scratch):
    dp, ctx, z = (lax.axis_index(a) for a in ALL)
    n_ctx = 2
    n_blocks = n_ctx * n_tensor
    n_units = n_blocks // 2
    span = grad.shape[1]
    part = grad.shape[2]
    wide = 3 * part
    n_rows, width = f0.shape[-2:]
    total_rows = n_blocks * span
    own_block = ctx * n_tensor + z
    own_slot = z * n_ctx + ctx
    mine = z * 8 + dp * 2 + ctx
    peers = everyone(4, 2, n_tensor)
    greet([at(*p) for p in peers])
    others = [(lax.rem(ctx + j, n_ctx), lax.rem(z + k, n_tensor))
              for k in (2, 3, 1, 0) for j in range(n_ctx) if (j or k) and k < n_tensor]
    half = len(scratch) // 2
    begin, core_step, first_step, second_step, third_step, end = sum_steps(n_tensor, (g1, g2), *scratch[:half])
    begin_last, core_last, first_last, second_last, third_last, end_last = sum_steps(n_tensor, (g0,), *scratch[half:])

    def to_heads(c, t):
        return remote(mixed_grad.at[t * n_ctx + c], grad.at[own_block], g_send.at[t * n_ctx + c],
                      g_recv.at[own_block], at(dp, c, t))

    def load(i):
        lines = pl.ds(i * 2 * span, 2 * span)
        return pltpu.make_async_copy(probs_in.at[:, lines], probs.at[:, lines], p_sem.at[i])

    here = pltpu.make_async_copy(mixed_grad.at[own_slot], grad.at[own_block], own_sem.at[0])

    def begin_all(j, carry):
        begin(j)
        return carry

    lax.fori_loop(0, n_tensor, begin_all, 0)

    def spread_grad(j, carry):
        t = far(n_tensor, j)
        weight = f0[t].reshape(8 * n_rows, width)[:, wide:]
        value = jnp.dot(first_low[...], weight, preferred_element_type=F32).astype(BF16)
        mixed_grad[pl.ds(t * n_ctx, n_ctx)] = value.reshape(n_ctx, span, part)
        to_heads(1 - ctx, t).start()

        @pl.when(t != z)
        def _():
            to_heads(ctx, t).start()

        @pl.when(t == z)
        def _():
            here.start()

        return carry

    lax.fori_loop(0, n_tensor, spread_grad, 0)
    for i in range(n_units):
        load(i).start()

    core_step(0)
    core_step(1)
    here.wait()
    for c, t in others:
        block = c * n_tensor + t
        remote(grad.at[block], grad.at[block], g_send.at[0], g_recv.at[block], at(dp, c, t)).wait_recv()
    for i in range(n_units):
        load(i).wait()

    def one_head(h):
        lanes = pl.ds(HEAD_DIM * h, HEAD_DIM)
        k_lanes = pl.ds(HEAD_DIM * (heads + h), HEAD_DIM)
        v_lanes = pl.ds(HEAD_DIM * (2 * heads + h), HEAD_DIM)
        key_sum[...] = jnp.zeros_like(key_sum)
        value_sum[...] = jnp.zeros_like(value_sum)

        def unit(i, carry):
            blocks = pl.ds(2 * i, 2)
            lines = pl.ds(pl.multiple_of(i * 2 * span, 2 * span), 2 * span)
            q = rows[blocks, :, lanes].reshape(2 * span, HEAD_DIM)
            k = rows[:, :, k_lanes].reshape(total_rows, HEAD_DIM)
            v = rows[:, :, v_lanes].reshape(total_rows, HEAD_DIM)
            up = grad[blocks, :, lanes].reshape(2 * span, HEAD_DIM)
            low = probs[h, lines, :]
            delta = jnp.sum(up.astype(F32) * mixed_float[lines, lanes], axis=-1, keepdims=True)
            pull = lax.dot_general(up, v, (((1,), (1,)), ((), ())), preferred_element_type=F32)
            score = (low.astype(F32) * (pull - delta)).astype(BF16)
            query = SCALE * jnp.dot(score, k, preferred_element_type=F32)
            send_rows[blocks, :, lanes] = query.astype(BF16).reshape(2, span, HEAD_DIM)
            key_sum[...] += lax.dot_general(q, score, (((0,), (0,)), ((), ())), preferred_element_type=F32)
            value_sum[...] += lax.dot_general(up, low, (((0,), (0,)), ((), ())), preferred_element_type=F32)
            return carry

        lax.fori_loop(0, n_units, unit, 0)
        key = (SCALE * key_sum[...]).T.astype(BF16)
        value = value_sum[...].T.astype(BF16)
        send_rows[:, :, k_lanes] = key.reshape(n_blocks, span, HEAD_DIM)
        send_rows[:, :, v_lanes] = value.reshape(n_blocks, span, HEAD_DIM)

    for h in range(heads):
        one_head(h)
        if h < 2:
            core_step(h + 2)

    def to_tokens(c, t):
        return remote(send_rows.at[c * n_tensor + t], qkv_grad.at[own_slot], q_send.at[c * n_tensor + t],
                      q_recv.at[own_slot], at(dp, c, t))

    there = pltpu.make_async_copy(send_rows.at[own_block], qkv_grad.at[own_slot], own_sem.at[1])

    def send_back(j, carry):
        t = far(n_tensor, j)
        to_tokens(1 - ctx, t).start()

        @pl.when(t != z)
        def _():
            to_tokens(ctx, t).start()

        @pl.when(t == z)
        def _():
            there.start()

        return carry

    lax.fori_loop(0, n_tensor, send_back, 0)

    turned[0] = first_low[...].T
    turned[1] = x[...].T
    small_send[...] = small[...]

    def merge_grad(t, carry):
        value = jnp.dot(turned[0], mixed[pl.ds(t * n_ctx, n_ctx)].reshape(n_ctx * span, part),
                        preferred_element_type=F32)
        g0[t, :, :, :, :, pl.ds(wide, part)] = value.astype(BF16).reshape(2, 2, 2, n_rows, part)
        return carry

    def rest(j, carry):
        @pl.when(j < n_tensor)
        def _():
            first_step(j)
            merge_grad(j, 0)

        @pl.when((j >= 2) & (j < n_tensor + 2))
        def _():
            second_step(j - 2)

        @pl.when(j >= 3)
        def _():
            third_step(j - 3)

        return carry

    lax.fori_loop(0, n_tensor + 3, rest, 0)

    def arrived(t, c):
        slot = t * n_ctx + c
        remote(qkv_grad.at[slot], qkv_grad.at[slot], q_send.at[0], q_recv.at[slot], at(dp, c, t)).wait_recv()

    def weight_grad(j):
        t = far(n_tensor, j)
        arrived(t, 1 - ctx)

        @pl.when(t != z)
        def _():
            arrived(t, ctx)

        @pl.when(t == z)
        def _():
            there.wait()

        pull = qkv_grad[pl.ds(t * n_ctx, n_ctx)].reshape(n_ctx * span, wide)
        value = jnp.dot(turned[1], pull, preferred_element_type=F32)
        g0[t, :, :, :, :, pl.ds(0, wide)] = value.astype(BF16).reshape(2, 2, 2, n_rows, wide)
        begin_last(j)
        small_send[pl.ds(t * 8, 8), 0, :] = scattered(total_rows_of(pull.astype(F32)), spread, owned)

    def weight_grads(j, carry):
        @pl.when(j < n_tensor)
        def _():
            weight_grad(j)

        @pl.when(j >= 1)
        def _():
            core_last(j - 1)

        return carry

    lax.fori_loop(0, n_tensor + 1, weight_grads, 0)
    small_copies = [
        remote(small_send.at[pt * 8 + pd * 2 + pc], small_in.at[n], s_send.at[n], s_recv.at[n], at(pd, pc, pt))
        for n, (pd, pc, pt) in enumerate(peers)
    ]
    for copy in small_copies:
        copy.start()
    input_grad[...] = first_grad[...]

    def add_input(j):
        pull = qkv_grad[pl.ds(j * n_ctx, n_ctx)].reshape(n_ctx * span, wide)
        weight = f0[j].reshape(8 * n_rows, width)[:, :wide]
        input_grad[...] += lax.dot_general(pull, weight, (((1,), (1,)), ((), ())), preferred_element_type=F32)

    def last(j, carry):
        @pl.when(j < n_tensor)
        def _():
            first_last(j)

        @pl.when((j >= 1) & (j < n_tensor + 1))
        def _():
            second_last(j - 1)

        @pl.when(j >= 2)
        def _():
            third_last(j - 2)

        @pl.when(j < n_tensor)
        def _():
            add_input(j)

        return carry

    lax.fori_loop(0, n_tensor + 2, last, 0)
    end((o1, o2))
    end_last((o0,))
    total = small_send[mine]
    for n in range(len(peers)):
        small_copies[n].wait()
        total = total + small_in[n]
    small_out[...] = total
    for c, t in others:
        to_tokens(c, t).wait_send()
        to_heads(c, t).wait_send()


def backward_attention(n_tensor, heads, first_low, first_grad, x, f0, mixed, small, spread, owned, rows, mixed_float,
                       probs, g1, g2):
    blocks, span, wide = rows.shape
    part = heads * HEAD_DIM
    length = blocks * span
    n_rows, cols = g1.shape[-2:]
    n_small = 8 * n_tensor
    dma = pltpu.SemaphoreType.DMA
    vmem = pl.BlockSpec(memory_space=pltpu.VMEM)
    hbm = pl.BlockSpec(memory_space=pl.ANY)
    shape = jax.ShapeDtypeStruct
    out = shape((n_rows, cols), F32)
    return pl.pallas_call(
        functools.partial(backward_kernel, n_tensor, heads),
        out_shape=(shape(first_grad.shape, F32), out, out, out, shape(small.shape[1:], F32)),
        in_specs=[vmem] * 10 + [hbm] * 3,
        out_specs=(vmem,) * 5,
        scratch_shapes=[
            pltpu.VMEM((2,) + x.shape[::-1], BF16),
            pltpu.VMEM(g1.shape, BF16),
            pltpu.VMEM((blocks, span, part), BF16),
            pltpu.VMEM((blocks, span, part), BF16),
            pltpu.VMEM((heads, length, length), BF16),
            pltpu.VMEM((blocks, span, wide), BF16),
            pltpu.VMEM((blocks, span, wide), BF16),
            pltpu.VMEM((HEAD_DIM, length), F32),
            pltpu.VMEM((HEAD_DIM, length), F32),
            pltpu.VMEM(small.shape, F32),
            pltpu.VMEM((n_small - 1,) + small.shape[1:], F32),
            dma((2,)), dma((blocks,)), dma((blocks,)), dma((blocks,)), dma((blocks,)), dma((blocks // 2,)),
            dma((n_small - 1,)), dma((n_small - 1,)),
        ] + sum_scratch(2, n_tensor, n_rows, cols) + sum_scratch(1, n_tensor, n_rows, cols),
        compiler_params=pltpu.CompilerParams(collective_id=2, has_side_effects=True, vmem_limit_bytes=58 << 20),
        cost_estimate=pl.CostEstimate(flops=0, bytes_accessed=g1.size * 24, transcendentals=0),
        name="backward_attention",
    )(first_low, first_grad, x, f0, mixed, small, spread, owned, rows, mixed_float, probs, g1, g2)


def norm_rows(total, gain, shift):
    center = total - jnp.mean(total, axis=-1, keepdims=True)
    spread = jnp.mean(center * center, axis=-1, keepdims=True)
    return center * lax.rsqrt(spread + EPS) * gain + shift


def gelu_exact(before):
    share = 0.5 + 0.5 * lax.erf(before * 0.5**0.5)
    dense = (0.5 / np.pi) ** 0.5 * jnp.exp(-0.5 * before * before)
    return before * share, share + before * dense


def dot(spec, a, b):
    return jnp.einsum(spec, a, b, preferred_element_type=F32)


def add_up(spec, a, b):
    return sum(dot(spec, a[t], b[t]) for t in range(a.shape[0]))


def local(
    inputs,
    cotangent,
    segments,
    triple_weight,
    attend_bias,
    merge_weight,
    merge_bias,
    first_gain,
    first_shift,
    expand_weight,
    expand_bias,
    shrink_weight,
    shrink_bias,
    second_gain,
    second_shift,
):
    n_dp, n_ctx, n_tensor = (lax.axis_size(a) for a in ALL)
    span, batch, width = inputs.shape
    rows = triple_weight.shape[1]
    part = triple_weight.shape[2]
    units = expand_weight.shape[1]
    owners = n_dp * n_ctx
    heads = part // HEAD_DIM
    count = batch * span
    small_part = part // owners
    unit_part = units // owners
    own_kernels = n_dp == 4 and n_ctx == 2 and batch == 2 and n_tensor == 4 and rows % 32 == 0

    narrow_in = (merge_bias, first_gain, first_shift, shrink_bias, second_gain, second_shift)
    x_low = jnp.transpose(inputs, (1, 0, 2)).reshape(count, width)
    cotangent_rows = jnp.transpose(cotangent, (1, 0, 2)).reshape(count, width)
    here = lax.axis_index("ctx")
    if own_kernels:
        labels = lax.dynamic_slice_in_dim(segments, here, 1, 0)
        lines = [attend_bias.reshape(1, -1)] + list(narrow_in) + [expand_bias]
        small = sum(
            jnp.pad(v.astype(F32), ((n, 7 - n), (0, 128 - v.shape[1]))) for n, v in enumerate(lines)
        )
        matrices = tables(n_tensor, owners, part, units)
        (f0, rows_all, mixed_float, probs, mixed, outputs_rows, first_low, first_low_grad, first_grad, small_grads,
         expand_grad, shrink_grad) = forward_layer(
            n_tensor, heads, x_low, cotangent_rows, triple_weight, merge_weight, expand_weight, shrink_weight, small,
            matrices, labels, labels.reshape(-1, 1)
        )
        inputs_gradient, r0, r1, r2, small_sum = backward_attention(
            n_tensor, heads, first_low_grad, first_grad, x_low, f0, mixed, small_grads, *matrices[:2],
            rows_all, mixed_float, probs, expand_grad, shrink_grad
        )
        narrow_out = [small_sum[:1, :small_part], small_sum[:1, small_part : 2 * small_part]]
        narrow_out += [small_sum[n : n + 1, :small_part] for n in range(1, 7)]
        expand_out = small_sum[7:, :unit_part]
    else:
        pieces = [attend_bias[0, 0], attend_bias[1, 0]] + [v[0] for v in narrow_in] + [expand_bias[0]]
        w0 = jnp.concatenate(
            [jnp.transpose(triple_weight, (1, 0, 2)).reshape(rows, 3 * part), merge_weight.T], axis=1
        )
        small = jnp.concatenate(pieces).astype(F32)
        f0, f1, f2 = (
            lax.all_gather(lax.all_gather(w, ("dp", "ctx"), axis=0, tiled=True), "tensor", axis=0, tiled=False)
            for w in (w0, expand_weight, shrink_weight.T)
        )
        small_all = lax.all_gather(lax.all_gather(small, ("dp", "ctx")), "tensor")
        f0, w_expand, w_shrink = (w.reshape(n_tensor, width, -1) for w in (f0, f1, f2))
        w_qkv, w_merge = f0[:, :, : 3 * part], f0[:, :, 3 * part :]
        narrow = small_all[:, :, : 8 * small_part].reshape(n_tensor, owners, 8, small_part)
        narrow = jnp.transpose(narrow, (2, 0, 1, 3)).reshape(8, n_tensor, part)
        merge_vec, gain_one, shift_one, shrink_vec, gain_two, shift_two = narrow[2:].reshape(6, width)
        expand_vec = small_all[:, :, 8 * small_part :].reshape(n_tensor, 1, units)
        qkv_vec = jnp.concatenate([narrow[0], jnp.zeros_like(narrow[0]), narrow[1]], axis=-1)[:, None]
        x = x_low.astype(F32)
        upstream = cotangent_rows.astype(F32)

        def to_tokens(value):
            value = value.reshape(batch, n_tensor, span, -1)
            out = lax.all_to_all(jnp.transpose(value, (1, 0, 2, 3)), "tensor", split_axis=0, concat_axis=0)
            return out.reshape(n_tensor, count, -1)

        qkv = (dot("rd,tde->tre", x_low, w_qkv) + qkv_vec).astype(BF16)
        mine = lax.all_to_all(
            qkv.reshape(n_tensor, batch, span, 3 * part), "tensor", split_axis=0, concat_axis=0
        )
        mine = jnp.transpose(mine, (1, 0, 2, 3)).reshape(batch, n_tensor * span, 3 * part)
        n_query = n_tensor * span
        own_labels = lax.dynamic_slice_in_dim(segments, here * n_query, n_query, 1)
        kv_rows = lax.all_gather(mine[..., part:], "ctx", axis=1, tiled=True)
        n_key = kv_rows.shape[1]
        q_four = mine[..., :part].reshape(batch, n_query, heads, HEAD_DIM)
        k_four = kv_rows[..., :part].reshape(batch, n_key, heads, HEAD_DIM)
        v_four = kv_rows[..., part:].reshape(batch, n_key, heads, HEAD_DIM)
        allowed = own_labels[:, None, :, None] == segments[:, None, None, :]
        scores = jnp.where(allowed, SCALE * dot("sqhd,skhd->shqk", q_four, k_four), NEG)
        top = jnp.max(scores, axis=-1)
        weights = jnp.where(allowed, jnp.exp(scores - top[..., None]), 0.0)
        total = jnp.sum(weights, axis=-1)
        mixed_float = dot("shqk,skhd->shqd", weights.astype(BF16), v_four) / total[..., None]
        logsum = top + jnp.log(total)
        mixed = to_tokens(jnp.transpose(mixed_float, (0, 2, 1, 3)).reshape(batch, n_query, part).astype(BF16))
        first_sum = x + add_up("re,de->rd", mixed, w_merge) + merge_vec
        first_norm = norm_rows(first_sum, gain_one, shift_one)
        first_low = first_norm.astype(BF16)
        before = dot("rd,tdf->trf", first_low, w_expand) + expand_vec
        active, slope = gelu_exact(before)
        active = active.astype(BF16)
        second_sum = first_norm + add_up("rf,df->rd", active, w_shrink) + shrink_vec
        outputs_rows = norm_rows(second_sum, gain_two, shift_two)

        second_grad, gain_two_grad, shift_two_grad = jax.vjp(norm_rows, second_sum, gain_two, shift_two)[1](upstream)
        shrink_vec_grad = jnp.sum(second_grad, axis=0)
        second_low = second_grad.astype(BF16)
        shrink_grad = dot("rd,trf->tdf", second_low, active).astype(BF16)
        active_grad = dot("rd,tdf->trf", second_low, w_shrink)
        before_low = (active_grad * slope).astype(BF16)
        expand_vec_grad = jnp.sum(before_low.astype(F32), axis=1)
        expand_grad = dot("rd,trf->tdf", first_low, before_low).astype(BF16)
        norm_back = add_up("rf,df->rd", before_low, w_expand)
        first_grad, gain_one_grad, shift_one_grad = jax.vjp(norm_rows, first_sum, gain_one, shift_one)[1](
            second_grad + norm_back
        )
        merge_vec_grad = jnp.sum(first_grad, axis=0)
        first_low_grad = first_grad.astype(BF16)
        vec_grads = jnp.stack(
            [merge_vec_grad, gain_one_grad, shift_one_grad, shrink_vec_grad, gain_two_grad, shift_two_grad]
        ).reshape(6, n_tensor, owners, small_part)
        vec_grads = jnp.transpose(vec_grads, (1, 2, 0, 3)).reshape(n_tensor, owners, 6 * small_part)
        small_grads = jnp.concatenate([vec_grads, expand_vec_grad.reshape(n_tensor, owners, unit_part)], axis=-1)
        merge_grad = dot("rd,tre->tde", first_low_grad, mixed).astype(BF16)
        mixed_grad = dot("rd,tde->tre", first_low_grad, w_merge).astype(BF16)
        grad_rows = lax.all_to_all(
            mixed_grad.reshape(n_tensor, batch, span, part), "tensor", split_axis=0, concat_axis=0
        )
        grad_four = jnp.transpose(grad_rows, (1, 0, 2, 3)).reshape(batch, n_query, heads, HEAD_DIM)
        delta = jnp.sum(jnp.transpose(grad_four.astype(F32), (0, 2, 1, 3)) * mixed_float, axis=-1)
        back_scores = SCALE * dot("sqhd,skhd->shqk", q_four, k_four)
        probs = jnp.where(allowed, jnp.exp(back_scores - logsum[..., None]), 0.0)
        prob_grad = dot("sqhd,skhd->shqk", grad_four, v_four)
        score_low = (probs * (prob_grad - delta[..., None])).astype(BF16)
        value_part = dot("shqk,sqhd->skhd", probs.astype(BF16), grad_four)
        query_part = SCALE * dot("shqk,skhd->sqhd", score_low, k_four)
        key_part = SCALE * dot("shqk,sqhd->skhd", score_low, q_four)
        query_part, key_part, value_part = (
            v.reshape(batch, -1, part).astype(BF16) for v in (query_part, key_part, value_part)
        )
        key_part, value_part = (
            lax.psum_scatter(v, "ctx", scatter_dimension=1, tiled=True) for v in (key_part, value_part)
        )
        qkv_grad = to_tokens(jnp.concatenate([query_part, key_part, value_part], axis=-1))
        triple_grad = dot("rd,tre->tde", x_low, qkv_grad).astype(BF16)
        attend_grad = jnp.sum(qkv_grad.astype(F32), axis=1).reshape(n_tensor, 3, owners, small_part)
        inputs_gradient = first_grad + add_up("re,de->rd", qkv_grad, w_qkv)
        small_grads = jnp.concatenate([attend_grad[:, 0], attend_grad[:, 2], small_grads], axis=-1)
        grads = (jnp.concatenate([triple_grad, merge_grad], axis=-1), expand_grad, shrink_grad)
        r0, r1, r2 = (
            lax.psum_scatter(
                lax.psum_scatter(g, "tensor", scatter_dimension=0), ("dp", "ctx"), scatter_dimension=0, tiled=True
            ).astype(F32)
            for g in grads
        )
        small_sum = lax.psum_scatter(
            lax.psum_scatter(small_grads, "tensor", scatter_dimension=0), ("dp", "ctx"), scatter_dimension=0
        )
        narrow_out = list(small_sum[: 8 * small_part].reshape(8, 1, small_part))
        expand_out = small_sum[8 * small_part :].reshape(1, unit_part)
    triple_out = jnp.transpose(r0[:, : 3 * part].reshape(rows, 3, part), (1, 0, 2))
    outputs_rows, inputs_gradient = (
        jnp.transpose(v.reshape(batch, span, width), (1, 0, 2)) for v in (outputs_rows, inputs_gradient)
    )
    return (
        outputs_rows,
        inputs_gradient,
        triple_out,
        jnp.stack(narrow_out[:2]),
        r0[:, 3 * part :].T,
        narrow_out[2],
        narrow_out[3],
        narrow_out[4],
        r1,
        expand_out,
        r2.T,
        narrow_out[5],
        narrow_out[6],
        narrow_out[7],
    )


def solution(mesh):
    in_specs = (
        P(("ctx", "tensor"), "dp", None),
        P(("ctx", "tensor"), "dp", None),
        P("dp", None),
        P(None, ("dp", "ctx"), "tensor"),
        P(None, "tensor", ("dp", "ctx")),
        P("tensor", ("dp", "ctx")),
        P("tensor", ("dp", "ctx")),
        P("tensor", ("dp", "ctx")),
        P("tensor", ("dp", "ctx")),
        P(("dp", "ctx"), "tensor"),
        P("tensor", ("dp", "ctx")),
        P("tensor", ("dp", "ctx")),
        P("tensor", ("dp", "ctx")),
        P("tensor", ("dp", "ctx")),
        P("tensor", ("dp", "ctx")),
    )
    out_specs = (
        P(("ctx", "tensor"), "dp", None),
        P(("ctx", "tensor"), "dp", None),
        P(None, ("dp", "ctx"), "tensor"),
        P(None, "tensor", ("dp", "ctx")),
        P("tensor", ("dp", "ctx")),
        P("tensor", ("dp", "ctx")),
        P("tensor", ("dp", "ctx")),
        P("tensor", ("dp", "ctx")),
        P(("dp", "ctx"), "tensor"),
        P("tensor", ("dp", "ctx")),
        P("tensor", ("dp", "ctx")),
        P("tensor", ("dp", "ctx")),
        P("tensor", ("dp", "ctx")),
        P("tensor", ("dp", "ctx")),
    )
    return jax.shard_map(local, mesh=mesh, in_specs=in_specs, out_specs=out_specs, check_vma=False)
```
